32 devices in a mesh: rep: 2 (over x), fsdp: 4 (over z), sp: 4 (over y, core).
Axes of the slice: x: 2, y: 2, z: 4, core: 2. Of those that a mesh axis runs over, the one named last changes fastest.
Arguments:
- tokens: bfloat16 [16, 1024, 768], P(('rep', 'fsdp'), 'sp'), may hold values from -6 to 6
- lengths: int32 [16, 4], P(('rep', 'fsdp')), may hold values from 1 to 512, 1024 in all within a row
- cotangent: bfloat16 [16, 1024, 768], P(('rep', 'fsdp'), 'sp'), may hold values from -6 to 6
- pre_gain: bfloat16 [768], P('fsdp'), may hold values from 0.5 to 1.5
- pre_shift: bfloat16 [768], P('fsdp'), may hold values from -2 to 2
- w_qkv: bfloat16 [768, 2304], P('fsdp'), may hold values from -0.21875 to 0.21875
- query_gain: bfloat16 [64], P('fsdp'), may hold values from 0.25 to 1.75
- key_gain: bfloat16 [64], P('fsdp'), may hold values from 0.25 to 1.75
- w_proj: bfloat16 [768, 768], P('fsdp'), may hold values from -0.875 to 0.875
- mid_gain: bfloat16 [768], P('fsdp'), may hold values from 0.5 to 1.5
- mid_shift: bfloat16 [768], P('fsdp'), may hold values from -2 to 2
- w_up: bfloat16 [768, 3072], P('fsdp'), may hold values from -0.21875 to 0.21875
- w_down: bfloat16 [3072, 768], P('fsdp'), may hold values from -0.109375 to 0.109375
Outputs:
- output: float32 [16, 1024, 768], P(('rep', 'fsdp'), 'sp')
- grad_tokens: float32 [16, 1024, 768], P(('rep', 'fsdp'), 'sp')
- grad_pre_gain: float32 [768], P('fsdp')
- grad_pre_shift: float32 [768], P('fsdp')
- grad_w_qkv: float32 [768, 2304], P('fsdp')
- grad_query_gain: float32 [64], P('fsdp')
- grad_key_gain: float32 [64], P('fsdp')
- grad_w_proj: float32 [768, 768], P('fsdp')
- grad_mid_gain: float32 [768], P('fsdp')
- grad_mid_shift: float32 [768], P('fsdp')
- grad_w_up: float32 [768, 3072], P('fsdp')
- grad_w_down: float32 [3072, 768], P('fsdp')
The draws below stay inside these ranges and needn't reach their ends.
Inputs may be any that keep to these rules, and one draw needn't show every extreme that they name: The 4 lengths of a row sum to 1024; in every row the largest is 512.
All inputs are finite; a program needn't handle non-finite values.
Results may differ from the reference program's by a relative error of at most 0.02.
Values may be sent and summed in bfloat16 or wider, within the bound.
A program may use at most 128 MiB of HBM per device.

```python
import math
from functools import partial
import jax
import jax.numpy as jnp
import numpy as np
from jax import lax

D = 768
H = 12
DH = 64
FF = 3072
L = 1024
PICS = 4
MAXPIC = 512
ROWS = 16


def steps_of(key, extent, cuts, smallest, largest):
    factor_of = 1.0
    for axis_at, blocks in cuts:
        steps = jax.random.uniform(jax.random.fold_in(jax.random.fold_in(key, 6), axis_at), (blocks,), jnp.float32, smallest / len(cuts), largest / len(cuts))
        factor_of = factor_of * jnp.repeat(jnp.exp(steps), extent[axis_at] // blocks).reshape((-1,) + (1,) * (len(extent) - 1 - axis_at))
    return factor_of


def profile(number_of, total, limit, skew):
    portions = [(1 << 20) // math.isqrt(rank ** skew) + 1 for rank in range(2, number_of + 1)]
    surplus, given = total - limit - (number_of - 1), [1] * (number_of - 1)
    while surplus > 0:
        candidates = [i for i in range(number_of - 1) if given[i] < limit]
        whole, remaining = sum([portions[i] for i in candidates]), surplus
        for i in candidates:
            addition = min(limit - given[i], max(1, remaining * portions[i] // whole), surplus)
            given[i] = given[i] + addition
            surplus = surplus - addition
    return np.array([limit] + given)


def uneven_parts(rng, number_of, total, bound, skew):
    if number_of == 2:
        one = jax.random.randint(rng, (), max(1, total - bound), min(bound, total - 1) + 1)
        return jnp.stack([one, total - one])
    sizes = jnp.asarray(profile(number_of, total, bound, skew), jnp.int32)
    pairs = (number_of - 1) // 2
    source_of, sink = sizes[1:1 + 2 * pairs:2], sizes[2:2 + 2 * pairs:2]
    room = jnp.minimum(source_of - 1, bound - sink)
    passed = jax.random.randint(jax.random.fold_in(rng, 1), (pairs,), 0, 1 << 20) % (room + 1)
    sizes = sizes.at[1:1 + 2 * pairs:2].set(source_of - passed).at[2:2 + 2 * pairs:2].set(sink + passed)
    return sizes[jax.random.permutation(jax.random.fold_in(rng, 2), number_of)]


def noise(stream_key, extent, deviation, most, cuts=(), kind=jnp.bfloat16):
    factor_of = steps_of(stream_key, extent, cuts, -0.22, 0.18) if cuts else 1.0
    values = jax.random.normal(stream_key, extent, jnp.float32) * deviation * factor_of
    return jnp.minimum(jnp.maximum(values, -most), most).astype(kind)


def setup_inputs(seed: int = 0) -> dict:
    key_of = jax.random.split(jax.random.key(seed), 14)
    return {
        "tokens": noise(key_of[0], (ROWS, L, D), 1.0, 6.0, ((0, 8), (1, 4))),
        "lengths": jax.vmap(lambda own: uneven_parts(own, PICS, L, MAXPIC, 1))(jax.random.split(key_of[1], ROWS)).reshape((ROWS, PICS)).astype(jnp.int32),
        "cotangent": noise(key_of[2], (ROWS, L, D), 1.0, 6.0, ((0, 8), (1, 4))),
        "pre_gain": jnp.clip(1.0 + 0.1 * jax.random.normal(key_of[3], (D,), jnp.float32), 0.5, 1.5).astype(jnp.bfloat16),
        "pre_shift": noise(key_of[4], (D,), 0.3, 2.0, ((0, 4),)),
        "w_qkv": noise(key_of[5], (D, 3 * D), D ** -0.5, 0.21875, ((0, 4),)),
        "query_gain": jnp.clip(1.0 + 0.15 * jax.random.normal(key_of[6], (DH,), jnp.float32), 0.25, 1.75).astype(jnp.bfloat16),
        "key_gain": jnp.clip(1.0 + 0.15 * jax.random.normal(key_of[7], (DH,), jnp.float32), 0.25, 1.75).astype(jnp.bfloat16),
        "w_proj": noise(key_of[8], (D, D), (D // 16) ** -0.5, 0.875, ((0, 4),)),
        "mid_gain": jnp.clip(1.0 + 0.1 * jax.random.normal(key_of[9], (D,), jnp.float32), 0.5, 1.5).astype(jnp.bfloat16),
        "mid_shift": noise(key_of[10], (D,), 0.3, 2.0, ((0, 4),)),
        "w_up": noise(key_of[11], (D, FF), D ** -0.5, 0.21875, ((0, 4),)),
        "w_down": noise(key_of[12], (FF, D), FF ** -0.5, 0.109375, ((0, 4),)),
    }


@jax.custom_vjp
def low(v):
    return lax.optimization_barrier(v.astype(jnp.bfloat16)).astype(jnp.float32)

@jax.custom_vjp
def low_back(v):
    return v

def low_keep(v):
    return (low(v), None)

def low_pass(kept, grad):
    return (grad,)

def back_keep(v):
    return (v, None)

def back_low(kept, grad):
    return (low(grad),)
low.defvjp(low_keep, low_pass)
low_back.defvjp(back_keep, back_low)
EPSILON = 1e-06
NEGATIVE = -1e+30
HIGHEST = lax.Precision.HIGHEST

def layer_norm(value, gain, shift):
    mean = lax.optimization_barrier(jnp.mean(value, axis=-1, keepdims=True))
    centred = value - mean
    spread = lax.optimization_barrier(jnp.mean(centred * centred, axis=-1, keepdims=True))
    return centred * lax.rsqrt(spread + EPSILON) * gain + shift

def head_norm(value, gain):
    mean = lax.optimization_barrier(jnp.mean(value, axis=-1, keepdims=True))
    centred = value - mean
    spread = lax.optimization_barrier(jnp.mean(centred * centred, axis=-1, keepdims=True))
    return centred * lax.rsqrt(spread + EPSILON) * gain

def gelu_exact(value):
    return jax.nn.gelu(value, approximate=False)

def picture_ids(lengths, length):
    ends = jnp.cumsum(lengths, axis=-1).astype(jnp.int32)
    place = jnp.arange(length, dtype=jnp.int32)
    return lax.optimization_barrier(jnp.sum((place[None, :, None] >= ends[:, None, :]).astype(jnp.int32), axis=-1))

def block_layer(params, inputs):
    xgroup, lgroup = inputs
    pre_gain, pre_shift, w_qkv, query_gain, key_gain, w_proj, mid_gain, mid_shift, w_up, w_down = params
    group, length, width = xgroup.shape
    normed = low(layer_norm(xgroup, pre_gain, pre_shift))
    qkv = low_back(jnp.einsum('gtd,dn->gtn', normed, w_qkv, precision=HIGHEST))
    split = qkv.reshape(group, length, 3, H, DH)
    query = low_back(low(head_norm(split[:, :, 0], query_gain)))
    key = low_back(low(head_norm(split[:, :, 1], key_gain)))
    value = low_back(low(split[:, :, 2]))
    ids = picture_ids(lgroup, length)
    score = jnp.einsum('gqhd,gkhd->ghqk', query, key, precision=HIGHEST) * (1.0 / math.sqrt(DH))
    score = low_back(score)
    keep = ids[:, None, :, None] == ids[:, None, None, :]
    score = jnp.where(keep, score, NEGATIVE)
    prob = low(jax.nn.softmax(score, axis=-1))
    mixed = jnp.einsum('ghqk,gkhd->gqhd', prob, value, precision=HIGHEST)
    attended = low_back(low(mixed)).reshape(group, length, width)
    attn = low_back(jnp.einsum('gtd,de->gte', attended, w_proj, precision=HIGHEST))
    resid = xgroup + attn
    mid = low(layer_norm(resid, mid_gain, mid_shift))
    inner = low_back(jnp.einsum('gtd,df->gtf', mid, w_up, precision=HIGHEST))
    act = low(gelu_exact(inner))
    branch = low_back(jnp.einsum('gtf,fd->gtd', act, w_down, precision=HIGHEST))
    return resid + branch

def reference(tokens, lengths, cotangent, pre_gain, pre_shift, w_qkv, query_gain, key_gain, w_proj, mid_gain, mid_shift, w_up, w_down):
    params = tuple((p.astype(jnp.float32) for p in (pre_gain, pre_shift, w_qkv, query_gain, key_gain, w_proj, mid_gain, mid_shift, w_up, w_down)))
    group = 2 if ROWS % 2 == 0 else 1
    count = ROWS // group
    xs = tokens.astype(jnp.float32).reshape(count, group, L, D)
    ls = lengths.astype(jnp.int32).reshape(count, group, PICS)

    def forward(xvals, pvals):
        stepper = jax.checkpoint(partial(block_layer, pvals))
        return lax.map(stepper, (xvals, ls))
    result, pull = jax.vjp(forward, xs, params)
    d_tokens, d_params = pull(cotangent.astype(jnp.float32).reshape(count, group, L, D))
    return (result.reshape(ROWS, L, D), d_tokens.reshape(ROWS, L, D), d_params[0], d_params[1], d_params[2], d_params[3], d_params[4], d_params[5], d_params[6], d_params[7], d_params[8], d_params[9])
```

```python
import functools
import math
from types import SimpleNamespace

import jax
import jax.numpy as jnp
from jax import lax
from jax.experimental import pallas as pl
from jax.experimental.pallas import tpu as pltpu
from jax.sharding import PartitionSpec as P

H = 12
DH = 64
EPSILON = 1e-06
MASKED = 1e30
MESH = pl.DeviceIdType.MESH
VMEM_LIMIT = 67043328
bf = jnp.bfloat16
f32 = jnp.float32


def nn(a, b):
    return lax.dot_general(a, b, (((1,), (0,)), ((), ())), preferred_element_type=f32)


def nt(a, b):
    return lax.dot_general(a, b, (((1,), (1,)), ((), ())), preferred_element_type=f32)


def at(i, size, base=0):
    if isinstance(i, int) and isinstance(base, int):
        return pl.ds(base + i * size, size)
    return pl.ds(pl.multiple_of(base + i * size, math.gcd(size, base) if isinstance(base, int) else size), size)


def same_head(n):
    a = lax.broadcasted_iota(jnp.int32, (n, n), 0) // DH
    b = lax.broadcasted_iota(jnp.int32, (n, n), 1) // DH
    return (a == b).astype(f32).astype(bf)


def split2(x):
    hi = x.astype(bf)
    return hi, (x - hi.astype(f32)).astype(bf)


def standardize(x):
    mean = jnp.mean(x, axis=-1, keepdims=True)
    c = x - mean
    r = lax.rsqrt(jnp.mean(c * c, axis=-1, keepdims=True) + EPSILON)
    return c * r, r


def transpose_to(src, dst):
    @pl.loop(0, dst.shape[0] // 128)
    def _(i):
        dst[at(i, 128), :] = src[:, at(i, 128)].astype(f32).T.astype(bf)


def wcols(m, b, s):
    w = m.W[b, :, :, s]
    return w.reshape(w.shape[0] * w.shape[1], w.shape[2])


def wrows(m, b, i):
    w = m.W[b, pl.ds(2 * i, 2), :, :]
    return w.reshape(2 * w.shape[1], w.shape[2])


def select_rows(m, rowbuf, dst):
    T, D = dst.shape

    @pl.loop(0, D // 256)
    def _(i):
        s = at(i, 256)
        dst[:, s] = (nn(m.ebuf[10], rowbuf[0, :, s]) + nn(m.ebuf[11], rowbuf[1, :, s])).astype(bf)


def place_stage(m):
    T = m.xs.shape[0]
    row = lax.broadcasted_iota(jnp.int32, (T, T), 0) + m.start + T * m.core
    row = jnp.where(row >= 2 * T, row - 2 * T, row)
    col = lax.broadcasted_iota(jnp.int32, (T, T), 1)
    m.ebuf[10] = (row == col).astype(f32).astype(bf)
    m.ebuf[11] = (row == col + T).astype(f32).astype(bf)
    t = row[:, :128]
    pic = sum((t >= e).astype(jnp.int32) for e in m.ends)
    lane = col[:, :128]
    hot = (lane == pic).astype(f32)
    m.maskq[...] = (hot * MASKED).astype(bf)
    m.maskk[...] = jnp.where(lane < 4, hot - 1.0, 0.0).astype(bf)


def restore_quarter(m, cat, quarter):
    T = m.xs.shape[0]
    n = T // 2
    i = lax.broadcasted_iota(jnp.int32, (n, T), 0) + quarter * n - m.start
    i = jnp.where(i < 0, i + 2 * T, i)
    col = lax.broadcasted_iota(jnp.int32, (n, T), 1)
    a = (i == col).astype(f32).astype(bf)
    b = (i == col + T).astype(f32).astype(bf)
    return (nn(a, cat[0]) + nn(b, cat[1])).astype(bf)


def gains_stage(m):
    D = m.gains.shape[1]
    n = D // 4
    k = DH // 4
    lane = lax.broadcasted_iota(jnp.int32, (256, D), 0)
    col = lax.broadcasted_iota(jnp.int32, (256, D), 1)
    wide = jnp.zeros((8, D), f32)
    head = jnp.zeros((8, D), f32)
    for u in range(4):
        g = m.gbuf[u].astype(bf)
        wide += nn(g, ((col == lane + n * u) & (lane < n)).astype(f32).astype(bf))
        head += nn(g, ((col % DH == lane + k * u) & (lane < k)).astype(f32).astype(bf))
    r = lax.broadcasted_iota(jnp.int32, (8, D), 0)
    m.gains[...] = jnp.where(r < 4, wide, head)


def norm_stage(src, gain, shift, dst, dstT):
    @pl.loop(0, src.shape[0] // 64)
    def _(i):
        s = at(i, 64)
        xh, _ = standardize(src[s, :].astype(f32))
        dst[s, :] = (xh * gain + shift).astype(bf)

    transpose_to(dst, dstT)


def qkv_stage(m, kind):
    D = m.xs.shape[1]

    @pl.loop(0, D // 256)
    def _(i):
        off, s = at(i, 256), at(i, 256, kind * D)
        acc = nn(m.mid[...], wcols(m, kind, off))
        if kind == 2:
            m.v[:, off] = acc.astype(bf)
            return
        B = same_head(256)
        hi, lo = split2(acc)
        c = acc - (nn(hi, B) + nn(lo, B)) * (1.0 / DH)
        r = lax.rsqrt(nn((c * c).astype(bf), B) * (1.0 / DH) + EPSILON)
        xh = c * r
        m.qkh[:, s] = xh.astype(bf)
        m.qkr[:, s] = r.astype(bf)
        val = (xh * m.gains[4 + kind : 5 + kind, off]).astype(bf)
        if kind == 0:
            m.q[:, off] = (val.astype(f32) * (1.0 / math.sqrt(DH))).astype(bf)
        else:
            m.k[:, off] = val


def lane_half(T, e):
    lane = lax.broadcasted_iota(jnp.int32, (T, 128), 1)
    return (lane < DH) if e == 0 else (lane >= DH)


def attend_pair(m, hp):
    T = m.q.shape[0]
    s = at(hp, 128)
    q2, k2, v2 = m.q[:, s].astype(f32), m.k[:, s], m.v[:, s]
    kx = jnp.concatenate([k2, m.maskk[...]], axis=1)
    vx = jnp.concatenate([v2, jnp.ones((T, 128), bf)], axis=1)
    outs, invs = [], []
    for e in (0, 1):
        qe = jnp.where(lane_half(T, e), q2, 0.0).astype(bf)
        E = jnp.exp(nt(jnp.concatenate([qe, m.maskq[...]], axis=1), kx)).astype(bf)
        m.ebuf[2 * hp + e] = E
        o = nn(E, vx)
        inv = 1.0 / o[:, 128:]
        outs.append(o[:, :128] * inv)
        invs.append(inv)
    first = lane_half(T, 0)
    m.att[:, s] = jnp.where(first, outs[0], outs[1]).astype(bf)
    m.linv[:, s] = jnp.where(first, invs[0], invs[1])


def proj_stage(m):
    @pl.loop(0, m.xs.shape[1] // 256)
    def _(i):
        s = at(i, 256)
        m.resid[:, s] = m.xs[:, s].astype(f32) + nn(m.att[...], wcols(m, 3, s))


def gelu_both(x):
    z = jnp.abs(x) * (1.0 / math.sqrt(2.0))
    t = 1.0 / (1.0 + 0.3275911 * z)
    p = ((((1.061405429 * t - 1.453152027) * t + 1.421413741) * t - 0.284496736) * t + 0.254829592) * t
    ex = jnp.exp(-0.5 * x * x)
    tail = 0.5 * p * ex
    phi = jnp.where(x < 0, tail, 1.0 - tail)
    return x * phi, phi + x * ex * (1.0 / math.sqrt(2.0 * math.pi))


def up_stage(m, j):
    D = m.xs.shape[1]

    @pl.loop(0, D // 256)
    def _(i):
        a, d = gelu_both(nn(m.mid[...], wcols(m, 4 + j, at(i, 256))))
        s = at(i, 256, j * D)
        m.act[:, s] = a.astype(bf)
        m.gp[:, s] = d.astype(bf)


def out_stage(m):
    D = m.xs.shape[1]

    @pl.loop(0, D // 256)
    def _(i):
        s = at(i, 256)
        acc = m.resid[:, s]
        for u in range(4):
            w = m.W[8:12, u, :, s]
            acc += nn(m.act[:, u * D : (u + 1) * D], w.reshape(D, 256))
        m.osel[:, s] = acc.astype(bf)


def dinner_stage(m, u):
    D = m.xs.shape[1]
    for i in range(2):
        w = m.W[8 + 2 * i : 10 + 2 * i, u, :, :]
        s = at(i, D // 2, u * D)
        d = nt(m.cot[...], w.reshape(D // 2, D))
        m.gp[:, s] = (d * m.gp[:, s].astype(f32)).astype(bf)


def dmid_stage(m):
    D = m.xs.shape[1]
    n = D // 2

    @pl.loop(0, 2)
    def _(i):
        acc = nt(m.gp[:, 0:D], wrows(m, 4, i))
        for j in range(1, 4):
            acc += nt(m.gp[:, j * D : (j + 1) * D], wrows(m, 4 + j, i))
        m.dres[:, at(i, n)] = acc


def dresid_stage(m):
    T, D = m.dres.shape
    g = m.gains[2:3, :]

    @pl.loop(0, T // 64)
    def _(i):
        s = at(i, 64)
        dm = m.dres[s, :]
        xh, r = standardize(m.resid[s, :])
        dx = dm * g
        m1 = jnp.mean(dx, axis=-1, keepdims=True)
        m2 = jnp.mean(dx * xh, axis=-1, keepdims=True)
        dr = m.cot[s, :].astype(f32) + r * (dx - m1 - xh * m2)
        m.dres[s, :] = dr
        m.dattn[s, :] = dr.astype(bf)
        m.gsum[2:3, :] += jnp.sum(dm * xh, axis=0, keepdims=True)
        m.gsum[3:4, :] += jnp.sum(dm, axis=0, keepdims=True)


def datt_stage(m):
    n = m.xs.shape[1] // 2

    @pl.loop(0, 2)
    def _(i):
        m.datt[:, at(i, n)] = nt(m.dattn[...], wrows(m, 3, i)).astype(bf)


def attend_back_pair(m, hp):
    T, D = m.q.shape
    s = at(hp, 128)
    do = m.datt[:, s].astype(f32)
    dos = do * m.linv[:, s]
    B = same_head(128)
    hi, lo = split2(dos * m.att[:, s].astype(f32))
    dl = nn(hi, B) + nn(lo, B)
    k2, v2 = m.k[:, s], m.v[:, s]
    lane = lax.broadcasted_iota(jnp.int32, (T, 128), 1)
    vx = jnp.concatenate([v2, (lane < 2).astype(f32).astype(bf)], axis=1)
    dosT = dos.T.astype(bf)
    qT = m.q[:, s].astype(f32).T.astype(bf)
    dqs, dks, dvs = [], [], []
    for e in (0, 1):
        de = jnp.where(lane_half(T, e), dos, 0.0).astype(bf)
        dle = dl[:, e * DH : e * DH + 1]
        dh = dle.astype(bf).astype(f32)
        dmask = jnp.where(lane == 0, -dh, jnp.where(lane == 1, dh - dle, 0.0)).astype(bf)
        t = nt(jnp.concatenate([de, dmask], axis=1), vx)
        E = m.ebuf[2 * hp + e]
        ds = (E.astype(f32) * t).astype(bf)
        dqs.append(nn(ds, k2))
        dks.append(nn(qT[e * DH : (e + 1) * DH, :], ds))
        dvs.append(nn(dosT[e * DH : (e + 1) * DH, :], E))
    dq = jnp.where(lane_half(T, 0), dqs[0], dqs[1]) * (1.0 / math.sqrt(DH))
    dk = jnp.concatenate(dks, axis=0).T
    dv = jnp.concatenate(dvs, axis=0).T
    m.dqkv[:, at(hp, 128, 2 * D)] = dv.astype(bf)
    for kind, d in ((0, dq), (1, dk)):
        d = d.astype(bf).astype(f32)
        w = at(hp, 128, kind * D)
        xh = m.qkh[:, w].astype(f32)
        r = m.qkr[:, w].astype(f32)
        m.gsum[4 + kind : 5 + kind, s] = jnp.sum(d * xh, axis=0, keepdims=True)
        dx = d * m.gains[4 + kind : 5 + kind, s]
        h1, l1 = split2(dx)
        m1 = (nn(h1, B) + nn(l1, B)) * (1.0 / DH)
        h2, l2 = split2(dx * xh)
        m2 = (nn(h2, B) + nn(l2, B)) * (1.0 / DH)
        m.dqkv[:, w] = (r * (dx - m1 - xh * m2)).astype(bf)


def dnormed_stage(m):
    D = m.xs.shape[1]
    n = D // 2

    @pl.loop(0, 2)
    def _(i):
        acc = nt(m.dqkv[:, 0:D], wrows(m, 0, i))
        for j in range(1, 3):
            acc += nt(m.dqkv[:, j * D : (j + 1) * D], wrows(m, j, i))
        m.resid[:, at(i, n)] = acc


def dtokens_stage(m):
    T, D = m.dres.shape
    g = m.gains[0:1, :]

    @pl.loop(0, T // 64)
    def _(i):
        s = at(i, 64)
        dn = m.resid[s, :]
        xh, r = standardize(m.xs[s, :].astype(f32))
        dx = dn * g
        m1 = jnp.mean(dx, axis=-1, keepdims=True)
        m2 = jnp.mean(dx * xh, axis=-1, keepdims=True)
        m.dtok[s, :] = (m.dres[s, :] + r * (dx - m1 - xh * m2)).astype(bf)
        m.gsum[0:1, :] += jnp.sum(dn * xh, axis=0, keepdims=True)
        m.gsum[1:2, :] += jnp.sum(dn, axis=0, keepdims=True)


def grad_down(m, u):
    D = m.xs.shape[1]
    n = D // 4

    @pl.loop(0, D // 256)
    def _(i):
        r = nn(m.cotT[...], m.act[:, at(i, 256, u * D)]).astype(bf)
        for j in range(4):
            m.G[j, u, :, at(i, 256)] = r[j * n : (j + 1) * n]


def grad_block(m, b, lhsT, rhs, base):
    D = m.xs.shape[1]
    n = D // 4

    @pl.loop(0, D // 256)
    def _(i):
        r = nn(lhsT[...], rhs[:, at(i, 256, base)]).astype(bf)
        for u in range(4):
            m.G[b, u, :, at(i, 256)] = r[u * n : (u + 1) * n]


class Comm:
    def __init__(self, m):
        self.m = m
        self.x, self.z, sp = lax.axis_index("rep"), lax.axis_index("fsdp"), lax.axis_index("sp")
        self.y, self.c = sp // 2, sp % 2
        x, y, z, c = self.x, self.y, self.z, self.c
        self.f1 = x + c * (y - x)
        self.f2 = y + c * (x - y)
        nx, ny = (1 - x, z, sp), (x, z, 2 * (1 - y) + c)
        self.nx, self.ny = nx, ny
        self.n1 = (x + (1 - c) * (1 - 2 * x), z, 2 * (y + c * (1 - 2 * y)) + c)
        self.n2 = (x + c * (1 - 2 * x), z, 2 * (y + (1 - c) * (1 - 2 * y)) + c)
        self.core = (x, z, 2 * y + 1 - c)
        self.zat = lambda u: (x, u, sp)
        self.z1 = z + 1 - 2 * (z % 2)
        self.zt = 3 - z
        self.mine = at(c, 384)
        self.other = at(1 - c, 384)
        self.q = 2 * self.f2 + self.f1

    def barrier(self):
        sem = pltpu.get_barrier_semaphore()
        peers = [self.nx, self.ny, self.core] + [self.zat((self.z + d) % 4) for d in (1, 2, 3)]
        for p in peers:
            pl.semaphore_signal(sem, inc=1, device_id=p, device_id_type=MESH)
        pl.semaphore_wait(sem, len(peers))

    def copy(self, src, dst, send, recv, dev):
        return pltpu.make_async_remote_copy(
            src_ref=src, dst_ref=dst, send_sem=send, recv_sem=recv, device_id=dev, device_id_type=MESH
        )

    def row_copies(self, arg, buf, k):
        s, r = self.m.rsem.at[0, k], self.m.rsem.at[1, k]
        mine = buf.at[self.y, at(self.c, 256)]
        there = buf.at[1 - self.y, at(self.c, 256)]
        local = pltpu.make_async_copy(arg.at[self.y], mine, s.at[0])
        near = self.copy(arg.at[self.y], mine, s.at[1], r.at[1], self.core)
        far = self.copy(arg.at[1 - self.y], mine, s.at[2], r.at[2], self.ny)
        pass_on = self.copy(there, there, s.at[3], r.at[3], self.core)
        return local, near, far, pass_on

    def row_start(self, arg, buf, k):
        local, near, far, _ = self.row_copies(arg, buf, k)
        far.start()
        near.start()
        local.start()

    def row_pass(self, arg, buf, k):
        _, _, far, pass_on = self.row_copies(arg, buf, k)
        far.wait_recv()
        pass_on.start()

    def row_wait(self, arg, buf, k):
        local, near, far, pass_on = self.row_copies(arg, buf, k)
        local.wait()
        near.wait()
        far.wait_send()
        pass_on.wait()

    def gain_copies(self):
        m = self.m
        out = [pltpu.make_async_copy(m.gpack, m.gbuf.at[self.z], m.gsem.at[0, 0])]
        for d in (1, 2, 3):
            dev = self.zat((self.z + d) % 4)
            out.append(self.copy(m.gpack, m.gbuf.at[self.z], m.gsem.at[0, d], m.gsem.at[1, d], dev))
        return out

    def shard(self, b, rows, cols):
        m = self.m
        arg, r0, c0 = (m.a_qkv, 0, 768 * b) if b < 3 else (m.a_proj, 0, 0) if b == 3 else (
            (m.a_up, 0, 768 * (b - 4)) if b < 8 else (m.a_down, 192 * (b - 8), 0))
        return arg.at[pl.ds(pl.multiple_of(r0 + rows[0], 16), rows[1]), pl.ds(pl.multiple_of(c0 + cols[0], 128), cols[1])]

    def own_copy(self, b):
        return pltpu.make_async_copy(self.shard(b, (0, 192), (0, 768)), self.m.W.at[b, self.z], self.m.wsem.at[0, 0, b])

    def z_start(self, b):
        m = self.m
        src = self.shard(b, (48 * self.q, 48), (384 * self.c, 384))
        for d in (1, 2, 3):
            dst = m.W.at[b, self.z, at(self.q, 48), self.mine]
            self.copy(src, dst, m.wsem.at[0, 1, b], m.wsem.at[1, 1, b], self.zat((self.z + d) % 4)).start()

    def plane(self, k, b):
        m = self.m
        rows, dev = {2: (at(self.q, 48), self.n1), 3: (at(self.f2, 96), self.n2), 4: (pl.ds(0, 192), self.core)}[k]
        out = []
        for d in (1, 2, 3):
            ref = m.W.at[b, (self.z + d) % 4, rows, self.mine]
            out.append(self.copy(ref, ref, m.wsem.at[0, k, b], m.wsem.at[1, k, b], dev))
        return out

    def w_all(self, k, b):
        m = self.m
        rows, dev = {1: (at(self.q, 48), self.core), 2: (at(self.q, 48), self.n1), 3: (at(self.f2, 96), self.n2),
                     4: (pl.ds(0, 192), self.core)}[k]
        ref = m.W.at[b, 0:3, rows, self.mine]
        return self.copy(ref, ref, m.wsem.at[0, k, b], m.wsem.at[1, k, b], dev)

    def ag_step(self, k, b):
        self.w_all(k, b).wait_recv()
        if k < 4:
            for cp in self.plane(k + 1, b):
                cp.start()
        else:
            for j in (1, 2, 3, 4):
                self.w_all(j, b).wait_send()

    def ag_tick(self, t, n=12):
        for k in (4, 3, 2, 1):
            b = t - (k - 1)
            if isinstance(t, int):
                if 0 <= b < n:
                    self.ag_step(k, b)
            else:
                self.ag_step(k, b)

    def rs_copies(self, k, b):
        m = self.m
        G, z, f1 = m.G, self.z, self.f1
        slot = b % 2
        rows = at(f1, 96)
        sem = lambda j: (m.psem.at[0, j, slot], m.psem.at[1, j, slot])
        if k == 0:
            return [self.copy(G.at[b, :, :, self.other], m.rA.at[slot], *sem(0), self.core)]
        if k == 1:
            return [self.copy(G.at[b, :, at(1 - f1, 96), self.mine], m.rB.at[slot], *sem(1), self.n1)]
        if k == 2:
            return [
                self.copy(G.at[b, self.z1, rows, self.mine], m.rC.at[slot, 0], *sem(2), self.zat(self.z1)),
                self.copy(G.at[b, 3 - self.z1, rows, self.mine], m.rC.at[slot, 1], *sem(7), self.zat(self.z1)),
            ]
        if k == 3:
            return [self.copy(G.at[b, self.zt, rows, self.mine], m.rD.at[slot], *sem(3), self.zat(self.zt))]
        if k == 4:
            return [self.copy(G.at[b, z, rows, self.mine], m.rE.at[slot], *sem(4), self.n2)]
        if k == 5:
            ref = G.at[b, z, rows, self.mine]
            return [self.copy(ref, ref, *sem(5), self.n1)]
        ref = G.at[b, z, :, self.mine]
        return [self.copy(ref, ref, *sem(6), self.core)]

    def rs_step(self, k, b):
        m = self.m
        G, z = m.G, self.z
        slot = b % 2
        rows = at(self.f1, 96)
        if k > 0:
            for cp in self.rs_copies(k - 1, b):
                cp.wait()
        if k == 1:

            @pl.loop(0, 4)
            def _(u):
                G[b, u, :, self.mine] = (G[b, u, :, self.mine].astype(f32) + m.rA[slot, u].astype(f32)).astype(bf)
        elif k == 2:

            @pl.loop(0, 4)
            def _(u):
                G[b, u, rows, self.mine] = (G[b, u, rows, self.mine].astype(f32) + m.rB[slot, u].astype(f32)).astype(bf)
        elif k == 3:
            for i, u in ((0, z), (1, self.zt)):
                G[b, u, rows, self.mine] = (G[b, u, rows, self.mine].astype(f32) + m.rC[slot, i].astype(f32)).astype(bf)
        elif k in (4, 5):
            r = (m.rD if k == 4 else m.rE)[slot]
            G[b, z, rows, self.mine] = (G[b, z, rows, self.mine].astype(f32) + r.astype(f32)).astype(bf)
        if k < 7:
            for cp in self.rs_copies(k, b):
                cp.start()
        else:
            self.fin_copy(b).start()

    def fin_copy(self, b):
        return pltpu.make_async_copy(self.m.G.at[b, self.z], self.m.fin.at[b], self.m.fsem.at[b])

    def rs_tick(self, t, n=12):
        for k in range(7, -1, -1):
            b = t - k
            if isinstance(t, int):
                if 0 <= b < n:
                    self.rs_step(k, b)
            else:
                self.rs_step(k, b)

    def vec_copy(self, i):
        m = self.m
        dev = [self.core, self.nx, self.ny, self.zat(self.z1), self.zat(self.zt)][i]
        return self.copy(m.gs.at[i], m.gr.at[i], m.vsem.at[0, i], m.vsem.at[1, i], dev)

    def vec_step(self, i):
        m = self.m
        if i == 0:
            m.gs[0] = m.gsum[...]
        else:
            self.vec_copy(i - 1).wait()
            m.gs[i] = m.gs[i - 1] + m.gr[i - 1]
        if i < 5:
            self.vec_copy(i).start()
        else:
            m.vec[...] = m.gs[5]

    def cat_copy(self, cat, k):
        half = cat.at[self.c]
        return self.copy(half, half, self.m.osem.at[0, k, 0], self.m.osem.at[1, k, 0], self.core)

    def quarter_copies(self, dst, k):
        m = self.m
        far = self.copy(m.quart.at[1], dst.at[self.y], m.osem.at[0, k, 1], m.osem.at[1, k, 1], self.ny)
        near = pltpu.make_async_copy(m.quart.at[0], dst.at[self.y], m.osem.at[0, k, 2])
        return far, near

    def result_send(self, cat, dst, k):
        m = self.m
        self.cat_copy(cat, k).wait()
        m.quart[1] = restore_quarter(m, cat, 2 * (1 - self.y) + self.c)
        far, near = self.quarter_copies(dst, k)
        far.start()
        m.quart[0] = restore_quarter(m, cat, 2 * self.y + self.c)
        near.start()

    def result_wait(self, dst, k):
        far, near = self.quarter_copies(dst, k)
        far.wait()
        near.wait()


SCRATCH = lambda T, D, FF: dict(
    gains=((8, D), f32), maskq=((T, 128), bf), maskk=((T, 128), bf), xs=((T, D), bf), cot=((T, D), bf),
    mid=((T, D), bf), normedT=((D, T), bf), midT=((D, T), bf), cotT=((D, T), bf),
    q=((T, D), bf), k=((T, D), bf), v=((T, D), bf), qkh=((T, 2 * D), bf), qkr=((T, 2 * D), bf),
    ebuf=((H, T, T), bf), att=((T, D), bf), linv=((T, D), f32), resid=((T, D), f32),
    act=((T, FF), bf), gp=((T, FF), bf), dres=((T, D), f32), datt=((T, D), bf), gsum=((8, D), f32),
)


def prepare(m, lengths, y):
    T = m.xs.shape[0]
    l = [lengths[y, k] for k in range(4)]
    m.ends = [l[0], l[0] + l[1], l[0] + l[1] + l[2]]
    m.start = jnp.where(l[0] == T, 0, jnp.where(l[1] == T, m.ends[0], jnp.where(l[2] == T, m.ends[1], m.ends[2])))
    m.dattn = m.mid
    m.dqkv = m.act
    m.attT = m.cotT


def layer_kernel(comm_names, *refs):
    m = SimpleNamespace(**dict(zip(comm_names, refs)))
    cm = Comm(m)
    m.osel, m.dtok = m.rowx.at[cm.c], m.rowc.at[cm.c]
    m.core = cm.c
    prepare(m, m.lengths, cm.y)
    cm.barrier()
    cm.row_start(m.tokens, m.rowx, 0)
    gains = cm.gain_copies()
    for g in gains:
        g.start()
    for b in range(12):
        cm.z_start(b)
        cm.own_copy(b).start()
        if b == 2:
            cm.row_start(m.cotangent, m.rowc, 1)
    m.gsum[...] = jnp.zeros_like(m.gsum)
    place_stage(m)
    cm.row_pass(m.tokens, m.rowx, 0)
    for g in gains:
        g.wait()
    gains_stage(m)
    cm.row_wait(m.tokens, m.rowx, 0)
    select_rows(m, m.rowx, m.xs)
    norm_stage(m.xs, m.gains[0:1, :], m.gains[1:2, :], m.mid, m.normedT)
    cm.row_pass(m.cotangent, m.rowc, 1)
    cm.row_wait(m.cotangent, m.rowc, 1)
    select_rows(m, m.rowc, m.cot)
    for b in range(12):
        cm.own_copy(b).wait()
    for t in range(15):
        cm.ag_tick(t)
    for kind in range(3):
        qkv_stage(m, kind)

    @pl.loop(0, H // 2)
    def _(hp):
        attend_pair(m, hp)

    proj_stage(m)
    norm_stage(m.resid, m.gains[2:3, :], m.gains[3:4, :], m.mid, m.midT)

    @pl.loop(0, 4)
    def _(j):
        up_stage(m, j)

    transpose_to(m.cot, m.cotT)
    for u in range(4):
        grad_down(m, u)
    out_stage(m)
    cm.cat_copy(m.rowx, 0).start()
    for u in range(4):
        dinner_stage(m, u)
    dmid_stage(m)

    @pl.loop(0, 4)
    def _(j):
        grad_block(m, 4 + j, m.midT, m.gp, j * 768)

    cm.result_send(m.rowx, m.outq, 0)
    dresid_stage(m)
    transpose_to(m.att, m.attT)
    grad_block(m, 8, m.attT, m.dattn, 0)
    datt_stage(m)

    @pl.loop(0, H // 2)
    def _(hp):
        attend_back_pair(m, hp)

    @pl.loop(0, 3)
    def _(j):
        grad_block(m, 9 + j, m.normedT, m.dqkv, j * 768)

    dnormed_stage(m)
    dtokens_stage(m)
    cm.cat_copy(m.rowc, 1).start()
    cm.result_wait(m.outq, 0)
    for i in range(6):
        cm.vec_step(i)
    cm.result_send(m.rowc, m.dtokq, 1)
    for t in range(19):
        cm.rs_tick(t)
    for b in range(12):
        cm.fin_copy(b).wait()
    cm.result_wait(m.dtokq, 1)


def fused_layer(tokens, lengths, cotangent, gpack, w_qkv, w_proj, w_up, w_down):
    T, D, FF = tokens.shape[0] * tokens.shape[1], tokens.shape[2], w_up.shape[1]
    any_, vmem = pl.BlockSpec(memory_space=pl.ANY), pl.BlockSpec(memory_space=pltpu.VMEM)
    ins = ["tokens", "lengths", "cotangent", "gpack", "a_qkv", "a_proj", "a_up", "a_down"]
    outs = dict(
        fin=((12, D // 4, D), bf), outq=(tokens.shape, bf), dtokq=(tokens.shape, bf), vec=((8, D), f32)
    )
    scratch = SCRATCH(T, D, FF)
    scratch.update(
        W=((12, 4, D // 4, D), bf), G=((12, 4, D // 4, D), bf), rowx=((2, T, D), bf), rowc=((2, T, D), bf),
        gbuf=((4, 8, 256), f32),
        rA=((2, 4, 192, 384), bf), rB=((2, 4, 96, 384), bf), rC=((2, 2, 96, 384), bf), rD=((2, 96, 384), bf),
        rE=((2, 96, 384), bf), quart=((2, T // 2, D), bf), gs=((6, 8, D), f32), gr=((5, 8, D), f32),
    )
    sems = dict(
        rsem=(2, 2, 4), gsem=(2, 4), wsem=(2, 5, 12), psem=(2, 8, 2), fsem=(12,), vsem=(2, 5), osem=(2, 2, 3)
    )
    names = ins + list(outs) + list(scratch) + list(sems)
    return pl.pallas_call(
        functools.partial(layer_kernel, names),
        out_shape=[jax.ShapeDtypeStruct(s, d) for s, d in outs.values()],
        in_specs=[any_, pl.BlockSpec(memory_space=pltpu.SMEM), any_, vmem] + [any_] * 4,
        out_specs=[any_, any_, any_, vmem],
        scratch_shapes=[pltpu.VMEM(s, d) for s, d in scratch.values()]
        + [pltpu.SemaphoreType.DMA(s) for s in sems.values()],
        compiler_params=pltpu.CompilerParams(collective_id=0, has_side_effects=True, vmem_limit_bytes=VMEM_LIMIT),
        name="layer",
    )(tokens, lengths, cotangent, gpack, w_qkv, w_proj, w_up, w_down)


def plain_kernel(names, *refs):
    m = SimpleNamespace(**dict(zip(names, refs)))
    sp = lax.axis_index("sp")
    m.core = sp % 2
    prepare(m, m.lengths, sp // 2)
    m.gsum[...] = jnp.zeros_like(m.gsum)
    place_stage(m)
    select_rows(m, m.rowx, m.xs)
    select_rows(m, m.rowc, m.cot)
    norm_stage(m.xs, m.gains[0:1, :], m.gains[1:2, :], m.mid, m.normedT)
    for kind in range(3):
        qkv_stage(m, kind)

    @pl.loop(0, H // 2)
    def _(hp):
        attend_pair(m, hp)

    proj_stage(m)
    norm_stage(m.resid, m.gains[2:3, :], m.gains[3:4, :], m.mid, m.midT)

    @pl.loop(0, 4)
    def _(j):
        up_stage(m, j)

    transpose_to(m.cot, m.cotT)
    for u in range(4):
        grad_down(m, u)
    out_stage(m)
    for u in range(4):
        dinner_stage(m, u)
    dmid_stage(m)

    @pl.loop(0, 4)
    def _(j):
        grad_block(m, 4 + j, m.midT, m.gp, j * 768)

    dresid_stage(m)
    transpose_to(m.att, m.attT)
    grad_block(m, 8, m.attT, m.dattn, 0)
    datt_stage(m)

    @pl.loop(0, H // 2)
    def _(hp):
        attend_back_pair(m, hp)

    dnormed_stage(m)

    @pl.loop(0, 3)
    def _(j):
        grad_block(m, 9 + j, m.normedT, m.dqkv, j * 768)

    dtokens_stage(m)


def general_layer(tokens, lengths, cotangent, vectors, w_qkv, w_proj, w_up, w_down):
    T, D, FF = tokens.shape[0] * tokens.shape[1], tokens.shape[2], w_up.shape[1]
    n = D // 4
    gather = lambda v: lax.all_gather(v, "fsdp", axis=0, tiled=True)
    qkv, proj, up, down = (gather(w) for w in (w_qkv, w_proj, w_up, w_down))
    by_columns = lambda w: w.reshape(4, n, -1, D).transpose(2, 0, 1, 3)
    W = jnp.concatenate(
        [by_columns(qkv), by_columns(proj), by_columns(up), down.reshape(4, 4, n, D).transpose(1, 0, 2, 3)]
    )
    gains = [gather(v).astype(f32) for v in vectors]
    gains = [jnp.tile(g, D // g.shape[0]) for g in gains] + [jnp.zeros(D, f32)] * 2
    sp = lax.axis_index("sp")
    whole_row = lambda v: lax.dynamic_index_in_dim(lax.all_gather(v, "sp", axis=1, tiled=True), sp // 2, 0, False)
    rowx, rowc = (whole_row(v).reshape(2, T, D) for v in (tokens, cotangent))
    scratch = SCRATCH(T, D, FF)
    gsum = scratch.pop("gsum")
    del scratch["gains"]
    outs = dict(G=(W.shape, bf), osel=((T, D), bf), dtok=((T, D), bf), gsum=gsum)
    vmem = pl.BlockSpec(memory_space=pltpu.VMEM)
    names = ["lengths", "W", "rowx", "rowc", "gains"] + list(outs) + list(scratch)
    G, osel, dtok, gsum = pl.pallas_call(
        functools.partial(plain_kernel, names),
        out_shape=[jax.ShapeDtypeStruct(s, d) for s, d in outs.values()],
        in_specs=[pl.BlockSpec(memory_space=pltpu.SMEM)] + [vmem] * 4,
        out_specs=[vmem] * 4,
        scratch_shapes=[pltpu.VMEM(s, d) for s, d in scratch.values()],
        compiler_params=pltpu.CompilerParams(vmem_limit_bytes=VMEM_LIMIT),
        name="layer",
    )(lengths, W, rowx, rowc, jnp.stack(gains))

    def reduce(v):
        part = lax.psum_scatter(v.astype(bf), "fsdp", scatter_dimension=0, tiled=True)
        return lax.psum(part, ("rep", "sp")).astype(f32)

    natural = lambda g: g.reshape(-1, D, D).transpose(1, 0, 2).reshape(D, -1)
    g_down = G[0:4].transpose(1, 3, 0, 2).reshape(4 * D, D)
    heads = jnp.sum(gsum[4:6].reshape(2, -1, DH), axis=1)
    vecs = [reduce(v) for v in (gsum[0], gsum[1], gsum[2], gsum[3], heads[0], heads[1])]
    start = jnp.sum(jnp.where(jnp.arange(4)[None] < jnp.argmax(lengths, axis=1)[:, None], lengths, 0), axis=1)

    def back(half):
        rows = lax.all_gather(half, "sp", axis=0, tiled=True).reshape(2, 2 * T, D)
        rows = jnp.stack([jnp.roll(rows[r], start[r], axis=0) for r in range(2)])
        size = 2 * T // 4
        return lax.dynamic_slice_in_dim(rows, sp * size, size, axis=1).astype(f32)

    return (back(osel), back(dtok), vecs[0], vecs[1], reduce(natural(G[9:12])), vecs[4], vecs[5],
            reduce(natural(G[8:9])), vecs[2], vecs[3], reduce(natural(G[4:8])), reduce(g_down))


def pack_gains(vectors):
    rows = [jnp.pad(v.astype(f32), (0, 256 - v.shape[0])) for v in vectors]
    return jnp.concatenate([jnp.stack(rows), jnp.zeros((8 - len(rows), 256), f32)])


def finish(fin, outq, dtokq, vec):
    n = fin.shape[1]
    blocks = fin.astype(f32)
    z = lax.axis_index("fsdp")
    down = blocks[0:4].reshape(4 * n, -1).T
    up = jnp.concatenate([blocks[4 + j] for j in range(4)], axis=1)
    qkv = jnp.concatenate([blocks[9 + j] for j in range(3)], axis=1)
    wide = lax.dynamic_slice(vec[:4], (0, z * n), (4, n))
    heads = jnp.sum(vec[4:6].reshape(2, -1, DH), axis=1)
    k = DH // 4
    heads = lax.dynamic_slice(heads, (0, z * k), (2, k))
    return (outq.astype(f32), dtokq.astype(f32), wide[0], wide[1], qkv, heads[0], heads[1], blocks[8],
            wide[2], wide[3], up, down)


def per_device(tokens, lengths, cotangent, pre_gain, pre_shift, w_qkv, query_gain, key_gain, w_proj, mid_gain,
               mid_shift, w_up, w_down):
    vectors = (pre_gain, pre_shift, mid_gain, mid_shift, query_gain, key_gain)
    if tuple(lax.axis_size(a) for a in ("rep", "fsdp", "sp")) != (2, 4, 4):
        return general_layer(tokens, lengths, cotangent, vectors, w_qkv, w_proj, w_up, w_down)
    gpack = pack_gains(vectors)
    return finish(*fused_layer(tokens, lengths, cotangent, gpack, w_qkv, w_proj, w_up, w_down))


def solution(mesh):
    rows, vec, mat = P(("rep", "fsdp"), "sp", None), P("fsdp"), P("fsdp", None)
    return jax.shard_map(
        per_device,
        mesh=mesh,
        in_specs=(rows, P(("rep", "fsdp"), None), rows, vec, vec, mat, vec, vec, mat, vec, vec, mat, mat),
        out_specs=(rows, rows, vec, vec, mat, vec, vec, mat, vec, vec, mat, mat),
        check_vma=False,
    )
```

```python
import functools
import math
from types import SimpleNamespace

import jax
import jax.numpy as jnp
from jax import lax
from jax.experimental import pallas as pl
from jax.experimental.pallas import tpu as pltpu
from jax.sharding import PartitionSpec as P

H = 12
DH = 64
EPSILON = 1e-06
MASKED = 1e30
MESH = pl.DeviceIdType.MESH
VMEM_LIMIT = 67043328
bf = jnp.bfloat16
f32 = jnp.float32


def nn(a, b):
    return lax.dot_general(a, b, (((1,), (0,)), ((), ())), preferred_element_type=f32)


def nt(a, b):
    return lax.dot_general(a, b, (((1,), (1,)), ((), ())), preferred_element_type=f32)


def at(i, size, base=0):
    if isinstance(i, int) and isinstance(base, int):
        return pl.ds(base + i * size, size)
    return pl.ds(pl.multiple_of(base + i * size, math.gcd(size, base) if isinstance(base, int) else size), size)


def same_head(n):
    a = lax.broadcasted_iota(jnp.int32, (n, n), 0) // DH
    b = lax.broadcasted_iota(jnp.int32, (n, n), 1) // DH
    return (a == b).astype(f32).astype(bf)


def split2(x):
    hi = x.astype(bf)
    return hi, (x - hi.astype(f32)).astype(bf)


def standardize(x):
    mean = jnp.mean(x, axis=-1, keepdims=True)
    c = x - mean
    r = lax.rsqrt(jnp.mean(c * c, axis=-1, keepdims=True) + EPSILON)
    return c * r, r


def transpose_to(src, dst):
    @pl.loop(0, dst.shape[0] // 128)
    def _(i):
        dst[at(i, 128), :] = src[:, at(i, 128)].astype(f32).T.astype(bf)


def wcols(m, b, s):
    w = m.W[b, :, :, s]
    return w.reshape(w.shape[0] * w.shape[1], w.shape[2])


def wrows(m, b, i):
    w = m.W[b, pl.ds(2 * i, 2), :, :]
    return w.reshape(2 * w.shape[1], w.shape[2])


def select_rows(m, rowbuf, dst):
    T, D = dst.shape

    @pl.loop(0, D // 256)
    def _(i):
        s = at(i, 256)
        dst[:, s] = (nn(m.ebuf[10], rowbuf[0, :, s]) + nn(m.ebuf[11], rowbuf[1, :, s])).astype(bf)


def select_cot(m):
    T, D = m.cot.shape

    @pl.loop(0, D // 256)
    def _(i):
        s = at(i, 256)
        m.cot[:, s] = (nn(m.rowx[0, :, 0:T], m.rowc[0, :, s]) + nn(m.rowx[1, :, 0:T], m.rowc[1, :, s])).astype(bf)


def place_stage(m):
    T = m.xs.shape[0]
    row = lax.broadcasted_iota(jnp.int32, (T, T), 0) + m.start + T * m.core
    row = jnp.where(row >= 2 * T, row - 2 * T, row)
    col = lax.broadcasted_iota(jnp.int32, (T, T), 1)
    m.ebuf[10] = (row == col).astype(f32).astype(bf)
    m.ebuf[11] = (row == col + T).astype(f32).astype(bf)
    t = row[:, :128]
    pic = sum((t >= e).astype(jnp.int32) for e in m.ends)
    lane = col[:, :128]
    hot = (lane == pic).astype(f32)
    m.maskq[...] = (hot * MASKED).astype(bf)
    m.maskk[...] = jnp.where(lane < 4, hot - 1.0, 0.0).astype(bf)


def restore_quarter(m, cat, quarter):
    T = m.xs.shape[0]
    n = T // 2
    i = lax.broadcasted_iota(jnp.int32, (n, T), 0) + quarter * n - m.start
    i = jnp.where(i < 0, i + 2 * T, i)
    col = lax.broadcasted_iota(jnp.int32, (n, T), 1)
    a = (i == col).astype(f32).astype(bf)
    b = (i == col + T).astype(f32).astype(bf)
    return (nn(a, cat[0]) + nn(b, cat[1])).astype(bf)


def gains_stage(m):
    D = m.gains.shape[1]
    n = D // 4
    k = DH // 4
    lane = lax.broadcasted_iota(jnp.int32, (256, D), 0)
    col = lax.broadcasted_iota(jnp.int32, (256, D), 1)
    wide = jnp.zeros((8, D), f32)
    head = jnp.zeros((8, D), f32)
    for u in range(4):
        g = m.gbuf[u].astype(bf)
        wide += nn(g, ((col == lane + n * u) & (lane < n)).astype(f32).astype(bf))
        head += nn(g, ((col % DH == lane + k * u) & (lane < k)).astype(f32).astype(bf))
    r = lax.broadcasted_iota(jnp.int32, (8, D), 0)
    m.gains[...] = jnp.where(r < 4, wide, head)


def norm_stage(src, gain, shift, dst, dstT):
    @pl.loop(0, src.shape[0] // 64)
    def _(i):
        s = at(i, 64)
        xh, _ = standardize(src[s, :].astype(f32))
        dst[s, :] = (xh * gain + shift).astype(bf)

    transpose_to(dst, dstT)


def qkv_stage(m, kind):
    D = m.xs.shape[1]

    @pl.loop(0, D // 256)
    def _(i):
        off, s = at(i, 256), at(i, 256, kind * D)
        acc = nn(m.mid[...], wcols(m, kind, off))
        if kind == 2:
            m.v[:, off] = acc.astype(bf)
            return
        B = same_head(256)
        hi, lo = split2(acc)
        c = acc - (nn(hi, B) + nn(lo, B)) * (1.0 / DH)
        r = lax.rsqrt(nn((c * c).astype(bf), B) * (1.0 / DH) + EPSILON)
        xh = c * r
        m.qkh[:, s] = xh.astype(bf)
        m.qkr[:, s] = r.astype(bf)
        val = (xh * m.gains[4 + kind : 5 + kind, off]).astype(bf)
        if kind == 0:
            m.q[:, off] = (val.astype(f32) * (1.0 / math.sqrt(DH))).astype(bf)
        else:
            m.k[:, off] = val


def lane_half(T, e):
    lane = lax.broadcasted_iota(jnp.int32, (T, 128), 1)
    return (lane < DH) if e == 0 else (lane >= DH)


def attend_pair(m, hp):
    T = m.q.shape[0]
    s = at(hp, 128)
    q2, k2, v2 = m.q[:, s].astype(f32), m.k[:, s], m.v[:, s]
    kx = jnp.concatenate([k2, m.maskk[...]], axis=1)
    outs = []
    for e in (0, 1):
        qe = jnp.where(lane_half(T, e), q2, 0.0).astype(bf)
        E = jnp.exp(nt(jnp.concatenate([qe, m.maskq[...]], axis=1), kx))
        p = (E * (1.0 / jnp.sum(E, axis=-1, keepdims=True))).astype(bf)
        m.ebuf[2 * hp + e] = p
        outs.append(nn(p, v2))
    m.att[:, s] = jnp.where(lane_half(T, 0), outs[0], outs[1]).astype(bf)


def proj_stage(m):
    @pl.loop(0, m.xs.shape[1] // 256)
    def _(i):
        s = at(i, 256)
        m.resid[:, s] = m.xs[:, s].astype(f32) + nn(m.att[...], wcols(m, 3, s))


def gelu_both(x):
    z = jnp.abs(x) * (1.0 / math.sqrt(2.0))
    t = 1.0 / (1.0 + 0.3275911 * z)
    p = ((((1.061405429 * t - 1.453152027) * t + 1.421413741) * t - 0.284496736) * t + 0.254829592) * t
    ex = jnp.exp(-0.5 * x * x)
    tail = 0.5 * p * ex
    phi = jnp.where(x < 0, tail, 1.0 - tail)
    return x * phi, phi + x * ex * (1.0 / math.sqrt(2.0 * math.pi))


def up_stage(m, j):
    D = m.xs.shape[1]

    @pl.loop(0, D // 256)
    def _(i):
        a, d = gelu_both(nn(m.mid[...], wcols(m, 4 + j, at(i, 256))))
        s = at(i, 256, j * D)
        m.act[:, s] = a.astype(bf)
        m.gp[:, s] = d.astype(bf)


def out_stage(m):
    D = m.xs.shape[1]

    @pl.loop(0, D // 256)
    def _(i):
        s = at(i, 256)
        acc = m.resid[:, s]
        for u in range(4):
            w = m.W[8:12, u, :, s]
            acc += nn(m.act[:, u * D : (u + 1) * D], w.reshape(D, 256))
        m.osel[:, s] = acc.astype(bf)


def dinner_stage(m, u):
    D = m.xs.shape[1]
    for i in range(2):
        w = m.W[8 + 2 * i : 10 + 2 * i, u, :, :]
        s = at(i, D // 2, u * D)
        d = nt(m.cot[...], w.reshape(D // 2, D))
        m.gp[:, s] = (d * m.gp[:, s].astype(f32)).astype(bf)


def dmid_stage(m):
    D = m.xs.shape[1]
    n = D // 2

    @pl.loop(0, 2)
    def _(i):
        acc = nt(m.gp[:, 0:D], wrows(m, 4, i))
        for j in range(1, 4):
            acc += nt(m.gp[:, j * D : (j + 1) * D], wrows(m, 4 + j, i))
        m.dres[:, at(i, n)] = acc


def dresid_stage(m):
    T, D = m.dres.shape
    g = m.gains[2:3, :]

    @pl.loop(0, T // 64)
    def _(i):
        s = at(i, 64)
        dm = m.dres[s, :]
        xh, r = standardize(m.resid[s, :])
        dx = dm * g
        m1 = jnp.mean(dx, axis=-1, keepdims=True)
        m2 = jnp.mean(dx * xh, axis=-1, keepdims=True)
        dr = m.cot[s, :].astype(f32) + r * (dx - m1 - xh * m2)
        m.dres[s, :] = dr
        m.dattn[s, :] = dr.astype(bf)
        m.gsum[2:3, :] += jnp.sum(dm * xh, axis=0, keepdims=True)
        m.gsum[3:4, :] += jnp.sum(dm, axis=0, keepdims=True)


def datt_stage(m):
    n = m.xs.shape[1] // 2

    @pl.loop(0, 2)
    def _(i):
        m.datt[:, at(i, n)] = nt(m.dattn[...], wrows(m, 3, i)).astype(bf)


def attend_back_pair(m, hp):
    T, D = m.q.shape
    s = at(hp, 128)
    do = m.datt[:, s].astype(f32)
    B = same_head(128)
    hi, lo = split2(do * m.att[:, s].astype(f32))
    dl = nn(hi, B) + nn(lo, B)
    k2, v2 = m.k[:, s], m.v[:, s]
    lane = lax.broadcasted_iota(jnp.int32, (T, 128), 1)
    vx = jnp.concatenate([v2, (lane < 2).astype(f32).astype(bf)], axis=1)
    doT = do.T.astype(bf)
    qT = m.q[:, s].astype(f32).T.astype(bf)
    dqs, dks, dvs = [], [], []
    for e in (0, 1):
        de = jnp.where(lane_half(T, e), do, 0.0).astype(bf)
        dle = dl[:, e * DH : e * DH + 1]
        dh = dle.astype(bf).astype(f32)
        dmask = jnp.where(lane == 0, -dh, jnp.where(lane == 1, dh - dle, 0.0)).astype(bf)
        t = nt(jnp.concatenate([de, dmask], axis=1), vx)
        E = m.ebuf[2 * hp + e]
        ds = (E.astype(f32) * t).astype(bf)
        dqs.append(nn(ds, k2))
        dks.append(nn(qT[e * DH : (e + 1) * DH, :], ds))
        dvs.append(nn(doT[e * DH : (e + 1) * DH, :], E))
    dq = jnp.where(lane_half(T, 0), dqs[0], dqs[1]) * (1.0 / math.sqrt(DH))
    dk = jnp.concatenate(dks, axis=0).T
    dv = jnp.concatenate(dvs, axis=0).T
    m.dqkv[:, at(hp, 128, 2 * D)] = dv.astype(bf)
    for kind, d in ((0, dq), (1, dk)):
        d = d.astype(bf).astype(f32)
        w = at(hp, 128, kind * D)
        xh = m.qkh[:, w].astype(f32)
        r = m.qkr[:, w].astype(f32)
        m.gsum[4 + kind : 5 + kind, s] = jnp.sum(d * xh, axis=0, keepdims=True)
        dx = d * m.gains[4 + kind : 5 + kind, s]
        h1, l1 = split2(dx)
        m1 = (nn(h1, B) + nn(l1, B)) * (1.0 / DH)
        h2, l2 = split2(dx * xh)
        m2 = (nn(h2, B) + nn(l2, B)) * (1.0 / DH)
        m.dqkv[:, w] = (r * (dx - m1 - xh * m2)).astype(bf)


def dnormed_stage(m):
    D = m.xs.shape[1]
    n = D // 2

    @pl.loop(0, 2)
    def _(i):
        acc = nt(m.dqkv[:, 0:D], wrows(m, 0, i))
        for j in range(1, 3):
            acc += nt(m.dqkv[:, j * D : (j + 1) * D], wrows(m, j, i))
        m.resid[:, at(i, n)] = acc


def dtokens_stage(m):
    T, D = m.dres.shape
    g = m.gains[0:1, :]

    @pl.loop(0, T // 64)
    def _(i):
        s = at(i, 64)
        dn = m.resid[s, :]
        xh, r = standardize(m.xs[s, :].astype(f32))
        dx = dn * g
        m1 = jnp.mean(dx, axis=-1, keepdims=True)
        m2 = jnp.mean(dx * xh, axis=-1, keepdims=True)
        m.dtok[s, :] = (m.dres[s, :] + r * (dx - m1 - xh * m2)).astype(bf)
        m.gsum[0:1, :] += jnp.sum(dn * xh, axis=0, keepdims=True)
        m.gsum[1:2, :] += jnp.sum(dn, axis=0, keepdims=True)


def grad_down(m, u):
    D = m.xs.shape[1]
    n = D // 4

    @pl.loop(0, D // 256)
    def _(i):
        r = nn(m.cotT[...], m.act[:, at(i, 256, u * D)]).astype(bf)
        for j in range(4):
            m.G[j, u, :, at(i, 256)] = r[j * n : (j + 1) * n]


def grad_block(m, b, lhsT, rhs, base):
    D = m.xs.shape[1]
    n = D // 4

    @pl.loop(0, D // 256)
    def _(i):
        r = nn(lhsT[...], rhs[:, at(i, 256, base)]).astype(bf)
        for u in range(4):
            m.G[b, u, :, at(i, 256)] = r[u * n : (u + 1) * n]


GATHER_Y = ()
REDUCE_X = ()
SLOTS = (2, 4, 4, 4, 4, 4, 4)
GATHER_EVERY, GATHER_LAG = 3.6, {1: 4.0, 2: 7.0, 3: 15.0, 4: 17.5}
REDUCE_EVERY, REDUCE_LAG = 4.75, (0.0, 2.0, 9.0, 15.0, 19.0, 23.0, 27.0, 29.0)


class Comm:
    def __init__(self, m):
        self.m = m
        self.x, self.z, sp = lax.axis_index("rep"), lax.axis_index("fsdp"), lax.axis_index("sp")
        self.y, self.c = sp // 2, sp % 2
        x, y, z, c = self.x, self.y, self.z, self.c
        nx, ny = (1 - x, z, sp), (x, z, 2 * (1 - y) + c)
        self.nx, self.ny = nx, ny
        n1 = (x + (1 - c) * (1 - 2 * x), z, 2 * (y + c * (1 - 2 * y)) + c)
        n2 = (x + c * (1 - 2 * x), z, 2 * (y + (1 - c) * (1 - 2 * y)) + c)
        self.orders = {"x": (x, y, nx, ny), "y": (y, x, ny, nx), "xy": (x + c * (y - x), y + c * (x - y), n1, n2)}
        self.core = (x, z, 2 * y + 1 - c)
        self.zat = lambda u: (x, u, sp)
        self.z1 = z + 1 - 2 * (z % 2)
        self.zt = 3 - z
        self.mine = at(c, 384)
        self.other = at(1 - c, 384)

    def gather_order(self, b):
        return self.orders["y" if b in GATHER_Y else "xy"]

    def reduce_order(self, b):
        return self.orders["x" if b in REDUCE_X else "xy"]

    def barrier(self):
        sem = pltpu.get_barrier_semaphore()
        peers = [self.nx, self.ny, self.core] + [self.zat((self.z + d) % 4) for d in (1, 2, 3)]
        for p in peers:
            pl.semaphore_signal(sem, inc=1, device_id=p, device_id_type=MESH)
        pl.semaphore_wait(sem, len(peers))

    def copy(self, src, dst, send, recv, dev):
        return pltpu.make_async_remote_copy(
            src_ref=src, dst_ref=dst, send_sem=send, recv_sem=recv, device_id=dev, device_id_type=MESH
        )

    def row_copies(self, arg, buf, k):
        s, r = self.m.rsem.at[0, k], self.m.rsem.at[1, k]
        mine = buf.at[self.y, at(self.c, 256)]
        there = buf.at[1 - self.y, at(self.c, 256)]
        local = pltpu.make_async_copy(arg.at[self.y], mine, s.at[0])
        near = self.copy(arg.at[self.y], mine, s.at[1], r.at[1], self.core)
        far = self.copy(arg.at[1 - self.y], mine, s.at[2], r.at[2], self.ny)
        pass_on = self.copy(there, there, s.at[3], r.at[3], self.core)
        return local, near, far, pass_on

    def row_start(self, arg, buf, k):
        local, near, far, _ = self.row_copies(arg, buf, k)
        far.start()
        near.start()
        local.start()

    def row_pass(self, arg, buf, k):
        _, _, far, pass_on = self.row_copies(arg, buf, k)
        far.wait_recv()
        pass_on.start()

    def row_wait(self, arg, buf, k):
        local, near, far, pass_on = self.row_copies(arg, buf, k)
        local.wait()
        near.wait()
        far.wait_send()
        pass_on.wait()

    def gain_copies(self):
        m = self.m
        out = [pltpu.make_async_copy(m.gpack, m.gbuf.at[self.z], m.gsem.at[0, 0])]
        for d in (1, 2, 3):
            dev = self.zat((self.z + d) % 4)
            out.append(self.copy(m.gpack, m.gbuf.at[self.z], m.gsem.at[0, d], m.gsem.at[1, d], dev))
        return out

    def shard(self, b, rows, cols):
        m = self.m
        arg, r0, c0 = (m.a_qkv, 0, 768 * b) if b < 3 else (m.a_proj, 0, 0) if b == 3 else (
            (m.a_up, 0, 768 * (b - 4)) if b < 8 else (m.a_down, 192 * (b - 8), 0))
        return arg.at[pl.ds(pl.multiple_of(r0 + rows[0], 16), rows[1]), pl.ds(pl.multiple_of(c0 + cols[0], 128), cols[1])]

    def own_copy(self, b):
        return pltpu.make_async_copy(self.shard(b, (0, 192), (0, 768)), self.m.W.at[b, self.z], self.m.wsem.at[0, 0, b])

    def z_start(self, b):
        m = self.m
        f1, f2, _, _ = self.gather_order(b)
        q = 2 * f2 + f1
        src = self.shard(b, (48 * q, 48), (384 * self.c, 384))
        for d in (1, 2, 3):
            dst = m.W.at[b, self.z, at(q, 48), self.mine]
            self.copy(src, dst, m.wsem.at[0, 1, b], m.wsem.at[1, 1, b], self.zat((self.z + d) % 4)).start()

    def plane(self, k, b):
        m = self.m
        f1, f2, n1, n2 = self.gather_order(b)
        rows, dev = {2: (at(2 * f2 + f1, 48), n1), 3: (at(f2, 96), n2), 4: (pl.ds(0, 192), self.core)}[k]
        out = []
        for d in (1, 2, 3):
            ref = m.W.at[b, (self.z + d) % 4, rows, self.mine]
            out.append(self.copy(ref, ref, m.wsem.at[0, k, b], m.wsem.at[1, k, b], dev))
        return out

    def w_all(self, k, b):
        m = self.m
        f1, f2, n1, n2 = self.gather_order(b)
        part = at(2 * f2 + f1, 48)
        rows, dev = {1: (part, self.core), 2: (part, n1), 3: (at(f2, 96), n2), 4: (pl.ds(0, 192), self.core)}[k]
        ref = m.W.at[b, 0:3, rows, self.mine]
        return self.copy(ref, ref, m.wsem.at[0, k, b], m.wsem.at[1, k, b], dev)

    def ag_step(self, k, b):
        self.w_all(k, b).wait_recv()
        if k < 4:
            for cp in self.plane(k + 1, b):
                cp.start()
        else:
            for j in (1, 2, 3, 4):
                self.w_all(j, b).wait_send()

    def rs_copies(self, k, b):
        m = self.m
        G, z = m.G, self.z
        f1, f2, n1, n2 = self.reduce_order(b)
        slot = b % SLOTS[k]
        rows = at(f1, 96)
        sem = lambda j: (m.psem.at[0, j, slot], m.psem.at[1, j, slot])
        if k == 0:
            return [self.copy(G.at[b, :, :, self.other], m.rA.at[slot], *sem(0), self.core)]
        if k == 1:
            return [self.copy(G.at[b, :, at(1 - f1, 96), self.mine], m.rB.at[slot], *sem(1), n1)]
        if k == 2:
            return [
                self.copy(G.at[b, self.z1, rows, self.mine], m.rC.at[slot, 0], *sem(2), self.zat(self.z1)),
                self.copy(G.at[b, 3 - self.z1, rows, self.mine], m.rC.at[slot, 1], *sem(7), self.zat(self.z1)),
            ]
        if k == 3:
            return [self.copy(G.at[b, self.zt, rows, self.mine], m.rD.at[slot], *sem(3), self.zat(self.zt))]
        if k == 4:
            return [self.copy(G.at[b, z, rows, self.mine], m.rE.at[slot], *sem(4), n2)]
        if k == 5:
            ref = G.at[b, z, rows, self.mine]
            return [self.copy(ref, ref, *sem(5), n1)]
        ref = G.at[b, z, :, self.mine]
        return [self.copy(ref, ref, *sem(6), self.core)]

    def rs_step(self, k, b):
        m = self.m
        G, z = m.G, self.z
        rows = at(self.reduce_order(b)[0], 96)
        if k > 0:
            slot = b % SLOTS[k - 1]
            for cp in self.rs_copies(k - 1, b):
                cp.wait()
        if k == 1:

            @pl.loop(0, 4)
            def _(u):
                G[b, u, :, self.mine] = (G[b, u, :, self.mine].astype(f32) + m.rA[slot, u].astype(f32)).astype(bf)
        elif k == 2:

            @pl.loop(0, 4)
            def _(u):
                G[b, u, rows, self.mine] = (G[b, u, rows, self.mine].astype(f32) + m.rB[slot, u].astype(f32)).astype(bf)
        elif k == 3:
            for i, u in ((0, z), (1, self.zt)):
                G[b, u, rows, self.mine] = (G[b, u, rows, self.mine].astype(f32) + m.rC[slot, i].astype(f32)).astype(bf)
        elif k in (4, 5):
            r = (m.rD if k == 4 else m.rE)[slot]
            G[b, z, rows, self.mine] = (G[b, z, rows, self.mine].astype(f32) + r.astype(f32)).astype(bf)
        if k < 7:
            for cp in self.rs_copies(k, b):
                cp.start()
        else:
            self.fin_copy(b).start()

    def fin_copy(self, b):
        return pltpu.make_async_copy(self.m.G.at[b, self.z], self.m.fin.at[b], self.m.fsem.at[b])

    def vec_copy(self, i):
        m = self.m
        dev = [self.core, self.nx, self.ny, self.zat(self.z1), self.zat(self.zt)][i]
        return self.copy(m.gs.at[i], m.gr.at[i], m.vsem.at[0, i], m.vsem.at[1, i], dev)

    def vec_step(self, i):
        m = self.m
        if i == 0:
            m.gs[0] = m.gsum[...]
        else:
            self.vec_copy(i - 1).wait()
            m.gs[i] = m.gs[i - 1] + m.gr[i - 1]
        if i < 5:
            self.vec_copy(i).start()
        else:
            m.vec[...] = m.gs[5]

    def cat_copy(self, cat, k):
        half = cat.at[self.c]
        return self.copy(half, half, self.m.osem.at[0, k, 0], self.m.osem.at[1, k, 0], self.core)

    def quarter_copies(self, dst, k):
        m = self.m
        far = self.copy(m.quart.at[1], dst.at[self.y], m.osem.at[0, k, 1], m.osem.at[1, k, 1], self.ny)
        near = pltpu.make_async_copy(m.quart.at[0], dst.at[self.y], m.osem.at[0, k, 2])
        return far, near

    def result_send(self, cat, dst, k):
        m = self.m
        self.cat_copy(cat, k).wait()
        m.quart[1] = restore_quarter(m, cat, 2 * (1 - self.y) + self.c)
        far, near = self.quarter_copies(dst, k)
        far.start()
        m.quart[0] = restore_quarter(m, cat, 2 * self.y + self.c)
        near.start()

    def result_wait(self, dst, k):
        far, near = self.quarter_copies(dst, k)
        far.wait()
        near.wait()


SCRATCH = lambda T, D, FF: dict(
    gains=((8, D), f32), maskq=((T, 128), bf), maskk=((T, 128), bf), xs=((T, D), bf), cot=((T, D), bf),
    mid=((T, D), bf), normedT=((D, T), bf), midT=((D, T), bf), cotT=((D, T), bf),
    q=((T, D), bf), k=((T, D), bf), v=((T, D), bf), qkh=((T, 2 * D), bf), qkr=((T, 2 * D), bf),
    ebuf=((H, T, T), bf), att=((T, D), bf), resid=((T, D), f32),
    act=((T, FF), bf), gp=((T, FF), bf), dres=((T, D), f32), datt=((T, D), bf), gsum=((8, D), f32),
)


def prepare(m, lengths, y):
    T = m.xs.shape[0]
    l = [lengths[y, k] for k in range(4)]
    m.ends = [l[0], l[0] + l[1], l[0] + l[1] + l[2]]
    m.start = jnp.where(l[0] == T, 0, jnp.where(l[1] == T, m.ends[0], jnp.where(l[2] == T, m.ends[1], m.ends[2])))
    m.dattn = m.mid
    m.dqkv = m.act
    m.attT = m.cotT


class Order:
    def __init__(self, cm):
        self.cm = cm
        self.now = 0.0
        self.steps = sorted((GATHER_EVERY * b + lag, k, b) for k, lag in GATHER_LAG.items() for b in range(12))
        self.hooks = {}
        self.sums = sorted((REDUCE_EVERY * b + lag, -k, b) for k, lag in enumerate(REDUCE_LAG) for b in range(12))
        self.check_slots()
        self.begin = 0.0
        self.ready = 0

    def check_slots(self):
        place = {(-k, b): i for i, (_, k, b) in enumerate(self.sums)}
        for k in range(5):
            for b in range(SLOTS[k], 12):
                used = place[k + 1, b - SLOTS[k]]
                seen = [x for x in range(b) if place[k, x] > used and place[k + 1, x] < place[k, b]]
                assert seen, (k, b)

    def gather_step(self):
        t, k, b = self.steps.pop(0)
        self.cm.ag_step(k, b)
        if (k, b) in self.hooks:
            self.hooks[k, b]()
        return t

    def need(self, b):
        while any(k == 4 and x == b for _, k, x in self.steps):
            self.now = max(self.now, self.gather_step())

    def reduce_step(self):
        t, k, b = self.sums.pop(0)
        self.cm.rs_step(-k, b)

    def pump(self):
        while self.steps and self.steps[0][0] <= self.now:
            self.gather_step()
        while self.ready and self.sums and self.begin + self.sums[0][0] <= self.now:
            _, k, b = self.sums[0]
            if b >= self.ready:
                self.begin = self.now - self.sums[0][0] + 0.01
                break
            self.reduce_step()

    def run(self, us, f, *args):
        self.pump()
        f(*args)
        self.now += us


def loop_pairs(f, m, lo, hi):
    @pl.loop(lo, hi)
    def _(hp):
        f(m, hp)


def layer_kernel(comm_names, *refs):
    m = SimpleNamespace(**dict(zip(comm_names, refs)))
    cm = Comm(m)
    m.osel, m.dtok = m.rowx.at[cm.c], m.rowc.at[cm.c]
    m.core = cm.c
    prepare(m, m.lengths, cm.y)
    o = Order(cm)
    m.gpack[...] = jnp.zeros_like(m.gpack)
    for i in range(6):
        g = getattr(m, "g%d" % i)
        m.gpack[i : i + 1, 0 : g.shape[0]] = g[...].astype(f32).reshape(1, g.shape[0])
    m.gsum[...] = jnp.zeros_like(m.gsum)
    cm.barrier()
    cm.row_start(m.tokens, m.rowx, 0)
    gains = cm.gain_copies()
    for g in gains:
        g.start()
    for b in range(12):
        cm.z_start(b)
        cm.own_copy(b).start()
    o.hooks[2, 6] = lambda: cm.row_start(m.cotangent, m.rowc, 1)
    o.run(4.0, place_stage, m)
    o.run(0, cm.row_pass, m.tokens, m.rowx, 0)
    for g in gains:
        g.wait()
    o.run(5.0, gains_stage, m)
    o.run(0, cm.row_wait, m.tokens, m.rowx, 0)
    o.run(2.0, select_rows, m, m.rowx, m.xs)
    for h in range(2):
        m.rowx[h, :, 0 : m.ebuf.shape[1]] = m.ebuf[10 + h]
    o.run(2.0, norm_stage, m.xs, m.gains[0:1, :], m.gains[1:2, :], m.mid, m.normedT)
    for b in range(12):
        cm.own_copy(b).wait()
    for kind in range(3):
        o.need(kind)
        o.run(2.2, qkv_stage, m, kind)
    for i in range(3):
        o.run(1.6, loop_pairs, attend_pair, m, 2 * i, 2 * i + 2)
    o.need(3)
    o.run(1.7, proj_stage, m)
    o.run(2.4, norm_stage, m.resid, m.gains[2:3, :], m.gains[3:4, :], m.mid, m.midT)
    for j in range(4):
        o.need(4 + j)
        o.run(1.4, up_stage, m, j)
    while (1, 0) in o.hooks or any(k == 2 and b <= 6 for _, k, b in o.steps):
        o.gather_step()
    o.run(0, cm.row_pass, m.cotangent, m.rowc, 1)
    o.pump()
    o.run(0, cm.row_wait, m.cotangent, m.rowc, 1)
    o.run(2.0, select_cot, m)
    o.run(0.7, transpose_to, m.cot, m.cotT)
    for u in range(4):
        o.run(1.3, grad_down, m, u)
    o.ready, o.begin = 4, o.now
    o.pump()
    o.need(11)
    o.run(5.2, out_stage, m)
    cm.cat_copy(m.rowx, 0).start()
    for u in range(4):
        o.run(1.3, dinner_stage, m, u)
    o.run(3.8, dmid_stage, m)
    o.run(2.0, cm.result_send, m.rowx, m.outq, 0)
    for j in range(4):
        o.run(0.95, grad_block, m, 4 + j, m.midT, m.gp, j * 768)
        o.ready += 1
    o.run(3.0, dresid_stage, m)
    o.run(0.7, transpose_to, m.att, m.attT)
    o.run(0.9, grad_block, m, 8, m.attT, m.dattn, 0)
    o.ready += 1
    o.run(1.0, datt_stage, m)
    for i in range(3):
        o.run(3.5, loop_pairs, attend_back_pair, m, 2 * i, 2 * i + 2)
    for j in range(3):
        o.run(1.0, grad_block, m, 9 + j, m.normedT, m.dqkv, j * 768)
        o.ready += 1
    o.run(3.0, dnormed_stage, m)
    o.run(2.0, dtokens_stage, m)
    cm.cat_copy(m.rowc, 1).start()
    cm.vec_step(0)
    o.pump()
    cm.result_wait(m.outq, 0)
    cm.result_send(m.rowc, m.dtokq, 1)
    i = 1
    while o.sums:
        for _ in range(6):
            if o.sums:
                o.reduce_step()
        if i < 6:
            cm.vec_step(i)
            i += 1
    while i < 6:
        cm.vec_step(i)
        i += 1
    for b in range(12):
        cm.fin_copy(b).wait()
    cm.result_wait(m.dtokq, 1)


def fused_layer(tokens, lengths, cotangent, vectors, w_qkv, w_proj, w_up, w_down):
    T, D, FF = tokens.shape[0] * tokens.shape[1], tokens.shape[2], w_up.shape[1]
    any_, vmem = pl.BlockSpec(memory_space=pl.ANY), pl.BlockSpec(memory_space=pltpu.VMEM)
    ins = ["tokens", "lengths", "cotangent", "a_qkv", "a_proj", "a_up", "a_down"] + ["g%d" % i for i in range(6)]
    outs = dict(
        fin=((12, D // 4, D), bf), outq=(tokens.shape, bf), dtokq=(tokens.shape, bf), vec=((8, D), f32)
    )
    scratch = SCRATCH(T, D, FF)
    scratch.update(
        W=((12, 4, D // 4, D), bf), G=((12, 4, D // 4, D), bf), rowx=((2, T, D), bf), rowc=((2, T, D), bf),
        gbuf=((4, 8, 256), f32), gpack=((8, 256), f32),
        rA=((SLOTS[0], 4, 192, 384), bf), rB=((SLOTS[1], 4, 96, 384), bf), rC=((SLOTS[2], 2, 96, 384), bf),
        rD=((SLOTS[3], 96, 384), bf),
        rE=((SLOTS[4], 96, 384), bf), quart=((2, T // 2, D), bf), gs=((6, 8, D), f32), gr=((5, 8, D), f32),
    )
    sems = dict(
        rsem=(2, 2, 4), gsem=(2, 4), wsem=(2, 5, 12), psem=(2, 8, 4), fsem=(12,), vsem=(2, 5), osem=(2, 2, 3)
    )
    names = ins + list(outs) + list(scratch) + list(sems)
    return pl.pallas_call(
        functools.partial(layer_kernel, names),
        out_shape=[jax.ShapeDtypeStruct(s, d) for s, d in outs.values()],
        in_specs=[any_, pl.BlockSpec(memory_space=pltpu.SMEM), any_] + [any_] * 4 + [vmem] * 6,
        out_specs=[any_, any_, any_, vmem],
        scratch_shapes=[pltpu.VMEM(s, d) for s, d in scratch.values()]
        + [pltpu.SemaphoreType.DMA(s) for s in sems.values()],
        compiler_params=pltpu.CompilerParams(collective_id=0, has_side_effects=True, vmem_limit_bytes=VMEM_LIMIT),
        name="layer",
    )(tokens, lengths, cotangent, w_qkv, w_proj, w_up, w_down, *vectors)


def plain_kernel(names, *refs):
    m = SimpleNamespace(**dict(zip(names, refs)))
    sp = lax.axis_index("sp")
    m.core = sp % 2
    prepare(m, m.lengths, sp // 2)
    m.gsum[...] = jnp.zeros_like(m.gsum)
    place_stage(m)
    select_rows(m, m.rowx, m.xs)
    select_rows(m, m.rowc, m.cot)
    norm_stage(m.xs, m.gains[0:1, :], m.gains[1:2, :], m.mid, m.normedT)
    for kind in range(3):
        qkv_stage(m, kind)

    @pl.loop(0, H // 2)
    def _(hp):
        attend_pair(m, hp)

    proj_stage(m)
    norm_stage(m.resid, m.gains[2:3, :], m.gains[3:4, :], m.mid, m.midT)

    @pl.loop(0, 4)
    def _(j):
        up_stage(m, j)

    transpose_to(m.cot, m.cotT)
    for u in range(4):
        grad_down(m, u)
    out_stage(m)
    for u in range(4):
        dinner_stage(m, u)
    dmid_stage(m)

    @pl.loop(0, 4)
    def _(j):
        grad_block(m, 4 + j, m.midT, m.gp, j * 768)

    dresid_stage(m)
    transpose_to(m.att, m.attT)
    grad_block(m, 8, m.attT, m.dattn, 0)
    datt_stage(m)

    @pl.loop(0, H // 2)
    def _(hp):
        attend_back_pair(m, hp)

    dnormed_stage(m)

    @pl.loop(0, 3)
    def _(j):
        grad_block(m, 9 + j, m.normedT, m.dqkv, j * 768)

    dtokens_stage(m)


def general_layer(tokens, lengths, cotangent, vectors, w_qkv, w_proj, w_up, w_down):
    T, D, FF = tokens.shape[0] * tokens.shape[1], tokens.shape[2], w_up.shape[1]
    n = D // 4
    gather = lambda v: lax.all_gather(v, "fsdp", axis=0, tiled=True)
    qkv, proj, up, down = (gather(w) for w in (w_qkv, w_proj, w_up, w_down))
    by_columns = lambda w: w.reshape(4, n, -1, D).transpose(2, 0, 1, 3)
    W = jnp.concatenate(
        [by_columns(qkv), by_columns(proj), by_columns(up), down.reshape(4, 4, n, D).transpose(1, 0, 2, 3)]
    )
    gains = [gather(v).astype(f32) for v in vectors]
    gains = [jnp.tile(g, D // g.shape[0]) for g in gains] + [jnp.zeros(D, f32)] * 2
    sp = lax.axis_index("sp")
    whole_row = lambda v: lax.dynamic_index_in_dim(lax.all_gather(v, "sp", axis=1, tiled=True), sp // 2, 0, False)
    rowx, rowc = (whole_row(v).reshape(2, T, D) for v in (tokens, cotangent))
    scratch = SCRATCH(T, D, FF)
    gsum = scratch.pop("gsum")
    del scratch["gains"]
    outs = dict(G=(W.shape, bf), osel=((T, D), bf), dtok=((T, D), bf), gsum=gsum)
    vmem = pl.BlockSpec(memory_space=pltpu.VMEM)
    names = ["lengths", "W", "rowx", "rowc", "gains"] + list(outs) + list(scratch)
    G, osel, dtok, gsum = pl.pallas_call(
        functools.partial(plain_kernel, names),
        out_shape=[jax.ShapeDtypeStruct(s, d) for s, d in outs.values()],
        in_specs=[pl.BlockSpec(memory_space=pltpu.SMEM)] + [vmem] * 4,
        out_specs=[vmem] * 4,
        scratch_shapes=[pltpu.VMEM(s, d) for s, d in scratch.values()],
        compiler_params=pltpu.CompilerParams(vmem_limit_bytes=VMEM_LIMIT),
        name="layer",
    )(lengths, W, rowx, rowc, jnp.stack(gains))

    def reduce(v):
        part = lax.psum_scatter(v.astype(bf), "fsdp", scatter_dimension=0, tiled=True)
        return lax.psum(part, ("rep", "sp")).astype(f32)

    natural = lambda g: g.reshape(-1, D, D).transpose(1, 0, 2).reshape(D, -1)
    g_down = G[0:4].transpose(1, 3, 0, 2).reshape(4 * D, D)
    heads = jnp.sum(gsum[4:6].reshape(2, -1, DH), axis=1)
    vecs = [reduce(v) for v in (gsum[0], gsum[1], gsum[2], gsum[3], heads[0], heads[1])]
    start = jnp.sum(jnp.where(jnp.arange(4)[None] < jnp.argmax(lengths, axis=1)[:, None], lengths, 0), axis=1)

    def back(half):
        rows = lax.all_gather(half, "sp", axis=0, tiled=True).reshape(2, 2 * T, D)
        rows = jnp.stack([jnp.roll(rows[r], start[r], axis=0) for r in range(2)])
        size = 2 * T // 4
        return lax.dynamic_slice_in_dim(rows, sp * size, size, axis=1).astype(f32)

    return (back(osel), back(dtok), vecs[0], vecs[1], reduce(natural(G[9:12])), vecs[4], vecs[5],
            reduce(natural(G[8:9])), vecs[2], vecs[3], reduce(natural(G[4:8])), reduce(g_down))


def finish_kernel(names, *refs):
    m = SimpleNamespace(**dict(zip(names, refs)))
    n, D = m.fin.shape[1], m.fin.shape[2]
    loads = [pltpu.make_async_copy(m.fin.at[b], m.inb.at[b], m.lsem.at[b]) for b in range(12)]
    rows = [(m.outq, m.out, 0), (m.dtokq, m.dtok, 1)]
    row_loads = [pltpu.make_async_copy(src, m.inr.at[i], m.lsem.at[12 + i]) for src, _, i in rows]
    for cp in row_loads[:1] + loads[:4] + loads[4:] + row_loads[1:]:
        cp.start()
    stores = []

    def store(src, dst):
        cp = pltpu.make_async_copy(src, dst, m.ssem.at[len(stores)])
        cp.start()
        stores.append(cp)

    def row(i):
        row_loads[i].wait()
        m.outr[i] = m.inr[i].astype(f32)
        store(m.outr.at[i], rows[i][1])

    row(0)
    for b in range(4):
        loads[b].wait()
        m.comb[b * n : (b + 1) * n, :] = m.inb[b].astype(f32)
    for h in range(2):

        @pl.loop(h * D // 256, (h + 1) * D // 256)
        def _(i):
            m.turned[at(i, 128), :] = m.comb[:, at(i, 128)].T

        half = pl.ds(h * (D // 2), D // 2)
        store(m.turned.at[half], m.g_down.at[half])
    for b in range(4, 12):
        loads[b].wait()
        m.outb[b - 4] = m.inb[b].astype(f32)
        dst, col = (m.g_up, (b - 4) * D) if b < 8 else (m.g_proj, 0) if b == 8 else (m.g_qkv, (b - 9) * D)
        store(m.outb.at[b - 4], dst.at[:, pl.ds(col, D)])
    row(1)
    z = lax.axis_index("fsdp")
    v = m.vec[...]
    wide = pltpu.roll(v, lax.rem(D - n * z, D), 1)
    for i, ref in enumerate((m.v0, m.v1, m.v2, m.v3)):
        ref[...] = wide[i, :n]
    h = v[:, :128]
    for i in range(1, D // 128):
        h += v[:, 128 * i : 128 * (i + 1)]
    h = h + pltpu.roll(h, DH, 1)
    h = pltpu.roll(h, lax.rem(128 - DH // 4 * z, 128), 1)
    for i, ref in enumerate((m.v4, m.v5)):
        ref[...] = h[4 + i, : DH // 4]
    for cp in stores:
        cp.wait()


def finish(fin, outq, dtokq, vec):
    n, D = fin.shape[1:]
    any_, vmem = pl.BlockSpec(memory_space=pl.ANY), pl.BlockSpec(memory_space=pltpu.VMEM)
    outs = dict(out=outq.shape, dtok=outq.shape, g_qkv=(n, 3 * D), g_proj=(n, D), g_up=(n, 4 * D), g_down=(D, D))
    vecs = {"v%d" % i: (n if i < 4 else DH // 4,) for i in range(6)}
    scratch = dict(
        inb=(fin.shape, bf), inr=((2,) + outq.shape, bf), outr=((2,) + outq.shape, f32), comb=((D, D), f32),
        turned=((D, D), f32), outb=((8, n, D), f32),
    )
    names = ["fin", "outq", "dtokq", "vec"] + list(outs) + list(vecs) + list(scratch) + ["lsem", "ssem"]
    out, dtok, qkv, proj, up, down, *v = pl.pallas_call(
        functools.partial(finish_kernel, names),
        out_shape=[jax.ShapeDtypeStruct(s, f32) for s in list(outs.values()) + list(vecs.values())],
        in_specs=[any_] * 3 + [vmem],
        out_specs=[any_] * 6 + [vmem] * 6,
        scratch_shapes=[pltpu.VMEM(s, d) for s, d in scratch.values()] + [pltpu.SemaphoreType.DMA((14,))] * 2,
        compiler_params=pltpu.CompilerParams(vmem_limit_bytes=VMEM_LIMIT),
        name="finish",
    )(fin, outq, dtokq, vec)
    return out, dtok, v[0], v[1], qkv, v[4], v[5], proj, v[2], v[3], up, down


def per_device(tokens, lengths, cotangent, pre_gain, pre_shift, w_qkv, query_gain, key_gain, w_proj, mid_gain,
               mid_shift, w_up, w_down):
    vectors = (pre_gain, pre_shift, mid_gain, mid_shift, query_gain, key_gain)
    if tuple(lax.axis_size(a) for a in ("rep", "fsdp", "sp")) != (2, 4, 4):
        return general_layer(tokens, lengths, cotangent, vectors, w_qkv, w_proj, w_up, w_down)
    return finish(*fused_layer(tokens, lengths, cotangent, vectors, w_qkv, w_proj, w_up, w_down))


def solution(mesh):
    rows, vec, mat = P(("rep", "fsdp"), "sp", None), P("fsdp"), P("fsdp", None)
    return jax.shard_map(
        per_device,
        mesh=mesh,
        in_specs=(rows, P(("rep", "fsdp"), None), rows, vec, vec, mat, vec, vec, mat, vec, vec, mat, mat),
        out_specs=(rows, rows, vec, vec, mat, vec, vec, mat, vec, vec, mat, mat),
        check_vma=False,
    )
```

```python
import functools
import math
from types import SimpleNamespace

import jax
import jax.numpy as jnp
from jax import lax
from jax.experimental import pallas as pl
from jax.experimental.pallas import tpu as pltpu
from jax.sharding import PartitionSpec as P

H = 12
DH = 64
EPSILON = 1e-06
MASKED = 1e30
MESH = pl.DeviceIdType.MESH
VMEM_LIMIT = 67043328
bf = jnp.bfloat16
f32 = jnp.float32


def nn(a, b):
    return lax.dot_general(a, b, (((1,), (0,)), ((), ())), preferred_element_type=f32)


def nt(a, b):
    return lax.dot_general(a, b, (((1,), (1,)), ((), ())), preferred_element_type=f32)


def at(i, size, base=0):
    if isinstance(i, int) and isinstance(base, int):
        return pl.ds(base + i * size, size)
    return pl.ds(pl.multiple_of(base + i * size, math.gcd(size, base) if isinstance(base, int) else size), size)


def same_head(n):
    a = lax.broadcasted_iota(jnp.int32, (n, n), 0) // DH
    b = lax.broadcasted_iota(jnp.int32, (n, n), 1) // DH
    return (a == b).astype(f32).astype(bf)


def split2(x):
    hi = x.astype(bf)
    return hi, (x - hi.astype(f32)).astype(bf)


def standardize(x):
    mean = jnp.mean(x, axis=-1, keepdims=True)
    c = x - mean
    r = lax.rsqrt(jnp.mean(c * c, axis=-1, keepdims=True) + EPSILON)
    return c * r, r


def transpose_to(src, dst):
    @pl.loop(0, dst.shape[0] // 128)
    def _(i):
        dst[at(i, 128), :] = src[:, at(i, 128)].astype(f32).T.astype(bf)


def wcols(m, b, s):
    w = m.W[b, :, :, s]
    return w.reshape(w.shape[0] * w.shape[1], w.shape[2])


def wrows(m, b, i):
    w = m.W[b, pl.ds(2 * i, 2), :, :]
    return w.reshape(2 * w.shape[1], w.shape[2])


def select_rows(m, rowbuf, dst):
    T, D = dst.shape

    @pl.loop(0, D // 256)
    def _(i):
        s = at(i, 256)
        dst[:, s] = (nn(m.ebuf[10], rowbuf[0, :, s]) + nn(m.ebuf[11], rowbuf[1, :, s])).astype(bf)


def select_cot(m):
    T, D = m.cot.shape

    @pl.loop(0, D // 256)
    def _(i):
        s = at(i, 256)
        m.cot[:, s] = (nn(m.rowx[0, :, 0:T], m.rowc[0, :, s]) + nn(m.rowx[1, :, 0:T], m.rowc[1, :, s])).astype(bf)


def source_rows(m, n):
    T = m.xs.shape[0]
    row = lax.broadcasted_iota(jnp.int32, (T, n), 0) + m.start + T * m.core
    return jnp.where(row >= 2 * T, row - 2 * T, row), lax.broadcasted_iota(jnp.int32, (T, n), 1)


def place_stage(m):
    T = m.xs.shape[0]
    row, col = source_rows(m, T)
    m.ebuf[10] = (row == col).astype(f32).astype(bf)
    m.ebuf[11] = (row == col + T).astype(f32).astype(bf)


def mask_stage(m):
    t, lane = source_rows(m, 128)
    pic = sum((t >= e).astype(jnp.int32) for e in m.ends)
    hot = (lane == pic).astype(f32)
    m.maskq[...] = (hot * MASKED).astype(bf)
    m.maskk[...] = jnp.where(lane < 4, hot - 1.0, 0.0).astype(bf)


def restore_quarter(m, cat, quarter):
    T = m.xs.shape[0]
    n = T // 2
    i = lax.broadcasted_iota(jnp.int32, (n, T), 0) + quarter * n - m.start
    i = jnp.where(i < 0, i + 2 * T, i)
    col = lax.broadcasted_iota(jnp.int32, (n, T), 1)
    a = (i == col).astype(f32).astype(bf)
    b = (i == col + T).astype(f32).astype(bf)
    return (nn(a, cat[0]) + nn(b, cat[1])).astype(bf)


def gains_stage(m):
    D = m.gains.shape[1]
    n = D // 4
    k = DH // 4
    lane = lax.broadcasted_iota(jnp.int32, (256, D), 0)
    col = lax.broadcasted_iota(jnp.int32, (256, D), 1)
    wide = jnp.zeros((8, D), f32)
    head = jnp.zeros((8, D), f32)
    for u in range(4):
        g = m.gbuf[u].astype(bf)
        wide += nn(g, ((col == lane + n * u) & (lane < n)).astype(f32).astype(bf))
        head += nn(g, ((col % DH == lane + k * u) & (lane < k)).astype(f32).astype(bf))
    r = lax.broadcasted_iota(jnp.int32, (8, D), 0)
    m.gains[...] = jnp.where(r < 4, wide, head)


def norm_stage(src, gain, shift, dst):
    @pl.loop(0, src.shape[0] // 64)
    def _(i):
        s = at(i, 64)
        xh, _ = standardize(src[s, :].astype(f32))
        dst[s, :] = (xh * gain + shift).astype(bf)


def qkv_stage(m, j):
    off = at(j, 256)
    m.v[:, off] = nn(m.mid[...], wcols(m, j, pl.ds(512, 256))).astype(bf)
    B = same_head(256)
    for kind in range(2):
        s = at(kind, 256, 512 * j)
        acc = nn(m.mid[...], wcols(m, j, pl.ds(256 * kind, 256)))
        hi, lo = split2(acc)
        c = acc - (nn(hi, B) + nn(lo, B)) * (1.0 / DH)
        r = lax.rsqrt(nn((c * c).astype(bf), B) * (1.0 / DH) + EPSILON)
        xh = c * r
        m.qkh[:, s] = xh.astype(bf)
        m.qkr[:, s] = r.astype(bf)
        val = (xh * m.gains[4 + kind : 5 + kind, off]).astype(bf)
        if kind == 0:
            m.q[:, off] = (val.astype(f32) * (1.0 / math.sqrt(DH))).astype(bf)
        else:
            m.k[:, off] = val


def lane_half(T, e):
    lane = lax.broadcasted_iota(jnp.int32, (T, 128), 1)
    return (lane < DH) if e == 0 else (lane >= DH)


def attend_pair(m, hp):
    T = m.q.shape[0]
    s = at(hp, 128)
    q2, k2, v2 = m.q[:, s].astype(f32), m.k[:, s], m.v[:, s]
    kx = jnp.concatenate([k2, m.maskk[...]], axis=1)
    outs = []
    for e in (0, 1):
        qe = jnp.where(lane_half(T, e), q2, 0.0).astype(bf)
        E = jnp.exp(nt(jnp.concatenate([qe, m.maskq[...]], axis=1), kx))
        p = (E * (1.0 / jnp.sum(E, axis=-1, keepdims=True))).astype(bf)
        m.ebuf[2 * hp + e] = p
        outs.append(nn(p, v2))
    m.att[:, s] = jnp.where(lane_half(T, 0), outs[0], outs[1]).astype(bf)


def proj_stage(m):
    @pl.loop(0, m.xs.shape[1] // 256)
    def _(i):
        s = at(i, 256)
        m.resid[:, s] = m.xs[:, s].astype(f32) + nn(m.att[...], wcols(m, 3, s))


def gelu_both(x):
    z = jnp.abs(x) * (1.0 / math.sqrt(2.0))
    t = 1.0 / (1.0 + 0.3275911 * z)
    p = ((((1.061405429 * t - 1.453152027) * t + 1.421413741) * t - 0.284496736) * t + 0.254829592) * t
    ex = jnp.exp(-0.5 * x * x)
    tail = 0.5 * p * ex
    phi = jnp.where(x < 0, tail, 1.0 - tail)
    return x * phi, phi + x * ex * (1.0 / math.sqrt(2.0 * math.pi))


def up_stage(m, j):
    D = m.xs.shape[1]

    @pl.loop(0, D // 256)
    def _(i):
        a, d = gelu_both(nn(m.mid[...], wcols(m, 4 + j, at(i, 256))))
        s = at(i, 256, j * D)
        m.act[:, s] = a.astype(bf)
        m.gp[:, s] = d.astype(bf)


def out_stage(m, i):
    D = m.xs.shape[1]
    s = at(i, 256)
    acc = m.resid[:, s]
    for u in range(4):
        w = m.W[8:12, u, :, s]
        acc += nn(m.act[:, u * D : (u + 1) * D], w.reshape(D, 256))
    m.osel[:, s] = acc.astype(bf)


def dinner_stage(m, u):
    D = m.xs.shape[1]
    for i in range(2):
        w = m.W[8 + 2 * i : 10 + 2 * i, u, :, :]
        s = at(i, D // 2, u * D)
        d = nt(m.cot[...], w.reshape(D // 2, D))
        m.gp[:, s] = (d * m.gp[:, s].astype(f32)).astype(bf)


def dmid_stage(m, i):
    D = m.xs.shape[1]
    acc = nt(m.gp[:, 0:D], wrows(m, 4, i))
    for j in range(1, 4):
        acc += nt(m.gp[:, j * D : (j + 1) * D], wrows(m, 4 + j, i))
    m.dres[:, at(i, D // 2)] = acc


def dresid_stage(m):
    T, D = m.dres.shape
    g = m.gains[2:3, :]

    @pl.loop(0, T // 64)
    def _(i):
        s = at(i, 64)
        dm = m.dres[s, :]
        xh, r = standardize(m.resid[s, :])
        dx = dm * g
        m1 = jnp.mean(dx, axis=-1, keepdims=True)
        m2 = jnp.mean(dx * xh, axis=-1, keepdims=True)
        dr = m.cot[s, :].astype(f32) + r * (dx - m1 - xh * m2)
        m.dres[s, :] = dr
        m.dattn[s, :] = dr.astype(bf)
        m.gsum[2:3, :] += jnp.sum(dm * xh, axis=0, keepdims=True)
        m.gsum[3:4, :] += jnp.sum(dm, axis=0, keepdims=True)


def datt_stage(m):
    n = m.xs.shape[1] // 2

    @pl.loop(0, 2)
    def _(i):
        m.datt[:, at(i, n)] = nt(m.dattn[...], wrows(m, 3, i)).astype(bf)


def attend_back_pair(m, j, i):
    T, D = m.q.shape
    hp = 2 * j + i
    s = at(hp, 128)
    do = m.datt[:, s].astype(f32)
    B = same_head(128)
    hi, lo = split2(do * m.att[:, s].astype(f32))
    dl = nn(hi, B) + nn(lo, B)
    k2, v2 = m.k[:, s], m.v[:, s]
    lane = lax.broadcasted_iota(jnp.int32, (T, 128), 1)
    vx = jnp.concatenate([v2, (lane < 2).astype(f32).astype(bf)], axis=1)
    doT = do.T.astype(bf)
    qT = m.q[:, s].astype(f32).T.astype(bf)
    dqs, dks, dvs = [], [], []
    for e in (0, 1):
        de = jnp.where(lane_half(T, e), do, 0.0).astype(bf)
        dle = dl[:, e * DH : e * DH + 1]
        dh = dle.astype(bf).astype(f32)
        dmask = jnp.where(lane == 0, -dh, jnp.where(lane == 1, dh - dle, 0.0)).astype(bf)
        t = nt(jnp.concatenate([de, dmask], axis=1), vx)
        E = m.ebuf[2 * hp + e]
        ds = (E.astype(f32) * t).astype(bf)
        dqs.append(nn(ds, k2))
        dks.append(nn(qT[e * DH : (e + 1) * DH, :], ds))
        dvs.append(nn(doT[e * DH : (e + 1) * DH, :], E))
    dq = jnp.where(lane_half(T, 0), dqs[0], dqs[1]) * (1.0 / math.sqrt(DH))
    dk = jnp.concatenate(dks, axis=0).T
    dv = jnp.concatenate(dvs, axis=0).T
    m.dqkv[:, at(i, 128, D * j + 512)] = dv.astype(bf)
    for kind, d in ((0, dq), (1, dk)):
        d = d.astype(bf).astype(f32)
        w = at(i, 128, 512 * j + 256 * kind)
        xh = m.qkh[:, w].astype(f32)
        r = m.qkr[:, w].astype(f32)
        m.gsum[4 + kind : 5 + kind, s] = jnp.sum(d * xh, axis=0, keepdims=True)
        dx = d * m.gains[4 + kind : 5 + kind, s]
        h1, l1 = split2(dx)
        m1 = (nn(h1, B) + nn(l1, B)) * (1.0 / DH)
        h2, l2 = split2(dx * xh)
        m2 = (nn(h2, B) + nn(l2, B)) * (1.0 / DH)
        m.dqkv[:, at(i, 128, D * j + 256 * kind)] = (r * (dx - m1 - xh * m2)).astype(bf)


def dnormed_stage(m, i):
    D = m.xs.shape[1]
    acc = nt(m.dqkv[:, 0:D], wrows(m, 0, i))
    for j in range(1, 3):
        acc += nt(m.dqkv[:, j * D : (j + 1) * D], wrows(m, j, i))
    m.resid[:, at(i, D // 2)] = acc


def dtokens_stage(m):
    T, D = m.dres.shape
    g = m.gains[0:1, :]

    @pl.loop(0, T // 64)
    def _(i):
        s = at(i, 64)
        dn = m.resid[s, :]
        xh, r = standardize(m.xs[s, :].astype(f32))
        dx = dn * g
        m1 = jnp.mean(dx, axis=-1, keepdims=True)
        m2 = jnp.mean(dx * xh, axis=-1, keepdims=True)
        m.dtok[s, :] = (m.dres[s, :] + r * (dx - m1 - xh * m2)).astype(bf)
        m.gsum[0:1, :] += jnp.sum(dn * xh, axis=0, keepdims=True)
        m.gsum[1:2, :] += jnp.sum(dn, axis=0, keepdims=True)


def grad_down(m, j):
    D = m.xs.shape[1]
    n = D // 4

    @pl.loop(0, 4)
    def _(u):
        m.G[j, u] = nn(m.cotT[j * n : (j + 1) * n, :], m.act[:, at(u, D)]).astype(bf)


def grad_block(m, b, lhsT, rhs, base):
    D = m.xs.shape[1]
    n = D // 4

    @pl.loop(0, D // 256)
    def _(i):
        r = nn(lhsT[...], rhs[:, at(i, 256, base)]).astype(bf)
        for u in range(4):
            m.G[b, u, :, at(i, 256)] = r[u * n : (u + 1) * n]


GATHER = ("y", "xy", "xy", "xy", "xy", "xy", "x", "y", "xy", "xy", "y", "x")
REDUCE = ("xy", "xy", "xy", "xy", "xy", "xy", "xy", "xy", "xy", "x", "xy", "x")
SLOTS = (2, 4, 4, 4, 4, 12, 12)
ORDER = (
    "rp0", "g1_0", "place", "rw0", "rs1", "g1_1", "g2_0", "g1_2", "selx", "g1_3", "rp1", "g3_0", "gains", "g2_1",
    "g4_0", "norm1", "g2_2", "g2_3", "g1_4", "g3_1", "qkv0", "att0", "g2_4", "g3_2", "g1_5", "g1_6", "g4_1", "qkv1",
    "g1_7", "rw1", "g4_2", "qkv2", "g2_5", "att1", "selc", "g2_6", "g3_3", "g2_7", "g3_4", "g1_8", "g1_9", "g1_10",
    "g1_11", "g4_3", "g3_5", "att2", "proj", "g3_6", "norm2", "midT", "g4_4", "g2_8", "g3_7", "g4_5", "g4_6", "up2",
    "g2_9", "up0", "g2_10", "g2_11", "cotT", "g4_7", "up1", "up3", "gd0", "r0_0", "g3_8", "gd1", "r0_1", "r1_0", "g3_9",
    "gd3", "g3_10", "g3_11", "g4_8", "g4_9", "r1_1", "gd2", "g4_10", "r0_2", "g4_11", "din2", "r2_0", "r1_2", "r0_3",
    "din0", "gu0", "r2_1", "out2", "out1", "r1_3", "r3_0", "r0_4", "r2_2", "din1", "din3", "r1_4", "dmid1", "r3_1",
    "r2_3", "gu1", "gu2", "r0_5", "r4_0", "dmid0", "r3_2", "r1_5", "out0", "r0_6", "r2_4", "dres", "r4_1", "attT",
    "r3_3", "cat0", "r1_6", "gu3", "r2_5", "r0_7", "r5_0", "datt", "gpj", "r1_7", "r4_2", "r0_8", "r3_4", "nT", "r2_6",
    "r5_1", "r1_8", "bk0", "gq0", "r6_0", "r0_9", "r4_3", "r5_2", "r3_5", "r2_7", "r4_4", "res0", "r1_9", "bk1", "r3_6",
    "r5_3", "r4_5", "gq1", "r2_8", "r5_4", "r0_10", "bk2", "gq2", "r4_6", "r1_10", "r3_7", "r0_11", "r2_9", "dn0",
    "dn1", "r3_8", "resw0", "r5_5", "r6_1", "r6_2", "r1_11", "dtok", "cat1", "r4_7", "r2_10", "r5_6", "res1", "r3_9",
    "v0", "v1", "r6_3", "r6_4", "r7_0", "r7_1", "r2_11", "r3_10", "r7_2", "v2", "r6_5", "r4_8", "r5_7", "r4_9", "r6_6",
    "r3_11", "v3", "r7_3", "r4_10", "r7_4", "r7_5", "r5_8", "r5_9", "r4_11", "v4", "r7_6", "r6_7", "r6_8", "r5_10",
    "r5_11", "v5", "r7_7", "r6_9", "r7_8", "r6_10", "r6_11", "r7_9", "r7_10", "r7_11",
)


class Comm:
    def __init__(self, m):
        self.m = m
        self.x, self.z, sp = lax.axis_index("rep"), lax.axis_index("fsdp"), lax.axis_index("sp")
        self.y, self.c = sp // 2, sp % 2
        x, y, z, c = self.x, self.y, self.z, self.c
        nx, ny = (1 - x, z, sp), (x, z, 2 * (1 - y) + c)
        self.nx, self.ny = nx, ny
        n1 = (x + (1 - c) * (1 - 2 * x), z, 2 * (y + c * (1 - 2 * y)) + c)
        n2 = (x + c * (1 - 2 * x), z, 2 * (y + (1 - c) * (1 - 2 * y)) + c)
        self.orders = {"x": (x, y, nx, ny), "y": (y, x, ny, nx), "xy": (x + c * (y - x), y + c * (x - y), n1, n2)}
        self.core = (x, z, 2 * y + 1 - c)
        self.zat = lambda u: (x, u, sp)
        self.z1 = z + 1 - 2 * (z % 2)
        self.zt = 3 - z
        self.mine = at(c, 384)
        self.other = at(1 - c, 384)

    def gather_order(self, b):
        return self.orders[GATHER[b]]

    def reduce_order(self, b):
        return self.orders[REDUCE[b]]

    def barrier(self):
        sem = pltpu.get_barrier_semaphore()
        peers = [self.nx, self.ny, self.core] + [self.zat((self.z + d) % 4) for d in (1, 2, 3)]
        for p in peers:
            pl.semaphore_signal(sem, inc=1, device_id=p, device_id_type=MESH)
        pl.semaphore_wait(sem, len(peers))

    def copy(self, src, dst, send, recv, dev):
        return pltpu.make_async_remote_copy(
            src_ref=src, dst_ref=dst, send_sem=send, recv_sem=recv, device_id=dev, device_id_type=MESH
        )

    def row_copies(self, arg, buf, k):
        s, r = self.m.rsem.at[0, k], self.m.rsem.at[1, k]
        mine = buf.at[self.y, at(self.c, 256)]
        there = buf.at[1 - self.y, at(self.c, 256)]
        local = pltpu.make_async_copy(arg.at[self.y], mine, s.at[0])
        near = self.copy(arg.at[self.y], mine, s.at[1], r.at[1], self.core)
        far = self.copy(arg.at[1 - self.y], mine, s.at[2], r.at[2], self.ny)
        pass_on = self.copy(there, there, s.at[3], r.at[3], self.core)
        return local, near, far, pass_on

    def row_start(self, arg, buf, k):
        local, near, far, _ = self.row_copies(arg, buf, k)
        far.start()
        near.start()
        local.start()

    def row_pass(self, arg, buf, k):
        _, _, far, pass_on = self.row_copies(arg, buf, k)
        far.wait_recv()
        pass_on.start()

    def row_wait(self, arg, buf, k):
        local, near, far, pass_on = self.row_copies(arg, buf, k)
        local.wait()
        near.wait()
        far.wait_send()
        pass_on.wait()

    def gain_copies(self):
        m = self.m
        out = [pltpu.make_async_copy(m.gpack, m.gbuf.at[self.z], m.gsem.at[0, 0])]
        for d in (1, 2, 3):
            dev = self.zat((self.z + d) % 4)
            out.append(self.copy(m.gpack, m.gbuf.at[self.z], m.gsem.at[0, d], m.gsem.at[1, d], dev))
        return out

    def shard(self, b, rows, cols):
        m = self.m
        arg, r0, c0 = (m.a_qkv, 0, 0) if b < 3 else (m.a_proj, 0, 0) if b == 3 else (
            (m.a_up, 0, 768 * (b - 4)) if b < 8 else (m.a_down, 192 * (b - 8), 0))
        return arg.at[pl.ds(pl.multiple_of(r0 + rows[0], 16), rows[1]), pl.ds(pl.multiple_of(c0 + cols[0], 128), cols[1])]

    def spans(self, b):
        c = self.c
        if b < 3:
            return [(256 * b + 1536 * c, 512 * c, 256), (768 + 256 * b + 128 * c, 256 + 128 * c, 128)]
        return [(384 * c, 384 * c, 384)]

    def own_copies(self, b):
        sem, dst = self.m.wsem.at[0, 0, b], self.m.W.at[b, self.z]
        if b < 3:
            return [
                pltpu.make_async_copy(self.shard(b, (0, 192), (768 * i + 256 * b, 256)), dst.at[:, pl.ds(256 * i, 256)], sem)
                for i in range(3)
            ]
        return [pltpu.make_async_copy(self.shard(b, (0, 192), (0, 768)), dst, sem)]

    def own_start(self, b):
        for cp in self.own_copies(b):
            cp.start()

    def own_wait(self, b):
        m = self.m
        pltpu.make_async_copy(m.W.at[b, self.z], m.W.at[b, self.z], m.wsem.at[0, 0, b]).wait()

    def z_start(self, b):
        m = self.m
        f1, f2, _, _ = self.gather_order(b)
        q = 2 * f2 + f1
        for d in (1, 2, 3):
            for src, to, n in self.spans(b):
                dst = m.W.at[b, self.z, at(q, 48), pl.ds(pl.multiple_of(to, 128), n)]
                sems = m.wsem.at[0, 1, b], m.wsem.at[1, 1, b]
                self.copy(self.shard(b, (48 * q, 48), (src, n)), dst, *sems, self.zat((self.z + d) % 4)).start()

    def plane(self, k, b):
        m = self.m
        f1, f2, n1, n2 = self.gather_order(b)
        rows, dev = {2: (at(2 * f2 + f1, 48), n1), 3: (at(f2, 96), n2), 4: (pl.ds(0, 192), self.core)}[k]
        out = []
        for d in (1, 2, 3):
            ref = m.W.at[b, (self.z + d) % 4, rows, self.mine]
            out.append(self.copy(ref, ref, m.wsem.at[0, k, b], m.wsem.at[1, k, b], dev))
        return out

    def w_all(self, k, b):
        m = self.m
        f1, f2, n1, n2 = self.gather_order(b)
        part = at(2 * f2 + f1, 48)
        rows, dev = {1: (part, self.core), 2: (part, n1), 3: (at(f2, 96), n2), 4: (pl.ds(0, 192), self.core)}[k]
        ref = m.W.at[b, 0:3, rows, self.mine]
        return self.copy(ref, ref, m.wsem.at[0, k, b], m.wsem.at[1, k, b], dev)

    def ag_step(self, k, b):
        self.w_all(k, b).wait_recv()
        if k < 4:
            for cp in self.plane(k + 1, b):
                cp.start()
        else:
            for j in (1, 2, 3, 4):
                self.w_all(j, b).wait_send()
            self.own_wait(b)

    def rs_copies(self, k, b):
        m = self.m
        G, z = m.G, self.z
        f1, f2, n1, n2 = self.reduce_order(b)
        slot = b % SLOTS[k]
        rows = at(f1, 96)
        sem = lambda j: (m.psem.at[0, j, slot], m.psem.at[1, j, slot])
        if k == 0:
            return [self.copy(G.at[b, :, :, self.other], m.rA.at[slot], *sem(0), self.core)]
        if k == 1:
            return [self.copy(G.at[b, :, at(1 - f1, 96), self.mine], m.rB.at[slot], *sem(1), n1)]
        if k == 2:
            return [
                self.copy(G.at[b, self.z1, rows, self.mine], m.rC.at[slot, 0], *sem(2), self.zat(self.z1)),
                self.copy(G.at[b, 3 - self.z1, rows, self.mine], m.rC.at[slot, 1], *sem(7), self.zat(self.z1)),
            ]
        if k == 3:
            return [self.copy(G.at[b, self.zt, rows, self.mine], m.rD.at[slot], *sem(3), self.zat(self.zt))]
        if k == 4:
            return [self.copy(G.at[b, z, rows, self.mine], m.rE.at[slot], *sem(4), n2)]
        if k == 5:
            ref = G.at[b, z, rows, self.mine]
            return [self.copy(ref, ref, *sem(5), n1)]
        ref = G.at[b, z, :, self.mine]
        return [self.copy(ref, ref, *sem(6), self.core)]

    def rs_step(self, k, b):
        m = self.m
        G, z = m.G, self.z
        rows = at(self.reduce_order(b)[0], 96)
        if k > 0:
            slot = b % SLOTS[k - 1]
            for cp in self.rs_copies(k - 1, b):
                cp.wait()
        if k == 1:

            @pl.loop(0, 4)
            def _(u):
                G[b, u, :, self.mine] = (G[b, u, :, self.mine].astype(f32) + m.rA[slot, u].astype(f32)).astype(bf)
        elif k == 2:

            @pl.loop(0, 4)
            def _(u):
                G[b, u, rows, self.mine] = (G[b, u, rows, self.mine].astype(f32) + m.rB[slot, u].astype(f32)).astype(bf)
        elif k == 3:
            for i, u in ((0, z), (1, self.zt)):
                G[b, u, rows, self.mine] = (G[b, u, rows, self.mine].astype(f32) + m.rC[slot, i].astype(f32)).astype(bf)
        elif k in (4, 5):
            r = (m.rD if k == 4 else m.rE)[slot]
            G[b, z, rows, self.mine] = (G[b, z, rows, self.mine].astype(f32) + r.astype(f32)).astype(bf)
        if k < 7:
            for cp in self.rs_copies(k, b):
                cp.start()
        else:
            self.fin_copy(b).start()

    def fin_copy(self, b):
        return pltpu.make_async_copy(self.m.G.at[b, self.z], self.m.fin.at[b], self.m.fsem.at[b])

    def vec_copy(self, i):
        m = self.m
        dev = [self.core, self.nx, self.ny, self.zat(self.z1), self.zat(self.zt)][i]
        return self.copy(m.gs.at[i], m.gr.at[i], m.vsem.at[0, i], m.vsem.at[1, i], dev)

    def vec_step(self, i):
        m = self.m
        if i == 0:
            m.gs[0] = m.gsum[...]
        else:
            self.vec_copy(i - 1).wait()
            m.gs[i] = m.gs[i - 1] + m.gr[i - 1]
        if i < 5:
            self.vec_copy(i).start()
        else:
            m.vec[...] = m.gs[5]

    def cat_copy(self, cat, k):
        half = cat.at[self.c]
        return self.copy(half, half, self.m.osem.at[0, k, 0], self.m.osem.at[1, k, 0], self.core)

    def quart(self, i):
        T, D = self.m.xs.shape
        return self.m.act.at[pl.ds(i * (T // 2), T // 2), pl.ds(3 * D, D)]

    def quarter_copies(self, dst, k):
        m = self.m
        far = self.copy(self.quart(1), dst.at[self.y], m.osem.at[0, k, 1], m.osem.at[1, k, 1], self.ny)
        near = pltpu.make_async_copy(self.quart(0), dst.at[self.y], m.osem.at[0, k, 2])
        return far, near

    def result_send(self, cat, dst, k):
        m = self.m
        self.cat_copy(cat, k).wait()
        self.quart(1)[...] = restore_quarter(m, cat, 2 * (1 - self.y) + self.c)
        far, near = self.quarter_copies(dst, k)
        far.start()
        self.quart(0)[...] = restore_quarter(m, cat, 2 * self.y + self.c)
        near.start()

    def result_wait(self, dst, k):
        far, near = self.quarter_copies(dst, k)
        far.wait()
        near.wait()


SCRATCH = lambda T, D, FF: dict(
    gains=((8, D), f32), maskq=((T, 128), bf), maskk=((T, 128), bf), xs=((T, D), bf), cot=((T, D), bf),
    mid=((T, D), bf), midT=((D, T), bf), cotT=((D, T), bf),
    q=((T, D), bf), k=((T, D), bf), v=((T, D), bf), qkh=((T, 2 * D), bf), qkr=((T, 2 * D), bf),
    ebuf=((H, T, T), bf), att=((T, D), bf), resid=((T, D), f32),
    act=((T, FF), bf), gp=((T, FF), bf), dres=((T, D), f32), datt=((T, D), bf), gsum=((8, D), f32),
)


def prepare(m, lengths, y):
    T = m.xs.shape[0]
    l = [lengths[y, k] for k in range(4)]
    m.ends = [l[0], l[0] + l[1], l[0] + l[1] + l[2]]
    m.start = jnp.where(l[0] == T, 0, jnp.where(l[1] == T, m.ends[0], jnp.where(l[2] == T, m.ends[1], m.ends[2])))
    m.dattn = m.mid
    m.dqkv = m.act
    m.attT = m.cotT


def two(f):
    @pl.loop(0, 2)
    def _(i):
        f(i)


def compute_pieces(m):
    D = m.xs.shape[1]
    pieces = {
        "place": lambda: place_stage(m),
        "norm1": lambda: norm_stage(m.xs, m.gains[0:1, :], m.gains[1:2, :], m.mid),
        "nT": lambda: (norm_stage(m.xs, m.gains[0:1, :], m.gains[1:2, :], m.mid), transpose_to(m.mid, m.midT)),
        "proj": lambda: proj_stage(m),
        "norm2": lambda: norm_stage(m.resid, m.gains[2:3, :], m.gains[3:4, :], m.mid),
        "midT": lambda: transpose_to(m.mid, m.midT),
        "cotT": lambda: transpose_to(m.cot, m.cotT),
        "dres": lambda: dresid_stage(m),
        "attT": lambda: transpose_to(m.att, m.attT),
        "gpj": lambda: grad_block(m, 8, m.attT, m.dattn, 0),
        "datt": lambda: datt_stage(m),
        "dtok": lambda: dtokens_stage(m),
    }

    def several(name, n, f):
        for i in range(n):
            pieces["%s%d" % (name, i)] = functools.partial(f, i)

    several("qkv", 3, lambda i: qkv_stage(m, i))
    several("att", 3, lambda j: two(lambda i: attend_pair(m, 2 * j + i)))
    several("up", 4, lambda i: up_stage(m, i))
    several("gd", 4, lambda i: grad_down(m, i))
    several("out", 3, lambda i: out_stage(m, i))
    several("din", 4, lambda i: dinner_stage(m, i))
    several("dmid", 2, lambda i: dmid_stage(m, i))
    several("gu", 4, lambda i: grad_block(m, 4 + i, m.midT, m.gp, i * D))
    several("bk", 3, lambda j: two(lambda i: attend_back_pair(m, j, i)))
    several("gq", 3, lambda i: grad_block(m, 9 + i, m.midT, m.dqkv, i * D))
    several("dn", 2, lambda i: dnormed_stage(m, i))
    return pieces


def layer_kernel(comm_names, *refs):
    m = SimpleNamespace(**dict(zip(comm_names, refs)))
    cm = Comm(m)
    m.osel, m.dtok = m.rowx.at[cm.c], m.rowc.at[cm.c]
    m.maskq, m.maskk = m.rowx.at[0, :, pl.ds(512, 128)], m.rowx.at[1, :, pl.ds(512, 128)]
    m.core = cm.c
    prepare(m, m.lengths, cm.y)
    m.gpack[...] = jnp.zeros_like(m.gpack)
    for i in range(6):
        g = getattr(m, "g%d" % i)
        m.gpack[i : i + 1, 0 : g.shape[0]] = g[...].astype(f32).reshape(1, g.shape[0])
    m.gsum[...] = jnp.zeros_like(m.gsum)
    cm.barrier()
    cm.row_start(m.tokens, m.rowx, 0)
    for g in cm.gain_copies():
        g.start()
    for b in range(12):
        cm.z_start(b)
        cm.own_start(b)

    def gains():
        for g in cm.gain_copies():
            g.wait()
        gains_stage(m)

    def selx():
        select_rows(m, m.rowx, m.xs)
        for h in range(2):
            m.rowx[h, :, 0 : m.ebuf.shape[1]] = m.ebuf[10 + h]
        mask_stage(m)

    rows = ((m.tokens, m.rowx, 0), (m.cotangent, m.rowc, 1))
    pieces = compute_pieces(m)
    pieces.update(
        gains=gains,
        selx=selx,
        selc=lambda: select_cot(m),
        rs1=lambda: cm.row_start(*rows[1]),
        cat0=lambda: cm.cat_copy(m.rowx, 0).start(),
        cat1=lambda: cm.cat_copy(m.rowc, 1).start(),
        res0=lambda: cm.result_send(m.rowx, m.outq, 0),
        res1=lambda: cm.result_send(m.rowc, m.dtokq, 1),
        resw0=lambda: cm.result_wait(m.outq, 0),
    )
    for k in range(2):
        pieces["rp%d" % k] = functools.partial(cm.row_pass, *rows[k])
        pieces["rw%d" % k] = functools.partial(cm.row_wait, *rows[k])
    for i in range(6):
        pieces["v%d" % i] = functools.partial(cm.vec_step, i)
    for b in range(12):
        for k in range(1, 5):
            pieces["g%d_%d" % (k, b)] = functools.partial(cm.ag_step, k, b)
        for k in range(8):
            pieces["r%d_%d" % (k, b)] = functools.partial(cm.rs_step, k, b)
    assert sorted(pieces) == sorted(ORDER)
    for name in ORDER:
        pieces[name]()
    for b in range(12):
        cm.fin_copy(b).wait()
    cm.result_wait(m.dtokq, 1)


def fused_layer(tokens, lengths, cotangent, vectors, w_qkv, w_proj, w_up, w_down):
    T, D, FF = tokens.shape[0] * tokens.shape[1], tokens.shape[2], w_up.shape[1]
    any_, vmem = pl.BlockSpec(memory_space=pl.ANY), pl.BlockSpec(memory_space=pltpu.VMEM)
    ins = ["tokens", "lengths", "cotangent", "a_qkv", "a_proj", "a_up", "a_down"] + ["g%d" % i for i in range(6)]
    outs = dict(
        fin=((12, D // 4, D), bf), outq=(tokens.shape, bf), dtokq=(tokens.shape, bf), vec=((8, D), f32)
    )
    scratch = SCRATCH(T, D, FF)
    del scratch["maskq"], scratch["maskk"]
    scratch.update(
        W=((12, 4, D // 4, D), bf), G=((12, 4, D // 4, D), bf), rowx=((2, T, D), bf), rowc=((2, T, D), bf),
        gbuf=((4, 8, 256), f32), gpack=((8, 256), f32),
        rA=((SLOTS[0], 4, 192, 384), bf), rB=((SLOTS[1], 4, 96, 384), bf), rC=((SLOTS[2], 2, 96, 384), bf),
        rD=((SLOTS[3], 96, 384), bf),
        rE=((SLOTS[4], 96, 384), bf), gs=((6, 8, D), f32), gr=((5, 8, D), f32),
    )
    sems = dict(
        rsem=(2, 2, 4), gsem=(2, 4), wsem=(2, 5, 12), psem=(2, 8, 12), fsem=(12,), vsem=(2, 5), osem=(2, 2, 3)
    )
    names = ins + list(outs) + list(scratch) + list(sems)
    return pl.pallas_call(
        functools.partial(layer_kernel, names),
        out_shape=[jax.ShapeDtypeStruct(s, d) for s, d in outs.values()],
        in_specs=[any_, pl.BlockSpec(memory_space=pltpu.SMEM), any_] + [any_] * 4 + [vmem] * 6,
        out_specs=[any_, any_, any_, vmem],
        scratch_shapes=[pltpu.VMEM(s, d) for s, d in scratch.values()]
        + [pltpu.SemaphoreType.DMA(s) for s in sems.values()],
        compiler_params=pltpu.CompilerParams(collective_id=0, has_side_effects=True, vmem_limit_bytes=VMEM_LIMIT),
        name="layer",
    )(tokens, lengths, cotangent, w_qkv, w_proj, w_up, w_down, *vectors)


def plain_kernel(names, *refs):
    m = SimpleNamespace(**dict(zip(names, refs)))
    sp = lax.axis_index("sp")
    m.core = sp % 2
    prepare(m, m.lengths, sp // 2)
    m.gsum[...] = jnp.zeros_like(m.gsum)
    pieces = compute_pieces(m)
    pieces["selx"] = lambda: (select_rows(m, m.rowx, m.xs), select_rows(m, m.rowc, m.cot), mask_stage(m))
    for name in ORDER:
        if name in pieces:
            pieces[name]()


def general_layer(tokens, lengths, cotangent, vectors, w_qkv, w_proj, w_up, w_down):
    T, D, FF = tokens.shape[0] * tokens.shape[1], tokens.shape[2], w_up.shape[1]
    n = D // 4
    gather = lambda v: lax.all_gather(v, "fsdp", axis=0, tiled=True)
    qkv, proj, up, down = (gather(w) for w in (w_qkv, w_proj, w_up, w_down))
    by_columns = lambda w: w.reshape(4, n, -1, D).transpose(2, 0, 1, 3)
    swap = lambda w: w.reshape(w.shape[0], 3, 3, -1).transpose(0, 2, 1, 3).reshape(w.shape)
    W = jnp.concatenate(
        [by_columns(swap(qkv)), by_columns(proj), by_columns(up), down.reshape(4, 4, n, D).transpose(1, 0, 2, 3)]
    )
    gains = [gather(v).astype(f32) for v in vectors]
    gains = [jnp.tile(g, D // g.shape[0]) for g in gains] + [jnp.zeros(D, f32)] * 2
    sp = lax.axis_index("sp")
    whole_row = lambda v: lax.dynamic_index_in_dim(lax.all_gather(v, "sp", axis=1, tiled=True), sp // 2, 0, False)
    rowx, rowc = (whole_row(v).reshape(2, T, D) for v in (tokens, cotangent))
    scratch = SCRATCH(T, D, FF)
    gsum = scratch.pop("gsum")
    del scratch["gains"]
    outs = dict(G=(W.shape, bf), osel=((T, D), bf), dtok=((T, D), bf), gsum=gsum)
    vmem = pl.BlockSpec(memory_space=pltpu.VMEM)
    names = ["lengths", "W", "rowx", "rowc", "gains"] + list(outs) + list(scratch)
    G, osel, dtok, gsum = pl.pallas_call(
        functools.partial(plain_kernel, names),
        out_shape=[jax.ShapeDtypeStruct(s, d) for s, d in outs.values()],
        in_specs=[pl.BlockSpec(memory_space=pltpu.SMEM)] + [vmem] * 4,
        out_specs=[vmem] * 4,
        scratch_shapes=[pltpu.VMEM(s, d) for s, d in scratch.values()],
        compiler_params=pltpu.CompilerParams(vmem_limit_bytes=VMEM_LIMIT),
        name="layer",
    )(lengths, W, rowx, rowc, jnp.stack(gains))

    def reduce(v):
        part = lax.psum_scatter(v.astype(bf), "fsdp", scatter_dimension=0, tiled=True)
        return lax.psum(part, ("rep", "sp")).astype(f32)

    natural = lambda g: g.reshape(-1, D, D).transpose(1, 0, 2).reshape(D, -1)
    g_down = G[0:4].transpose(1, 3, 0, 2).reshape(4 * D, D)
    heads = jnp.sum(gsum[4:6].reshape(2, -1, DH), axis=1)
    vecs = [reduce(v) for v in (gsum[0], gsum[1], gsum[2], gsum[3], heads[0], heads[1])]
    start = jnp.sum(jnp.where(jnp.arange(4)[None] < jnp.argmax(lengths, axis=1)[:, None], lengths, 0), axis=1)

    def back(half):
        rows = lax.all_gather(half, "sp", axis=0, tiled=True).reshape(2, 2 * T, D)
        rows = jnp.stack([jnp.roll(rows[r], start[r], axis=0) for r in range(2)])
        size = 2 * T // 4
        return lax.dynamic_slice_in_dim(rows, sp * size, size, axis=1).astype(f32)

    return (back(osel), back(dtok), vecs[0], vecs[1], reduce(swap(natural(G[9:12]))), vecs[4], vecs[5],
            reduce(natural(G[8:9])), vecs[2], vecs[3], reduce(natural(G[4:8])), reduce(g_down))


def finish_kernel(names, *refs):
    m = SimpleNamespace(**dict(zip(names, refs)))
    n, D = m.fin.shape[1], m.fin.shape[2]
    loads = [pltpu.make_async_copy(m.fin.at[b], m.inb.at[b], m.lsem.at[b]) for b in range(12)]
    rows = [(m.outq, m.out, 0), (m.dtokq, m.dtok, 1)]
    row_loads = [pltpu.make_async_copy(src, m.inr.at[i], m.lsem.at[12 + i]) for src, _, i in rows]
    for cp in row_loads[:1] + loads[:4] + loads[4:] + row_loads[1:]:
        cp.start()
    stores = []

    def store(src, dst):
        cp = pltpu.make_async_copy(src, dst, m.ssem.at[len(stores)])
        cp.start()
        stores.append(cp)

    def row(i):
        row_loads[i].wait()
        m.outr[i] = m.inr[i].astype(f32)
        store(m.outr.at[i], rows[i][1])

    row(0)
    for b in range(4):
        loads[b].wait()
        m.comb[b * n : (b + 1) * n, :] = m.inb[b].astype(f32)
    for h in range(2):

        @pl.loop(h * D // 256, (h + 1) * D // 256)
        def _(i):
            m.turned[at(i, 128), :] = m.comb[:, at(i, 128)].T

        half = pl.ds(h * (D // 2), D // 2)
        store(m.turned.at[half], m.g_down.at[half])
    for b in range(4, 12):
        loads[b].wait()
        m.outb[b - 4] = m.inb[b].astype(f32)
        if b < 9:
            dst, col = (m.g_up, (b - 4) * D) if b < 8 else (m.g_proj, 0)
            store(m.outb.at[b - 4], dst.at[:, pl.ds(col, D)])
        else:
            for i in range(3):
                store(m.outb.at[b - 4, :, pl.ds(256 * i, 256)], m.g_qkv.at[:, pl.ds(D * i + 256 * (b - 9), 256)])
    row(1)
    z = lax.axis_index("fsdp")
    v = m.vec[...]
    wide = pltpu.roll(v, lax.rem(D - n * z, D), 1)
    for i, ref in enumerate((m.v0, m.v1, m.v2, m.v3)):
        ref[...] = wide[i, :n]
    h = v[:, :128]
    for i in range(1, D // 128):
        h += v[:, 128 * i : 128 * (i + 1)]
    h = h + pltpu.roll(h, DH, 1)
    h = pltpu.roll(h, lax.rem(128 - DH // 4 * z, 128), 1)
    for i, ref in enumerate((m.v4, m.v5)):
        ref[...] = h[4 + i, : DH // 4]
    for cp in stores:
        cp.wait()


def finish(fin, outq, dtokq, vec):
    n, D = fin.shape[1:]
    any_, vmem = pl.BlockSpec(memory_space=pl.ANY), pl.BlockSpec(memory_space=pltpu.VMEM)
    outs = dict(out=outq.shape, dtok=outq.shape, g_qkv=(n, 3 * D), g_proj=(n, D), g_up=(n, 4 * D), g_down=(D, D))
    vecs = {"v%d" % i: (n if i < 4 else DH // 4,) for i in range(6)}
    scratch = dict(
        inb=(fin.shape, bf), inr=((2,) + outq.shape, bf), outr=((2,) + outq.shape, f32), comb=((D, D), f32),
        turned=((D, D), f32), outb=((8, n, D), f32),
    )
    names = ["fin", "outq", "dtokq", "vec"] + list(outs) + list(vecs) + list(scratch) + ["lsem", "ssem"]
    out, dtok, qkv, proj, up, down, *v = pl.pallas_call(
        functools.partial(finish_kernel, names),
        out_shape=[jax.ShapeDtypeStruct(s, f32) for s in list(outs.values()) + list(vecs.values())],
        in_specs=[any_] * 3 + [vmem],
        out_specs=[any_] * 6 + [vmem] * 6,
        scratch_shapes=[pltpu.VMEM(s, d) for s, d in scratch.values()] + [pltpu.SemaphoreType.DMA((20,))] * 2,
        compiler_params=pltpu.CompilerParams(vmem_limit_bytes=VMEM_LIMIT),
        name="finish",
    )(fin, outq, dtokq, vec)
    return out, dtok, v[0], v[1], qkv, v[4], v[5], proj, v[2], v[3], up, down


def per_device(tokens, lengths, cotangent, pre_gain, pre_shift, w_qkv, query_gain, key_gain, w_proj, mid_gain,
               mid_shift, w_up, w_down):
    vectors = (pre_gain, pre_shift, mid_gain, mid_shift, query_gain, key_gain)
    if tuple(lax.axis_size(a) for a in ("rep", "fsdp", "sp")) != (2, 4, 4):
        return general_layer(tokens, lengths, cotangent, vectors, w_qkv, w_proj, w_up, w_down)
    return finish(*fused_layer(tokens, lengths, cotangent, vectors, w_qkv, w_proj, w_up, w_down))


def solution(mesh):
    rows, vec, mat = P(("rep", "fsdp"), "sp", None), P("fsdp"), P("fsdp", None)
    return jax.shard_map(
        per_device,
        mesh=mesh,
        in_specs=(rows, P(("rep", "fsdp"), None), rows, vec, vec, mat, vec, vec, mat, vec, vec, mat, mat),
        out_specs=(rows, rows, vec, vec, mat, vec, vec, mat, vec, vec, mat, mat),
        check_vma=False,
    )
```

```python
import functools
import math
from types import SimpleNamespace

import jax
import jax.numpy as jnp
from jax import lax
from jax.experimental import pallas as pl
from jax.experimental.pallas import tpu as pltpu
from jax.sharding import PartitionSpec as P

H = 12
DH = 64
EPSILON = 1e-06
MASKED = 1e30
MESH = pl.DeviceIdType.MESH
VMEM_LIMIT = 67043328
bf = jnp.bfloat16
f32 = jnp.float32


def nn(a, b):
    return lax.dot_general(a, b, (((1,), (0,)), ((), ())), preferred_element_type=f32)


def nt(a, b):
    return lax.dot_general(a, b, (((1,), (1,)), ((), ())), preferred_element_type=f32)


def at(i, size, base=0):
    if isinstance(i, int) and isinstance(base, int):
        return pl.ds(base + i * size, size)
    return pl.ds(pl.multiple_of(base + i * size, math.gcd(size, base) if isinstance(base, int) else size), size)


def same_head(n):
    a = lax.broadcasted_iota(jnp.int32, (n, n), 0) // DH
    b = lax.broadcasted_iota(jnp.int32, (n, n), 1) // DH
    return (a == b).astype(f32).astype(bf)


def split2(x):
    hi = x.astype(bf)
    return hi, (x - hi.astype(f32)).astype(bf)


def standardize(x):
    mean = jnp.mean(x, axis=-1, keepdims=True)
    c = x - mean
    r = lax.rsqrt(jnp.mean(c * c, axis=-1, keepdims=True) + EPSILON)
    return c * r, r


def transpose_to(src, dst):
    @pl.loop(0, dst.shape[0] // 128)
    def _(i):
        dst[at(i, 128), :] = src[:, at(i, 128)].astype(f32).T.astype(bf)


def wcols(m, b, s):
    w = m.W[b, :, :, s]
    return w.reshape(w.shape[0] * w.shape[1], w.shape[2])


def wrows(m, b, i):
    w = m.W[b, pl.ds(2 * i, 2), :, :]
    return w.reshape(2 * w.shape[1], w.shape[2])


def select_rows(m, rowbuf, dst):
    T, D = dst.shape

    @pl.loop(0, D // 256)
    def _(i):
        s = at(i, 256)
        dst[:, s] = (nn(m.ebuf[10], rowbuf[0, :, s]) + nn(m.ebuf[11], rowbuf[1, :, s])).astype(bf)


def select_cot(m):
    T, D = m.cot.shape

    @pl.loop(0, D // 256)
    def _(i):
        s = at(i, 256)
        m.cot[:, s] = (nn(m.rowx[0, :, 0:T], m.rowc[0, :, s]) + nn(m.rowx[1, :, 0:T], m.rowc[1, :, s])).astype(bf)


def source_rows(m, n):
    T = m.xs.shape[0]
    row = lax.broadcasted_iota(jnp.int32, (T, n), 0) + m.start + T * m.core
    return jnp.where(row >= 2 * T, row - 2 * T, row), lax.broadcasted_iota(jnp.int32, (T, n), 1)


def place_stage(m):
    T = m.xs.shape[0]
    row, col = source_rows(m, T)
    m.ebuf[10] = (row == col).astype(f32).astype(bf)
    m.ebuf[11] = (row == col + T).astype(f32).astype(bf)


def mask_stage(m):
    t, lane = source_rows(m, 128)
    pic = sum((t >= e).astype(jnp.int32) for e in m.ends)
    hot = (lane == pic).astype(f32)
    m.maskq[...] = (hot * MASKED).astype(bf)
    m.maskk[...] = jnp.where(lane < 4, hot - 1.0, 0.0).astype(bf)


def restore_quarter(m, cat, quarter, dst):
    T, D = m.xs.shape
    n = T // 2
    i = lax.broadcasted_iota(jnp.int32, (n, T), 0) + quarter * n - m.start
    i = jnp.where(i < 0, i + 2 * T, i)
    col = lax.broadcasted_iota(jnp.int32, (n, T), 1)
    a = (i == col).astype(f32).astype(bf)
    b = (i == col + T).astype(f32).astype(bf)

    @pl.loop(0, D // 256)
    def _(k):
        s = at(k, 256)
        dst[:, s] = (nn(a, cat[0, :, s]) + nn(b, cat[1, :, s])).astype(bf)


def gains_stage(m):
    D = m.gains.shape[1]
    n = D // 4
    k = DH // 4
    lane = lax.broadcasted_iota(jnp.int32, (256, D), 0)
    col = lax.broadcasted_iota(jnp.int32, (256, D), 1)
    wide = jnp.zeros((8, D), f32)
    head = jnp.zeros((8, D), f32)
    for u in range(4):
        g = m.gbuf[u].astype(bf)
        wide += nn(g, ((col == lane + n * u) & (lane < n)).astype(f32).astype(bf))
        head += nn(g, ((col % DH == lane + k * u) & (lane < k)).astype(f32).astype(bf))
    r = lax.broadcasted_iota(jnp.int32, (8, D), 0)
    m.gains[...] = jnp.where(r < 4, wide, head)


def norm_stage(src, gain, shift, dst):
    @pl.loop(0, src.shape[0] // 64)
    def _(i):
        s = at(i, 64)
        xh, _ = standardize(src[s, :].astype(f32))
        dst[s, :] = (xh * gain + shift).astype(bf)


def qkv_stage(m, j):
    off = at(j, 256)
    m.v[:, off] = nn(m.mid[...], wcols(m, j, pl.ds(512, 256))).astype(bf)

    @pl.loop(0, 2)
    def _(kind):
        B = same_head(256)
        s = at(kind, 256, 512 * j)
        acc = nn(m.mid[...], wcols(m, j, at(kind, 256)))
        hi, lo = split2(acc)
        c = acc - (nn(hi, B) + nn(lo, B)) * (1.0 / DH)
        r = lax.rsqrt(nn((c * c).astype(bf), B) * (1.0 / DH) + EPSILON)
        xh = c * r
        m.qkh[:, s] = xh.astype(bf)
        m.qkr[:, s] = r.astype(bf)
        val = (xh * m.gains[pl.ds(4 + kind, 1), off]).astype(bf).astype(f32)
        m.qk[kind, :, off] = (val * jnp.where(kind == 0, 1.0 / math.sqrt(DH), 1.0)).astype(bf)


def lane_half(T, e):
    lane = lax.broadcasted_iota(jnp.int32, (T, 128), 1)
    return (lane < DH) if e == 0 else (lane >= DH)


def attend_pair(m, hp):
    T = m.xs.shape[0]
    s = at(hp, 128)
    q2, k2, v2 = m.qk[0, :, s].astype(f32), m.qk[1, :, s], m.v[:, s]
    kx = jnp.concatenate([k2, m.maskk[...]], axis=1)
    outs = []
    for e in (0, 1):
        qe = jnp.where(lane_half(T, e), q2, 0.0).astype(bf)
        E = jnp.exp(nt(jnp.concatenate([qe, m.maskq[...]], axis=1), kx))
        p = (E * (1.0 / jnp.sum(E, axis=-1, keepdims=True))).astype(bf)
        m.ebuf[2 * hp + e] = p
        outs.append(nn(p, v2))
    m.att[:, s] = jnp.where(lane_half(T, 0), outs[0], outs[1]).astype(bf)


def proj_stage(m):
    @pl.loop(0, m.xs.shape[1] // 256)
    def _(i):
        s = at(i, 256)
        m.resid[:, s] = m.xs[:, s].astype(f32) + nn(m.att[...], wcols(m, 3, s))


def gelu_both(x):
    z = jnp.abs(x) * (1.0 / math.sqrt(2.0))
    t = 1.0 / (1.0 + 0.3275911 * z)
    p = ((((1.061405429 * t - 1.453152027) * t + 1.421413741) * t - 0.284496736) * t + 0.254829592) * t
    ex = jnp.exp(-0.5 * x * x)
    tail = 0.5 * p * ex
    phi = jnp.where(x < 0, tail, 1.0 - tail)
    return x * phi, phi + x * ex * (1.0 / math.sqrt(2.0 * math.pi))


def up_stage(m, j):
    D = m.xs.shape[1]

    @pl.loop(0, D // 256)
    def _(i):
        a, d = gelu_both(nn(m.mid[...], wcols(m, 4 + j, at(i, 256))))
        s = at(i, 256, j * D)
        m.act[:, s] = a.astype(bf)
        m.gp[:, s] = d.astype(bf)


def out_stage(m, i):
    D = m.xs.shape[1]
    s = at(i, 256)
    acc = m.resid[:, s]
    for u in range(4):
        w = m.W[8:12, u, :, s]
        acc += nn(m.act[:, u * D : (u + 1) * D], w.reshape(D, 256))
    m.osel[:, s] = acc.astype(bf)


def dinner_stage(m, u):
    D = m.xs.shape[1]
    for i in range(2):
        w = m.W[8 + 2 * i : 10 + 2 * i, u, :, :]
        s = at(i, D // 2, u * D)
        d = nt(m.cot[...], w.reshape(D // 2, D))
        m.gp[:, s] = (d * m.gp[:, s].astype(f32)).astype(bf)


def dmid_stage(m, i):
    D = m.xs.shape[1]
    acc = nt(m.gp[:, 0:D], wrows(m, 4, i))
    for j in range(1, 4):
        acc += nt(m.gp[:, j * D : (j + 1) * D], wrows(m, 4 + j, i))
    m.dres[:, at(i, D // 2)] = acc


def dresid_stage(m):
    T, D = m.dres.shape
    g = m.gains[2:3, :]

    @pl.loop(0, T // 64)
    def _(i):
        s = at(i, 64)
        dm = m.dres[s, :]
        xh, r = standardize(m.resid[s, :])
        dx = dm * g
        m1 = jnp.mean(dx, axis=-1, keepdims=True)
        m2 = jnp.mean(dx * xh, axis=-1, keepdims=True)
        dr = m.cot[s, :].astype(f32) + r * (dx - m1 - xh * m2)
        m.dres[s, :] = dr
        m.dattn[s, :] = dr.astype(bf)
        m.gsum[2:3, :] += jnp.sum(dm * xh, axis=0, keepdims=True)
        m.gsum[3:4, :] += jnp.sum(dm, axis=0, keepdims=True)


def datt_stage(m):
    n = m.xs.shape[1] // 2

    @pl.loop(0, 2)
    def _(i):
        m.datt[:, at(i, n)] = nt(m.dattn[...], wrows(m, 3, i)).astype(bf)


def attend_back_pair(m, j, i):
    T, D = m.xs.shape
    hp = 2 * j + i
    s = at(hp, 128)
    do = m.datt[:, s].astype(f32)
    B = same_head(128)
    hi, lo = split2(do * m.att[:, s].astype(f32))
    dl = nn(hi, B) + nn(lo, B)
    k2, v2 = m.qk[1, :, s], m.v[:, s]
    lane = lax.broadcasted_iota(jnp.int32, (T, 128), 1)
    vx = jnp.concatenate([v2, (lane < 2).astype(f32).astype(bf)], axis=1)
    doT = do.T.astype(bf)
    qT = m.qk[0, :, s].astype(f32).T.astype(bf)
    dqs, dks, dvs = [], [], []
    for e in (0, 1):
        de = jnp.where(lane_half(T, e), do, 0.0).astype(bf)
        dle = dl[:, e * DH : e * DH + 1]
        dh = dle.astype(bf).astype(f32)
        dmask = jnp.where(lane == 0, -dh, jnp.where(lane == 1, dh - dle, 0.0)).astype(bf)
        t = nt(jnp.concatenate([de, dmask], axis=1), vx)
        E = m.ebuf[2 * hp + e]
        ds = (E.astype(f32) * t).astype(bf)
        dqs.append(nn(ds, k2))
        dks.append(nn(qT[e * DH : (e + 1) * DH, :], ds))
        dvs.append(nn(doT[e * DH : (e + 1) * DH, :], E))
    dq = jnp.where(lane_half(T, 0), dqs[0], dqs[1]) * (1.0 / math.sqrt(DH))
    dk = jnp.concatenate(dks, axis=0).T
    dv = jnp.concatenate(dvs, axis=0).T
    m.dqkv[:, at(i, 128, D * j + 512)] = dv.astype(bf)
    for kind, d in ((0, dq), (1, dk)):
        d = d.astype(bf).astype(f32)
        w = at(i, 128, 512 * j + 256 * kind)
        xh = m.qkh[:, w].astype(f32)
        r = m.qkr[:, w].astype(f32)
        m.gsum[4 + kind : 5 + kind, s] = jnp.sum(d * xh, axis=0, keepdims=True)
        dx = d * m.gains[4 + kind : 5 + kind, s]
        h1, l1 = split2(dx)
        m1 = (nn(h1, B) + nn(l1, B)) * (1.0 / DH)
        h2, l2 = split2(dx * xh)
        m2 = (nn(h2, B) + nn(l2, B)) * (1.0 / DH)
        m.dqkv[:, at(i, 128, D * j + 256 * kind)] = (r * (dx - m1 - xh * m2)).astype(bf)


def dnormed_stage(m, i):
    D = m.xs.shape[1]
    acc = nt(m.dqkv[:, 0:D], wrows(m, 0, i))
    for j in range(1, 3):
        acc += nt(m.dqkv[:, j * D : (j + 1) * D], wrows(m, j, i))
    m.resid[:, at(i, D // 2)] = acc


def dtokens_stage(m):
    T, D = m.dres.shape
    g = m.gains[0:1, :]

    @pl.loop(0, T // 64)
    def _(i):
        s = at(i, 64)
        dn = m.resid[s, :]
        xh, r = standardize(m.xs[s, :].astype(f32))
        dx = dn * g
        m1 = jnp.mean(dx, axis=-1, keepdims=True)
        m2 = jnp.mean(dx * xh, axis=-1, keepdims=True)
        m.dtok[s, :] = (m.dres[s, :] + r * (dx - m1 - xh * m2)).astype(bf)
        m.gsum[0:1, :] += jnp.sum(dn * xh, axis=0, keepdims=True)
        m.gsum[1:2, :] += jnp.sum(dn, axis=0, keepdims=True)


def grad_down(m, j):
    D = m.xs.shape[1]
    n = D // 4

    @pl.loop(0, 4)
    def _(u):
        m.G[j, u] = nn(m.cotT[j * n : (j + 1) * n, :], m.act[:, at(u, D)]).astype(bf)


def grad_block(m, b, lhsT, rhs, base):
    D = m.xs.shape[1]
    n = D // 4

    @pl.loop(0, D // 256)
    def _(i):
        r = nn(lhsT[...], rhs[:, at(i, 256, base)]).astype(bf)
        for u in range(4):
            m.G[b, u, :, at(i, 256)] = r[u * n : (u + 1) * n]


GATHER = ("y", "xy", "xy", "xy", "xy", "xy", "x", "y", "xy", "xy", "y", "x")
REDUCE = ("xy", "xy", "xy", "xy", "xy", "xy", "xy", "xy", "xy", "x", "xy", "x")
SLOTS = (2, 4, 4, 4, 4, 12, 12)
ORDER = (
    "rp0", "g1_0", "place", "rw0", "rs1", "g1_1", "g2_0", "g1_2", "selx", "g1_3", "rp1", "g3_0", "gains", "g2_1",
    "g4_0", "norm1", "g2_2", "g2_3", "g1_4", "g3_1", "qkv0", "att0", "g2_4", "g3_2", "g1_5", "g1_6", "g4_1", "qkv1",
    "g1_7", "rw1", "g4_2", "qkv2", "g2_5", "att1", "selc", "g2_6", "g3_3", "g2_7", "g3_4", "g1_8", "g1_9", "g1_10",
    "g1_11", "g4_3", "g3_5", "att2", "proj", "g3_6", "norm2", "midT", "g4_4", "g2_8", "g3_7", "g4_5", "g4_6", "up2",
    "g2_9", "up0", "g2_10", "g2_11", "cotT", "g4_7", "up1", "up3", "gd0", "r0_0", "g3_8", "gd1", "r0_1", "r1_0", "g3_9",
    "gd3", "g3_10", "g3_11", "g4_8", "g4_9", "r1_1", "gd2", "g4_10", "r0_2", "g4_11", "din2", "r2_0", "r1_2", "r0_3",
    "din0", "gu0", "r2_1", "out2", "out1", "r1_3", "r3_0", "r0_4", "r2_2", "din1", "din3", "r1_4", "dmid1", "r3_1",
    "r2_3", "gu1", "gu2", "r0_5", "r4_0", "dmid0", "r3_2", "r1_5", "out0", "r0_6", "r2_4", "dres", "r4_1", "attT",
    "r3_3", "cat0", "r1_6", "gu3", "r2_5", "r0_7", "r5_0", "datt", "gpj", "r1_7", "r4_2", "r0_8", "r3_4", "nT", "r2_6",
    "r5_1", "r1_8", "bk0", "gq0", "r6_0", "r0_9", "r4_3", "r5_2", "r3_5", "r2_7", "r4_4", "res0", "r1_9", "bk1", "r3_6",
    "r5_3", "r4_5", "gq1", "r2_8", "r5_4", "r0_10", "bk2", "gq2", "r4_6", "r1_10", "r3_7", "r0_11", "r2_9", "dn0",
    "dn1", "r3_8", "resw0", "r5_5", "r6_1", "r6_2", "r1_11", "dtok", "cat1", "r4_7", "r2_10", "r5_6", "res1", "r3_9",
    "v0", "v1", "r6_3", "r6_4", "r7_0", "r7_1", "r2_11", "r3_10", "r7_2", "v2", "r6_5", "r4_8", "r5_7", "r4_9", "r6_6",
    "r3_11", "v3", "r7_3", "r4_10", "r7_4", "r7_5", "r5_8", "r5_9", "r4_11", "v4", "r7_6", "r6_7", "r6_8", "r5_10",
    "r5_11", "v5", "r7_7", "r6_9", "r7_8", "r6_10", "r6_11", "r7_9", "r7_10", "r7_11",
)


class Comm:
    def __init__(self, m):
        self.m = m
        self.x, self.z, sp = lax.axis_index("rep"), lax.axis_index("fsdp"), lax.axis_index("sp")
        self.y, self.c = sp // 2, sp % 2
        x, y, z, c = self.x, self.y, self.z, self.c
        nx, ny = (1 - x, z, sp), (x, z, 2 * (1 - y) + c)
        self.nx, self.ny = nx, ny
        n1 = (x + (1 - c) * (1 - 2 * x), z, 2 * (y + c * (1 - 2 * y)) + c)
        n2 = (x + c * (1 - 2 * x), z, 2 * (y + (1 - c) * (1 - 2 * y)) + c)
        self.orders = {"x": (x, y, nx, ny), "y": (y, x, ny, nx), "xy": (x + c * (y - x), y + c * (x - y), n1, n2)}
        self.core = (x, z, 2 * y + 1 - c)
        self.zat = lambda u: (x, u, sp)
        self.z1 = z + 1 - 2 * (z % 2)
        self.zt = 3 - z
        self.mine = at(c, 384)
        self.other = at(1 - c, 384)

    def gather_order(self, b):
        return self.orders[GATHER[b]]

    def reduce_order(self, b):
        return self.orders[REDUCE[b]]

    def barrier(self):
        sem = pltpu.get_barrier_semaphore()
        peers = [self.nx, self.ny, self.core] + [self.zat((self.z + d) % 4) for d in (1, 2, 3)]
        for p in peers:
            pl.semaphore_signal(sem, inc=1, device_id=p, device_id_type=MESH)
        pl.semaphore_wait(sem, len(peers))

    def copy(self, src, dst, send, recv, dev):
        return pltpu.make_async_remote_copy(
            src_ref=src, dst_ref=dst, send_sem=send, recv_sem=recv, device_id=dev, device_id_type=MESH
        )

    def row_copies(self, arg, buf, k):
        s, r = self.m.rsem.at[0, k], self.m.rsem.at[1, k]
        mine = buf.at[self.y, at(self.c, 256)]
        there = buf.at[1 - self.y, at(self.c, 256)]
        local = pltpu.make_async_copy(arg.at[self.y], mine, s.at[0])
        near = self.copy(arg.at[self.y], mine, s.at[1], r.at[1], self.core)
        far = self.copy(arg.at[1 - self.y], mine, s.at[2], r.at[2], self.ny)
        pass_on = self.copy(there, there, s.at[3], r.at[3], self.core)
        return local, near, far, pass_on

    def row_start(self, arg, buf, k):
        local, near, far, _ = self.row_copies(arg, buf, k)
        far.start()
        near.start()
        local.start()

    def row_pass(self, arg, buf, k):
        _, _, far, pass_on = self.row_copies(arg, buf, k)
        far.wait_recv()
        pass_on.start()

    def row_wait(self, arg, buf, k):
        local, near, far, pass_on = self.row_copies(arg, buf, k)
        local.wait()
        near.wait()
        far.wait_send()
        pass_on.wait()

    def gain_copies(self):
        m = self.m
        out = [pltpu.make_async_copy(m.gpack, m.gbuf.at[self.z], m.gsem.at[0, 0])]
        for d in (1, 2, 3):
            dev = self.zat((self.z + d) % 4)
            out.append(self.copy(m.gpack, m.gbuf.at[self.z], m.gsem.at[0, d], m.gsem.at[1, d], dev))
        return out

    def shard(self, b, rows, cols):
        m = self.m
        arg, r0, c0 = (m.a_qkv, 0, 0) if b < 3 else (m.a_proj, 0, 0) if b == 3 else (
            (m.a_up, 0, 768 * (b - 4)) if b < 8 else (m.a_down, 192 * (b - 8), 0))
        return arg.at[pl.ds(pl.multiple_of(r0 + rows[0], 16), rows[1]), pl.ds(pl.multiple_of(c0 + cols[0], 128), cols[1])]

    def spans(self, b):
        c = self.c
        if b < 3:
            return [(256 * b + 1536 * c, 512 * c, 256), (768 + 256 * b + 128 * c, 256 + 128 * c, 128)]
        return [(384 * c, 384 * c, 384)]

    def own_copies(self, b):
        sem, dst = self.m.wsem.at[0, 0, b], self.m.W.at[b, self.z]
        if b < 3:
            return [
                pltpu.make_async_copy(self.shard(b, (0, 192), (768 * i + 256 * b, 256)), dst.at[:, pl.ds(256 * i, 256)], sem)
                for i in range(3)
            ]
        return [pltpu.make_async_copy(self.shard(b, (0, 192), (0, 768)), dst, sem)]

    def own_start(self, b):
        for cp in self.own_copies(b):
            cp.start()

    def own_wait(self, b):
        m = self.m
        pltpu.make_async_copy(m.W.at[b, self.z], m.W.at[b, self.z], m.wsem.at[0, 0, b]).wait()

    def z_start(self, b):
        m = self.m
        f1, f2, _, _ = self.gather_order(b)
        q = 2 * f2 + f1
        for d in (1, 2, 3):
            for src, to, n in self.spans(b):
                dst = m.W.at[b, self.z, at(q, 48), pl.ds(pl.multiple_of(to, 128), n)]
                sems = m.wsem.at[0, 1, b], m.wsem.at[1, 1, b]
                self.copy(self.shard(b, (48 * q, 48), (src, n)), dst, *sems, self.zat((self.z + d) % 4)).start()

    def plane(self, k, b):
        m = self.m
        f1, f2, n1, n2 = self.gather_order(b)
        rows, dev = {2: (at(2 * f2 + f1, 48), n1), 3: (at(f2, 96), n2), 4: (pl.ds(0, 192), self.core)}[k]
        out = []
        for d in (1, 2, 3):
            ref = m.W.at[b, (self.z + d) % 4, rows, self.mine]
            out.append(self.copy(ref, ref, m.wsem.at[0, k, b], m.wsem.at[1, k, b], dev))
        return out

    def w_all(self, k, b):
        m = self.m
        f1, f2, n1, n2 = self.gather_order(b)
        part = at(2 * f2 + f1, 48)
        rows, dev = {1: (part, self.core), 2: (part, n1), 3: (at(f2, 96), n2), 4: (pl.ds(0, 192), self.core)}[k]
        ref = m.W.at[b, 0:3, rows, self.mine]
        return self.copy(ref, ref, m.wsem.at[0, k, b], m.wsem.at[1, k, b], dev)

    def ag_step(self, k, b):
        self.w_all(k, b).wait_recv()
        if k < 4:
            for cp in self.plane(k + 1, b):
                cp.start()
        else:
            for j in (1, 2, 3, 4):
                self.w_all(j, b).wait_send()
            self.own_wait(b)

    def rs_copies(self, k, b):
        m = self.m
        G, z = m.G, self.z
        f1, f2, n1, n2 = self.reduce_order(b)
        slot = b % SLOTS[k]
        rows = at(f1, 96)
        sem = lambda j: (m.psem.at[0, j, slot], m.psem.at[1, j, slot])
        if k == 0:
            return [self.copy(G.at[b, :, :, self.other], m.rA.at[slot], *sem(0), self.core)]
        if k == 1:
            return [self.copy(G.at[b, :, at(1 - f1, 96), self.mine], m.rB.at[slot], *sem(1), n1)]
        if k == 2:
            return [
                self.copy(G.at[b, self.z1, rows, self.mine], m.rC.at[slot, 0], *sem(2), self.zat(self.z1)),
                self.copy(G.at[b, 3 - self.z1, rows, self.mine], m.rC.at[slot, 1], *sem(7), self.zat(self.z1)),
            ]
        if k == 3:
            return [self.copy(G.at[b, self.zt, rows, self.mine], m.rD.at[slot], *sem(3), self.zat(self.zt))]
        if k == 4:
            return [self.copy(G.at[b, z, rows, self.mine], m.rE.at[slot], *sem(4), n2)]
        if k == 5:
            ref = G.at[b, z, rows, self.mine]
            return [self.copy(ref, ref, *sem(5), n1)]
        ref = G.at[b, z, :, self.mine]
        return [self.copy(ref, ref, *sem(6), self.core)]

    def rs_step(self, k, b):
        m = self.m
        G, z = m.G, self.z
        rows = at(self.reduce_order(b)[0], 96)
        if k > 0:
            slot = b % SLOTS[k - 1]
            for cp in self.rs_copies(k - 1, b):
                cp.wait()
        if k == 1:

            @pl.loop(0, 4)
            def _(u):
                G[b, u, :, self.mine] = (G[b, u, :, self.mine].astype(f32) + m.rA[slot, u].astype(f32)).astype(bf)
        elif k == 2:

            @pl.loop(0, 4)
            def _(u):
                G[b, u, rows, self.mine] = (G[b, u, rows, self.mine].astype(f32) + m.rB[slot, u].astype(f32)).astype(bf)
        elif k == 3:
            for i, u in ((0, z), (1, self.zt)):
                G[b, u, rows, self.mine] = (G[b, u, rows, self.mine].astype(f32) + m.rC[slot, i].astype(f32)).astype(bf)
        elif k in (4, 5):
            r = (m.rD if k == 4 else m.rE)[slot]
            G[b, z, rows, self.mine] = (G[b, z, rows, self.mine].astype(f32) + r.astype(f32)).astype(bf)
        if k < 7:
            for cp in self.rs_copies(k, b):
                cp.start()
        else:
            self.fin_copy(b).start()

    def fin_copy(self, b):
        return pltpu.make_async_copy(self.m.G.at[b, self.z], self.m.fin.at[b], self.m.fsem.at[b])

    def vec_copy(self, i):
        m = self.m
        dev = [self.core, self.nx, self.ny, self.zat(self.z1), self.zat(self.zt)][i]
        return self.copy(m.gs.at[i], m.gr.at[i], m.vsem.at[0, i], m.vsem.at[1, i], dev)

    def vec_step(self, i):
        m = self.m
        if i == 0:
            m.gs[0] = m.gsum[...]
        else:
            self.vec_copy(i - 1).wait()
            m.gs[i] = m.gs[i - 1] + m.gr[i - 1]
        if i < 5:
            self.vec_copy(i).start()
        else:
            m.vec[...] = m.gs[5]

    def cat_copy(self, cat, k):
        half = cat.at[self.c]
        return self.copy(half, half, self.m.osem.at[0, k, 0], self.m.osem.at[1, k, 0], self.core)

    def quart(self, i):
        T, D = self.m.xs.shape
        return self.m.act.at[pl.ds(i * (T // 2), T // 2), pl.ds(3 * D, D)]

    def quarter_copies(self, dst, k):
        m = self.m
        far = self.copy(self.quart(1), dst.at[self.y], m.osem.at[0, k, 1], m.osem.at[1, k, 1], self.ny)
        near = pltpu.make_async_copy(self.quart(0), dst.at[self.y], m.osem.at[0, k, 2])
        return far, near

    def result_send(self, cat, dst, k):
        m = self.m
        self.cat_copy(cat, k).wait()
        restore_quarter(m, cat, 2 * (1 - self.y) + self.c, self.quart(1))
        far, near = self.quarter_copies(dst, k)
        far.start()
        restore_quarter(m, cat, 2 * self.y + self.c, self.quart(0))
        near.start()

    def result_wait(self, dst, k):
        far, near = self.quarter_copies(dst, k)
        far.wait()
        near.wait()


SCRATCH = lambda T, D, FF: dict(
    gains=((8, D), f32), maskq=((T, 128), bf), maskk=((T, 128), bf), xs=((T, D), bf), cot=((T, D), bf),
    mid=((T, D), bf), midT=((D, T), bf), cotT=((D, T), bf),
    qk=((2, T, D), bf), v=((T, D), bf), qkh=((T, 2 * D), bf), qkr=((T, 2 * D), bf),
    ebuf=((H, T, T), bf), att=((T, D), bf), resid=((T, D), f32),
    act=((T, FF), bf), gp=((T, FF), bf), dres=((T, D), f32), datt=((T, D), bf), gsum=((8, D), f32),
)


def prepare(m, lengths, y):
    T = m.xs.shape[0]
    l = [lengths[y, k] for k in range(4)]
    m.ends = [l[0], l[0] + l[1], l[0] + l[1] + l[2]]
    m.start = jnp.where(l[0] == T, 0, jnp.where(l[1] == T, m.ends[0], jnp.where(l[2] == T, m.ends[1], m.ends[2])))
    m.dattn = m.mid
    m.dqkv = m.act
    m.attT = m.cotT


def two(f):
    @pl.loop(0, 2)
    def _(i):
        f(i)


def compute_pieces(m):
    D = m.xs.shape[1]
    pieces = {
        "place": lambda: place_stage(m),
        "norm1": lambda: norm_stage(m.xs, m.gains[0:1, :], m.gains[1:2, :], m.mid),
        "nT": lambda: (norm_stage(m.xs, m.gains[0:1, :], m.gains[1:2, :], m.mid), transpose_to(m.mid, m.midT)),
        "proj": lambda: proj_stage(m),
        "norm2": lambda: norm_stage(m.resid, m.gains[2:3, :], m.gains[3:4, :], m.mid),
        "midT": lambda: transpose_to(m.mid, m.midT),
        "cotT": lambda: transpose_to(m.cot, m.cotT),
        "dres": lambda: dresid_stage(m),
        "attT": lambda: transpose_to(m.att, m.attT),
        "gpj": lambda: grad_block(m, 8, m.attT, m.dattn, 0),
        "datt": lambda: datt_stage(m),
        "dtok": lambda: dtokens_stage(m),
    }

    def several(name, n, f):
        for i in range(n):
            pieces["%s%d" % (name, i)] = functools.partial(f, i)

    several("qkv", 3, lambda i: qkv_stage(m, i))
    several("att", 3, lambda j: two(lambda i: attend_pair(m, 2 * j + i)))
    several("up", 4, lambda i: up_stage(m, i))
    several("gd", 4, lambda i: grad_down(m, i))
    several("out", 3, lambda i: out_stage(m, i))
    several("din", 4, lambda i: dinner_stage(m, i))
    several("dmid", 2, lambda i: dmid_stage(m, i))
    several("gu", 4, lambda i: grad_block(m, 4 + i, m.midT, m.gp, i * D))
    several("bk", 3, lambda j: two(lambda i: attend_back_pair(m, j, i)))
    several("gq", 3, lambda i: grad_block(m, 9 + i, m.midT, m.dqkv, i * D))
    several("dn", 2, lambda i: dnormed_stage(m, i))
    return pieces


def layer_kernel(comm_names, *refs):
    m = SimpleNamespace(**dict(zip(comm_names, refs)))
    cm = Comm(m)
    m.osel, m.dtok = m.rowx.at[cm.c], m.rowc.at[cm.c]
    m.maskq, m.maskk = m.rowx.at[0, :, pl.ds(512, 128)], m.rowx.at[1, :, pl.ds(512, 128)]
    m.core = cm.c
    prepare(m, m.lengths, cm.y)
    m.gpack[...] = jnp.zeros_like(m.gpack)
    for i in range(6):
        g = getattr(m, "g%d" % i)
        m.gpack[i : i + 1, 0 : g.shape[0]] = g[...].astype(f32).reshape(1, g.shape[0])
    m.gsum[...] = jnp.zeros_like(m.gsum)
    cm.barrier()
    cm.row_start(m.tokens, m.rowx, 0)
    for g in cm.gain_copies():
        g.start()
    for b in range(12):
        cm.z_start(b)
        cm.own_start(b)

    def gains():
        for g in cm.gain_copies():
            g.wait()
        gains_stage(m)

    def selx():
        select_rows(m, m.rowx, m.xs)
        for h in range(2):
            m.rowx[h, :, 0 : m.ebuf.shape[1]] = m.ebuf[10 + h]
        mask_stage(m)

    rows = ((m.tokens, m.rowx, 0), (m.cotangent, m.rowc, 1))
    pieces = compute_pieces(m)
    pieces.update(
        gains=gains,
        selx=selx,
        selc=lambda: select_cot(m),
        rs1=lambda: cm.row_start(*rows[1]),
        cat0=lambda: cm.cat_copy(m.rowx, 0).start(),
        cat1=lambda: cm.cat_copy(m.rowc, 1).start(),
        res0=lambda: cm.result_send(m.rowx, m.outq, 0),
        res1=lambda: cm.result_send(m.rowc, m.dtokq, 1),
        resw0=lambda: cm.result_wait(m.outq, 0),
    )
    for k in range(2):
        pieces["rp%d" % k] = functools.partial(cm.row_pass, *rows[k])
        pieces["rw%d" % k] = functools.partial(cm.row_wait, *rows[k])
    for i in range(6):
        pieces["v%d" % i] = functools.partial(cm.vec_step, i)
    for b in range(12):
        for k in range(1, 5):
            pieces["g%d_%d" % (k, b)] = functools.partial(cm.ag_step, k, b)
        for k in range(8):
            pieces["r%d_%d" % (k, b)] = functools.partial(cm.rs_step, k, b)
    assert sorted(pieces) == sorted(ORDER)
    for name in ORDER:
        pieces[name]()
    for b in range(12):
        cm.fin_copy(b).wait()
    cm.result_wait(m.dtokq, 1)


def fused_layer(tokens, lengths, cotangent, vectors, w_qkv, w_proj, w_up, w_down):
    T, D, FF = tokens.shape[0] * tokens.shape[1], tokens.shape[2], w_up.shape[1]
    any_, vmem = pl.BlockSpec(memory_space=pl.ANY), pl.BlockSpec(memory_space=pltpu.VMEM)
    ins = ["tokens", "lengths", "cotangent", "a_qkv", "a_proj", "a_up", "a_down"] + ["g%d" % i for i in range(6)]
    outs = dict(
        fin=((12, D // 4, D), bf), outq=(tokens.shape, bf), dtokq=(tokens.shape, bf), vec=((8, D), f32)
    )
    scratch = SCRATCH(T, D, FF)
    del scratch["maskq"], scratch["maskk"]
    scratch.update(
        W=((12, 4, D // 4, D), bf), G=((12, 4, D // 4, D), bf), rowx=((2, T, D), bf), rowc=((2, T, D), bf),
        gbuf=((4, 8, 256), f32), gpack=((8, 256), f32),
        rA=((SLOTS[0], 4, 192, 384), bf), rB=((SLOTS[1], 4, 96, 384), bf), rC=((SLOTS[2], 2, 96, 384), bf),
        rD=((SLOTS[3], 96, 384), bf),
        rE=((SLOTS[4], 96, 384), bf), gs=((6, 8, D), f32), gr=((5, 8, D), f32),
    )
    sems = dict(
        rsem=(2, 2, 4), gsem=(2, 4), wsem=(2, 5, 12), psem=(2, 8, 12), fsem=(12,), vsem=(2, 5), osem=(2, 2, 3)
    )
    names = ins + list(outs) + list(scratch) + list(sems)
    return pl.pallas_call(
        functools.partial(layer_kernel, names),
        out_shape=[jax.ShapeDtypeStruct(s, d) for s, d in outs.values()],
        in_specs=[any_, pl.BlockSpec(memory_space=pltpu.SMEM), any_] + [any_] * 4 + [vmem] * 6,
        out_specs=[any_, any_, any_, vmem],
        scratch_shapes=[pltpu.VMEM(s, d) for s, d in scratch.values()]
        + [pltpu.SemaphoreType.DMA(s) for s in sems.values()],
        compiler_params=pltpu.CompilerParams(collective_id=0, has_side_effects=True, vmem_limit_bytes=VMEM_LIMIT),
        name="layer",
    )(tokens, lengths, cotangent, w_qkv, w_proj, w_up, w_down, *vectors)


def plain_kernel(names, *refs):
    m = SimpleNamespace(**dict(zip(names, refs)))
    sp = lax.axis_index("sp")
    m.core = sp % 2
    prepare(m, m.lengths, sp // 2)
    m.gsum[...] = jnp.zeros_like(m.gsum)
    pieces = compute_pieces(m)
    pieces["selx"] = lambda: (select_rows(m, m.rowx, m.xs), select_rows(m, m.rowc, m.cot), mask_stage(m))
    for name in ORDER:
        if name in pieces:
            pieces[name]()


def general_layer(tokens, lengths, cotangent, vectors, w_qkv, w_proj, w_up, w_down):
    T, D, FF = tokens.shape[0] * tokens.shape[1], tokens.shape[2], w_up.shape[1]
    n = D // 4
    gather = lambda v: lax.all_gather(v, "fsdp", axis=0, tiled=True)
    qkv, proj, up, down = (gather(w) for w in (w_qkv, w_proj, w_up, w_down))
    by_columns = lambda w: w.reshape(4, n, -1, D).transpose(2, 0, 1, 3)
    swap = lambda w: w.reshape(w.shape[0], 3, 3, -1).transpose(0, 2, 1, 3).reshape(w.shape)
    W = jnp.concatenate(
        [by_columns(swap(qkv)), by_columns(proj), by_columns(up), down.reshape(4, 4, n, D).transpose(1, 0, 2, 3)]
    )
    gains = [gather(v).astype(f32) for v in vectors]
    gains = [jnp.tile(g, D // g.shape[0]) for g in gains] + [jnp.zeros(D, f32)] * 2
    sp = lax.axis_index("sp")
    whole_row = lambda v: lax.dynamic_index_in_dim(lax.all_gather(v, "sp", axis=1, tiled=True), sp // 2, 0, False)
    rowx, rowc = (whole_row(v).reshape(2, T, D) for v in (tokens, cotangent))
    scratch = SCRATCH(T, D, FF)
    gsum = scratch.pop("gsum")
    del scratch["gains"]
    outs = dict(G=(W.shape, bf), osel=((T, D), bf), dtok=((T, D), bf), gsum=gsum)
    vmem = pl.BlockSpec(memory_space=pltpu.VMEM)
    names = ["lengths", "W", "rowx", "rowc", "gains"] + list(outs) + list(scratch)
    G, osel, dtok, gsum = pl.pallas_call(
        functools.partial(plain_kernel, names),
        out_shape=[jax.ShapeDtypeStruct(s, d) for s, d in outs.values()],
        in_specs=[pl.BlockSpec(memory_space=pltpu.SMEM)] + [vmem] * 4,
        out_specs=[vmem] * 4,
        scratch_shapes=[pltpu.VMEM(s, d) for s, d in scratch.values()],
        compiler_params=pltpu.CompilerParams(vmem_limit_bytes=VMEM_LIMIT),
        name="layer",
    )(lengths, W, rowx, rowc, jnp.stack(gains))

    def reduce(v):
        part = lax.psum_scatter(v.astype(bf), "fsdp", scatter_dimension=0, tiled=True)
        return lax.psum(part, ("rep", "sp")).astype(f32)

    natural = lambda g: g.reshape(-1, D, D).transpose(1, 0, 2).reshape(D, -1)
    g_down = G[0:4].transpose(1, 3, 0, 2).reshape(4 * D, D)
    heads = jnp.sum(gsum[4:6].reshape(2, -1, DH), axis=1)
    vecs = [reduce(v) for v in (gsum[0], gsum[1], gsum[2], gsum[3], heads[0], heads[1])]
    start = jnp.sum(jnp.where(jnp.arange(4)[None] < jnp.argmax(lengths, axis=1)[:, None], lengths, 0), axis=1)

    def back(half):
        rows = lax.all_gather(half, "sp", axis=0, tiled=True).reshape(2, 2 * T, D)
        rows = jnp.stack([jnp.roll(rows[r], start[r], axis=0) for r in range(2)])
        size = 2 * T // 4
        return lax.dynamic_slice_in_dim(rows, sp * size, size, axis=1).astype(f32)

    return (back(osel), back(dtok), vecs[0], vecs[1], reduce(swap(natural(G[9:12]))), vecs[4], vecs[5],
            reduce(natural(G[8:9])), vecs[2], vecs[3], reduce(natural(G[4:8])), reduce(g_down))


def widen(src, dst):
    @pl.loop(0, src.shape[0] // 64)
    def _(i):
        dst[at(i, 64), :] = src[at(i, 64), :].astype(f32)


def finish_kernel(names, *refs):
    m = SimpleNamespace(**dict(zip(names, refs)))
    n, D = m.fin.shape[1], m.fin.shape[2]
    loads = [pltpu.make_async_copy(m.fin.at[b], m.inb.at[b], m.lsem.at[b]) for b in range(12)]
    rows = [(m.outq, m.out, 0), (m.dtokq, m.dtok, 1)]
    row_loads = [pltpu.make_async_copy(src, m.inr.at[i], m.lsem.at[12 + i]) for src, _, i in rows]
    for cp in row_loads[:1] + loads[:4] + loads[4:] + row_loads[1:]:
        cp.start()
    stores = []

    def store(src, dst):
        cp = pltpu.make_async_copy(src, dst, m.ssem.at[len(stores)])
        cp.start()
        stores.append(cp)

    def row(i):
        row_loads[i].wait()
        widen(m.inr.at[i, 0], m.outr.at[i, 0])
        widen(m.inr.at[i, 1], m.outr.at[i, 1])
        store(m.outr.at[i], rows[i][1])

    row(0)
    for b in range(4):
        loads[b].wait()
        widen(m.inb.at[b], m.comb.at[b * n : (b + 1) * n])
    for h in range(2):

        @pl.loop(h * D // 256, (h + 1) * D // 256)
        def _(i):
            m.turned[at(i, 128), :] = m.comb[:, at(i, 128)].T

        half = pl.ds(h * (D // 2), D // 2)
        store(m.turned.at[half], m.g_down.at[half])
    for b in range(4, 12):
        loads[b].wait()
        widen(m.inb.at[b], m.outb.at[b - 4])
        if b < 9:
            dst, col = (m.g_up, (b - 4) * D) if b < 8 else (m.g_proj, 0)
            store(m.outb.at[b - 4], dst.at[:, pl.ds(col, D)])
        else:
            for i in range(3):
                store(m.outb.at[b - 4, :, pl.ds(256 * i, 256)], m.g_qkv.at[:, pl.ds(D * i + 256 * (b - 9), 256)])
    row(1)
    z = lax.axis_index("fsdp")
    v = m.vec[...]
    wide = pltpu.roll(v, lax.rem(D - n * z, D), 1)
    for i, ref in enumerate((m.v0, m.v1, m.v2, m.v3)):
        ref[...] = wide[i, :n]
    h = v[:, :128]
    for i in range(1, D // 128):
        h += v[:, 128 * i : 128 * (i + 1)]
    h = h + pltpu.roll(h, DH, 1)
    h = pltpu.roll(h, lax.rem(128 - DH // 4 * z, 128), 1)
    for i, ref in enumerate((m.v4, m.v5)):
        ref[...] = h[4 + i, : DH // 4]
    for cp in stores:
        cp.wait()


def finish(fin, outq, dtokq, vec):
    n, D = fin.shape[1:]
    any_, vmem = pl.BlockSpec(memory_space=pl.ANY), pl.BlockSpec(memory_space=pltpu.VMEM)
    outs = dict(out=outq.shape, dtok=outq.shape, g_qkv=(n, 3 * D), g_proj=(n, D), g_up=(n, 4 * D), g_down=(D, D))
    vecs = {"v%d" % i: (n if i < 4 else DH // 4,) for i in range(6)}
    scratch = dict(
        inb=(fin.shape, bf), inr=((2,) + outq.shape, bf), outr=((2,) + outq.shape, f32), comb=((D, D), f32),
        turned=((D, D), f32), outb=((8, n, D), f32),
    )
    names = ["fin", "outq", "dtokq", "vec"] + list(outs) + list(vecs) + list(scratch) + ["lsem", "ssem"]
    out, dtok, qkv, proj, up, down, *v = pl.pallas_call(
        functools.partial(finish_kernel, names),
        out_shape=[jax.ShapeDtypeStruct(s, f32) for s in list(outs.values()) + list(vecs.values())],
        in_specs=[any_] * 3 + [vmem],
        out_specs=[any_] * 6 + [vmem] * 6,
        scratch_shapes=[pltpu.VMEM(s, d) for s, d in scratch.values()] + [pltpu.SemaphoreType.DMA((20,))] * 2,
        compiler_params=pltpu.CompilerParams(vmem_limit_bytes=VMEM_LIMIT),
        name="finish",
    )(fin, outq, dtokq, vec)
    return out, dtok, v[0], v[1], qkv, v[4], v[5], proj, v[2], v[3], up, down


def per_device(tokens, lengths, cotangent, pre_gain, pre_shift, w_qkv, query_gain, key_gain, w_proj, mid_gain,
               mid_shift, w_up, w_down):
    vectors = (pre_gain, pre_shift, mid_gain, mid_shift, query_gain, key_gain)
    if tuple(lax.axis_size(a) for a in ("rep", "fsdp", "sp")) != (2, 4, 4):
        return general_layer(tokens, lengths, cotangent, vectors, w_qkv, w_proj, w_up, w_down)
    return finish(*fused_layer(tokens, lengths, cotangent, vectors, w_qkv, w_proj, w_up, w_down))


def solution(mesh):
    rows, vec, mat = P(("rep", "fsdp"), "sp", None), P("fsdp"), P("fsdp", None)
    return jax.shard_map(
        per_device,
        mesh=mesh,
        in_specs=(rows, P(("rep", "fsdp"), None), rows, vec, vec, mat, vec, vec, mat, vec, vec, mat, mat),
        out_specs=(rows, rows, vec, vec, mat, vec, vec, mat, vec, vec, mat, mat),
        check_vma=False,
    )
```

```python
import functools
import math
from types import SimpleNamespace

import jax
import jax.numpy as jnp
from jax import lax
from jax.experimental import pallas as pl
from jax.experimental.pallas import tpu as pltpu
from jax.sharding import PartitionSpec as P

H = 12
DH = 64
EPSILON = 1e-06
MASKED = 1e30
MESH = pl.DeviceIdType.MESH
VMEM_LIMIT = 67043328
bf = jnp.bfloat16
f32 = jnp.float32


def nn(a, b):
    return lax.dot_general(a, b, (((1,), (0,)), ((), ())), preferred_element_type=f32)


def nt(a, b):
    return lax.dot_general(a, b, (((1,), (1,)), ((), ())), preferred_element_type=f32)


def at(i, size, base=0):
    if isinstance(i, int) and isinstance(base, int):
        return pl.ds(base + i * size, size)
    return pl.ds(pl.multiple_of(base + i * size, math.gcd(size, base) if isinstance(base, int) else size), size)


def same_head(n):
    a = lax.broadcasted_iota(jnp.int32, (n, n), 0) // DH
    b = lax.broadcasted_iota(jnp.int32, (n, n), 1) // DH
    return (a == b).astype(f32).astype(bf)


def split2(x):
    hi = x.astype(bf)
    return hi, (x - hi.astype(f32)).astype(bf)


def standardize(x):
    mean = jnp.mean(x, axis=-1, keepdims=True)
    c = x - mean
    r = lax.rsqrt(jnp.mean(c * c, axis=-1, keepdims=True) + EPSILON)
    return c * r, r


def transpose_to(src, dst):
    @pl.loop(0, dst.shape[0] // 128)
    def _(i):
        dst[at(i, 128), :] = src[:, at(i, 128)].astype(f32).T.astype(bf)


def wcols(m, b, s):
    w = m.W[b, :, :, s]
    return w.reshape(w.shape[0] * w.shape[1], w.shape[2])


def wrows(m, b, i):
    w = m.W[b, pl.ds(2 * i, 2), :, :]
    return w.reshape(2 * w.shape[1], w.shape[2])


def select_rows(m, rowbuf, dst):
    T, D = dst.shape

    @pl.loop(0, D // 256)
    def _(i):
        s = at(i, 256)
        dst[:, s] = (nn(m.ebuf[10], rowbuf[0, :, s]) + nn(m.ebuf[11], rowbuf[1, :, s])).astype(bf)


def select_cot(m):
    T, D = m.cot.shape

    @pl.loop(0, D // 256)
    def _(i):
        s = at(i, 256)
        m.cot[:, s] = (nn(m.rowx[0, :, 0:T], m.rowc[0, :, s]) + nn(m.rowx[1, :, 0:T], m.rowc[1, :, s])).astype(bf)


def source_rows(m, n):
    T = m.xs.shape[0]
    row = lax.broadcasted_iota(jnp.int32, (T, n), 0) + m.start + T * m.core
    return jnp.where(row >= 2 * T, row - 2 * T, row), lax.broadcasted_iota(jnp.int32, (T, n), 1)


def place_stage(m):
    T = m.xs.shape[0]
    row, col = source_rows(m, T)
    m.ebuf[10] = (row == col).astype(f32).astype(bf)
    m.ebuf[11] = (row == col + T).astype(f32).astype(bf)


def mask_stage(m):
    t, lane = source_rows(m, 128)
    pic = sum((t >= e).astype(jnp.int32) for e in m.ends)
    hot = (lane == pic).astype(f32)
    m.maskq[...] = (hot * MASKED).astype(bf)
    m.maskk[...] = jnp.where(lane < 4, hot - 1.0, 0.0).astype(bf)


def restore_quarter(m, cat, quarter, dst):
    T, D = m.xs.shape
    n = T // 2
    i = lax.broadcasted_iota(jnp.int32, (n, T), 0) + quarter * n - m.start
    i = jnp.where(i < 0, i + 2 * T, i)
    col = lax.broadcasted_iota(jnp.int32, (n, T), 1)
    a = (i == col).astype(f32).astype(bf)
    b = (i == col + T).astype(f32).astype(bf)

    @pl.loop(0, D // 256)
    def _(k):
        s = at(k, 256)
        dst[:, s] = (nn(a, cat[0, :, s]) + nn(b, cat[1, :, s])).astype(bf)


def gains_stage(m):
    D = m.gains.shape[1]
    n = D // 4
    k = DH // 4
    lane = lax.broadcasted_iota(jnp.int32, (256, D), 0)
    col = lax.broadcasted_iota(jnp.int32, (256, D), 1)
    wide = jnp.zeros((8, D), f32)
    head = jnp.zeros((8, D), f32)
    for u in range(4):
        g = m.gbuf[u].astype(bf)
        wide += nn(g, ((col == lane + n * u) & (lane < n)).astype(f32).astype(bf))
        head += nn(g, ((col % DH == lane + k * u) & (lane < k)).astype(f32).astype(bf))
    r = lax.broadcasted_iota(jnp.int32, (8, D), 0)
    m.gains[...] = jnp.where(r < 4, wide, head)


def norm_stage(src, gain, shift, dst):
    @pl.loop(0, src.shape[0] // 64)
    def _(i):
        s = at(i, 64)
        xh, _ = standardize(src[s, :].astype(f32))
        dst[s, :] = (xh * gain + shift).astype(bf)


def qkv_stage(m, j):
    off = at(j, 256)
    m.v[:, off] = nn(m.mid[...], wcols(m, j, pl.ds(512, 256))).astype(bf)

    @pl.loop(0, 2)
    def _(kind):
        B = same_head(256)
        s = at(kind, 256, 512 * j)
        acc = nn(m.mid[...], wcols(m, j, at(kind, 256)))
        hi, lo = split2(acc)
        c = acc - (nn(hi, B) + nn(lo, B)) * (1.0 / DH)
        r = lax.rsqrt(nn((c * c).astype(bf), B) * (1.0 / DH) + EPSILON)
        xh = c * r
        m.qkh[:, s] = xh.astype(bf)
        m.qkr[:, s] = r.astype(bf)
        val = (xh * m.gains[pl.ds(4 + kind, 1), off]).astype(bf).astype(f32)
        m.qk[kind, :, off] = (val * jnp.where(kind == 0, 1.0 / math.sqrt(DH), 1.0)).astype(bf)


def lane_half(T, e):
    lane = lax.broadcasted_iota(jnp.int32, (T, 128), 1)
    return (lane < DH) if e == 0 else (lane >= DH)


def attend_pair(m, hp):
    T = m.xs.shape[0]
    s = at(hp, 128)
    q2, k2, v2 = m.qk[0, :, s].astype(f32), m.qk[1, :, s], m.v[:, s]
    kx = jnp.concatenate([k2, m.maskk[...]], axis=1)
    outs = []
    for e in (0, 1):
        qe = jnp.where(lane_half(T, e), q2, 0.0).astype(bf)
        E = jnp.exp(nt(jnp.concatenate([qe, m.maskq[...]], axis=1), kx))
        p = (E * (1.0 / jnp.sum(E, axis=-1, keepdims=True))).astype(bf)
        m.ebuf[2 * hp + e] = p
        outs.append(nn(p, v2))
    m.att[:, s] = jnp.where(lane_half(T, 0), outs[0], outs[1]).astype(bf)


def proj_stage(m):
    @pl.loop(0, m.xs.shape[1] // 256)
    def _(i):
        s = at(i, 256)
        m.resid[:, s] = m.xs[:, s].astype(f32) + nn(m.att[...], wcols(m, 3, s))


def gelu_both(x):
    z = jnp.abs(x) * (1.0 / math.sqrt(2.0))
    t = 1.0 / (1.0 + 0.3275911 * z)
    p = ((((1.061405429 * t - 1.453152027) * t + 1.421413741) * t - 0.284496736) * t + 0.254829592) * t
    ex = jnp.exp(-0.5 * x * x)
    tail = 0.5 * p * ex
    phi = jnp.where(x < 0, tail, 1.0 - tail)
    return x * phi, phi + x * ex * (1.0 / math.sqrt(2.0 * math.pi))


def up_stage(m, j):
    D = m.xs.shape[1]

    @pl.loop(0, D // 256)
    def _(i):
        a, d = gelu_both(nn(m.mid[...], wcols(m, 4 + j, at(i, 256))))
        s = at(i, 256, j * D)
        m.act[:, s] = a.astype(bf)
        m.gp[:, s] = d.astype(bf)


def out_stage(m, i):
    D = m.xs.shape[1]
    s = at(i, 256)
    acc = m.resid[:, s]
    for u in range(4):
        w = m.W[8:12, u, :, s]
        acc += nn(m.act[:, u * D : (u + 1) * D], w.reshape(D, 256))
    m.osel[:, s] = acc.astype(bf)


def dinner_stage(m, u):
    D = m.xs.shape[1]
    for i in range(2):
        w = m.W[8 + 2 * i : 10 + 2 * i, u, :, :]
        s = at(i, D // 2, u * D)
        d = nt(m.cot[...], w.reshape(D // 2, D))
        m.gp[:, s] = (d * m.gp[:, s].astype(f32)).astype(bf)


def dmid_stage(m, i):
    D = m.xs.shape[1]
    acc = nt(m.gp[:, 0:D], wrows(m, 4, i))
    for j in range(1, 4):
        acc += nt(m.gp[:, j * D : (j + 1) * D], wrows(m, 4 + j, i))
    m.dres[:, at(i, D // 2)] = acc


def dresid_stage(m):
    T, D = m.dres.shape
    g = m.gains[2:3, :]

    @pl.loop(0, T // 64)
    def _(i):
        s = at(i, 64)
        dm = m.dres[s, :]
        xh, r = standardize(m.resid[s, :])
        dx = dm * g
        m1 = jnp.mean(dx, axis=-1, keepdims=True)
        m2 = jnp.mean(dx * xh, axis=-1, keepdims=True)
        dr = m.cot[s, :].astype(f32) + r * (dx - m1 - xh * m2)
        m.dres[s, :] = dr
        m.dattn[s, :] = dr.astype(bf)
        m.gsum[2:3, :] += jnp.sum(dm * xh, axis=0, keepdims=True)
        m.gsum[3:4, :] += jnp.sum(dm, axis=0, keepdims=True)


def datt_stage(m):
    n = m.xs.shape[1] // 2

    @pl.loop(0, 2)
    def _(i):
        m.datt[:, at(i, n)] = nt(m.dattn[...], wrows(m, 3, i)).astype(bf)


def attend_back_pair(m, j, i):
    T, D = m.xs.shape
    hp = 2 * j + i
    s = at(hp, 128)
    do = m.datt[:, s].astype(f32)
    B = same_head(128)
    hi, lo = split2(do * m.att[:, s].astype(f32))
    dl = nn(hi, B) + nn(lo, B)
    k2, v2 = m.qk[1, :, s], m.v[:, s]
    lane = lax.broadcasted_iota(jnp.int32, (T, 128), 1)
    vx = jnp.concatenate([v2, (lane < 2).astype(f32).astype(bf)], axis=1)
    doT = do.T.astype(bf)
    qT = m.qk[0, :, s].astype(f32).T.astype(bf)
    dqs, dks, dvs = [], [], []
    for e in (0, 1):
        de = jnp.where(lane_half(T, e), do, 0.0).astype(bf)
        dle = dl[:, e * DH : e * DH + 1]
        dh = dle.astype(bf).astype(f32)
        dmask = jnp.where(lane == 0, -dh, jnp.where(lane == 1, dh - dle, 0.0)).astype(bf)
        t = nt(jnp.concatenate([de, dmask], axis=1), vx)
        E = m.ebuf[2 * hp + e]
        ds = (E.astype(f32) * t).astype(bf)
        dqs.append(nn(ds, k2))
        dks.append(nn(qT[e * DH : (e + 1) * DH, :], ds))
        dvs.append(nn(doT[e * DH : (e + 1) * DH, :], E))
    dq = jnp.where(lane_half(T, 0), dqs[0], dqs[1]) * (1.0 / math.sqrt(DH))
    dk = jnp.concatenate(dks, axis=0).T
    dv = jnp.concatenate(dvs, axis=0).T
    m.dqkv[:, at(i, 128, D * j + 512)] = dv.astype(bf)
    for kind, d in ((0, dq), (1, dk)):
        d = d.astype(bf).astype(f32)
        w = at(i, 128, 512 * j + 256 * kind)
        xh = m.qkh[:, w].astype(f32)
        r = m.qkr[:, w].astype(f32)
        m.gsum[4 + kind : 5 + kind, s] = jnp.sum(d * xh, axis=0, keepdims=True)
        dx = d * m.gains[4 + kind : 5 + kind, s]
        h1, l1 = split2(dx)
        m1 = (nn(h1, B) + nn(l1, B)) * (1.0 / DH)
        h2, l2 = split2(dx * xh)
        m2 = (nn(h2, B) + nn(l2, B)) * (1.0 / DH)
        m.dqkv[:, at(i, 128, D * j + 256 * kind)] = (r * (dx - m1 - xh * m2)).astype(bf)


def dnormed_stage(m, i):
    D = m.xs.shape[1]
    acc = nt(m.dqkv[:, 0:D], wrows(m, 0, i))
    for j in range(1, 3):
        acc += nt(m.dqkv[:, j * D : (j + 1) * D], wrows(m, j, i))
    m.resid[:, at(i, D // 2)] = acc


def dtokens_stage(m):
    T, D = m.dres.shape
    g = m.gains[0:1, :]

    @pl.loop(0, T // 64)
    def _(i):
        s = at(i, 64)
        dn = m.resid[s, :]
        xh, r = standardize(m.xs[s, :].astype(f32))
        dx = dn * g
        m1 = jnp.mean(dx, axis=-1, keepdims=True)
        m2 = jnp.mean(dx * xh, axis=-1, keepdims=True)
        m.dtok[s, :] = (m.dres[s, :] + r * (dx - m1 - xh * m2)).astype(bf)
        m.gsum[0:1, :] += jnp.sum(dn * xh, axis=0, keepdims=True)
        m.gsum[1:2, :] += jnp.sum(dn, axis=0, keepdims=True)


def grad_down(m, j):
    D = m.xs.shape[1]
    n = D // 4

    @pl.loop(0, 4)
    def _(u):
        m.G[j, u] = nn(m.cotT[j * n : (j + 1) * n, :], m.act[:, at(u, D)]).astype(bf)


def grad_block(m, b, lhsT, rhs, base):
    D = m.xs.shape[1]
    n = D // 4

    @pl.loop(0, D // 256)
    def _(i):
        r = nn(lhsT[...], rhs[:, at(i, 256, base)]).astype(bf)
        for u in range(4):
            m.G[b, u, :, at(i, 256)] = r[u * n : (u + 1) * n]


GATHER = ("y", "xy", "xy", "xy", "xy", "xy", "y", "x", "xy", "xy", "xy", "xy")
REDUCE = ("xy", "xy", "xy", "xy", "xy", "xy", "xy", "xy", "xy", "x", "y", "x")
SLOTS = (2, 4, 4, 4, 4, 12, 12)
KINDS = (
    "g", "r", "v", "rs", "rp", "rw", "cat", "res", "resw", "place", "gains", "selx", "norm1", "qkv", "att", "proj",
    "norm2", "midT", "up", "selc", "cotT", "gd", "out", "din", "dmid", "gu", "dres", "attT", "gpj", "datt", "nT", "bk",
    "gq", "dn", "dtok",
)
ORDER = (
    9000, 4000, 100, 5000, 3001, 200, 11000, 101, 300, 10000, 102, 12000, 103, 201, 4001, 400, 13000, 202, 203, 14000,
    301, 104, 401, 302, 105, 106, 107, 5001, 13001, 204, 205, 14001, 303, 19000, 206, 20000, 108, 109, 402, 403, 304,
    110, 207, 13002, 14002, 111, 15000, 16000, 17000, 305, 306, 404, 208, 18000, 209, 307, 210, 405, 18001, 406, 407,
    18002, 211, 18003, 308, 21000, 1000, 21001, 1001, 21003, 309, 1100, 310, 1101, 408, 311, 21002, 409, 410, 1002, 411,
    22001, 22000, 1200, 1102, 1003, 23000, 25000, 1201, 1103, 23001, 1004, 23002, 25001, 1300, 1202, 1104, 1005, 23003,
    25003, 1301, 1203, 1105, 25002, 1006, 24001, 24000, 22002, 1400, 1302, 6000, 1204, 27000, 1106, 26000, 1401, 1007,
    28000, 1303, 1500, 29000, 1205, 1107, 1402, 1008, 31000, 1304, 1501, 1502, 1206, 1108, 30000, 1403, 32000, 1009,
    7000, 1305, 1207, 1109, 31001, 32001, 1503, 1010, 1404, 1306, 1600, 1208, 31002, 1405, 1307, 1110, 1209, 32002,
    1011, 33000, 33001, 1504, 1111, 34000, 6001, 1406, 1505, 1407, 1601, 1308, 1309, 2000, 8000, 1602, 1210, 7001, 1603,
    1700, 1211, 1701, 1702, 1604, 2001, 1703, 2002, 1506, 1507, 1408, 1310, 1311, 2003, 1409, 1508, 1704, 2004, 1605,
    1606, 1607, 1410, 1411, 1509, 1608, 1705, 1510, 1511, 1609, 1706, 1707, 1708, 1709, 2005, 1610, 1611, 1710, 1711,
)


def entry(kind, number=0):
    return 1000 * KINDS.index(kind) + number


class Comm:
    def __init__(self, m):
        self.m = m
        self.x, self.z, sp = lax.axis_index("rep"), lax.axis_index("fsdp"), lax.axis_index("sp")
        self.y, self.c = sp // 2, sp % 2
        x, y, z, c = self.x, self.y, self.z, self.c
        nx, ny = (1 - x, z, sp), (x, z, 2 * (1 - y) + c)
        self.nx, self.ny = nx, ny
        n1 = (x + (1 - c) * (1 - 2 * x), z, 2 * (y + c * (1 - 2 * y)) + c)
        n2 = (x + c * (1 - 2 * x), z, 2 * (y + (1 - c) * (1 - 2 * y)) + c)
        self.orders = {"x": (x, y, nx, ny), "y": (y, x, ny, nx), "xy": (x + c * (y - x), y + c * (x - y), n1, n2)}
        self.core = (x, z, 2 * y + 1 - c)
        self.zat = lambda u: (x, u, sp)
        self.z1 = z + 1 - 2 * (z % 2)
        self.zt = 3 - z
        self.mine = at(c, 384)
        self.other = at(1 - c, 384)

    def gather_order(self, b):
        return self.orders[GATHER[b]]

    def reduce_order(self, b):
        return self.orders[REDUCE[b]]

    def barrier(self, meanwhile):
        sem = pltpu.get_barrier_semaphore()
        peers = [self.zat((self.z + d) % 4) for d in (1, 2, 3)] + [self.nx, self.ny, self.core]
        for p in peers:
            pl.semaphore_signal(sem, inc=1, device_id=p, device_id_type=MESH)
        meanwhile()
        pl.semaphore_wait(sem, len(peers))

    def copy(self, src, dst, send, recv, dev):
        return pltpu.make_async_remote_copy(
            src_ref=src, dst_ref=dst, send_sem=send, recv_sem=recv, device_id=dev, device_id_type=MESH
        )

    def row_copies(self, arg, buf, k):
        s, r = self.m.rsem.at[0, k], self.m.rsem.at[1, k]
        mine = buf.at[self.y, at(self.c, 256)]
        there = buf.at[1 - self.y, at(self.c, 256)]
        local = pltpu.make_async_copy(arg.at[self.y], mine, s.at[0])
        near = self.copy(arg.at[self.y], mine, s.at[1], r.at[1], self.core)
        far = self.copy(arg.at[1 - self.y], mine, s.at[2], r.at[2], self.ny)
        pass_on = self.copy(there, there, s.at[3], r.at[3], self.core)
        return local, near, far, pass_on

    def row_start(self, arg, buf, k):
        local, near, far, _ = self.row_copies(arg, buf, k)
        far.start()
        near.start()
        local.start()

    def row_pass(self, arg, buf, k):
        _, _, far, pass_on = self.row_copies(arg, buf, k)
        far.wait_recv()
        pass_on.start()

    def row_wait(self, arg, buf, k):
        local, near, far, pass_on = self.row_copies(arg, buf, k)
        local.wait()
        near.wait()
        far.wait_send()
        pass_on.wait()

    def gain_copies(self):
        m = self.m
        out = [pltpu.make_async_copy(m.gpack, m.gbuf.at[self.z], m.gsem.at[0, 0])]
        for d in (1, 2, 3):
            dev = self.zat((self.z + d) % 4)
            out.append(self.copy(m.gpack, m.gbuf.at[self.z], m.gsem.at[0, d], m.gsem.at[1, d], dev))
        return out

    def shard(self, b, rows, cols):
        m = self.m
        arg, r0, c0 = (m.a_qkv, 0, 0) if b < 3 else (m.a_proj, 0, 0) if b == 3 else (
            (m.a_up, 0, 768 * (b - 4)) if b < 8 else (m.a_down, 192 * (b - 8), 0))
        return arg.at[pl.ds(pl.multiple_of(r0 + rows[0], 16), rows[1]), pl.ds(pl.multiple_of(c0 + cols[0], 128), cols[1])]

    def spans(self, b):
        c = self.c
        if b < 3:
            return [(256 * b + 1536 * c, 512 * c, 256), (768 + 256 * b + 128 * c, 256 + 128 * c, 128)]
        return [(384 * c, 384 * c, 384)]

    def own_copies(self, b):
        sem, dst = self.m.wsem.at[0, 0, b], self.m.W.at[b, self.z]
        if b < 3:
            return [
                pltpu.make_async_copy(self.shard(b, (0, 192), (768 * i + 256 * b, 256)), dst.at[:, pl.ds(256 * i, 256)], sem)
                for i in range(3)
            ]
        return [pltpu.make_async_copy(self.shard(b, (0, 192), (0, 768)), dst, sem)]

    def own_start(self, b):
        for cp in self.own_copies(b):
            cp.start()

    def own_wait(self, b):
        m = self.m
        pltpu.make_async_copy(m.W.at[b, self.z], m.W.at[b, self.z], m.wsem.at[0, 0, b]).wait()

    def part(self, b):
        if GATHER[b] == "xz":
            return self.x * 96, 96
        f1, f2, _, _ = self.gather_order(b)
        return (2 * f2 + f1) * 48, 48

    def z_start(self, b):
        m = self.m
        first, count = self.part(b)
        for d in (1, 2, 3):
            for src, to, n in self.spans(b):
                dst = m.W.at[b, self.z, pl.ds(pl.multiple_of(first, 16), count), pl.ds(pl.multiple_of(to, 128), n)]
                sems = m.wsem.at[0, 1, b], m.wsem.at[1, 1, b]
                self.copy(self.shard(b, (first, count), (src, n)), dst, *sems, self.zat((self.z + d) % 4)).start()

    def leg(self, k, b):
        if k == 4:
            return pl.ds(0, 192), self.core
        if k == 3:
            _, f2, _, n2 = self.gather_order(b)
            return at(f2, 96), n2
        first, count = self.part(b)
        dev = self.nx if GATHER[b] == "xz" else self.gather_order(b)[2]
        return pl.ds(pl.multiple_of(first, 16), count), self.core if k == 1 else dev

    def plane(self, k, b):
        m = self.m
        rows, dev = self.leg(k, b)
        out = []
        for d in (1, 2, 3):
            ref = m.W.at[b, (self.z + d) % 4, rows, self.mine]
            out.append(self.copy(ref, ref, m.wsem.at[0, k, b], m.wsem.at[1, k, b], dev))
        return out

    def w_all(self, k, b):
        m = self.m
        rows, dev = self.leg(k, b)
        ref = m.W.at[b, 0:3, rows, self.mine]
        return self.copy(ref, ref, m.wsem.at[0, k, b], m.wsem.at[1, k, b], dev)

    def ag_step(self, k, b):
        stages = (1, 2, 4) if GATHER[b] == "xz" else (1, 2, 3, 4)
        if k not in stages:
            return
        self.w_all(k, b).wait_recv()
        if k < 4:
            for cp in self.plane(stages[stages.index(k) + 1], b):
                cp.start()
        else:
            for j in stages:
                self.w_all(j, b).wait_send()
            self.own_wait(b)

    def rs_copies(self, k, b):
        m = self.m
        G, z = m.G, self.z
        f1, f2, n1, n2 = self.reduce_order(b)
        slot = b % SLOTS[k]
        rows = at(f1, 96)
        sem = lambda j: (m.psem.at[0, j, slot], m.psem.at[1, j, slot])
        if k == 0:
            return [self.copy(G.at[b, :, :, self.other], m.rA.at[slot], *sem(0), self.core)]
        if k == 1:
            return [self.copy(G.at[b, :, at(1 - f1, 96), self.mine], m.rB.at[slot], *sem(1), n1)]
        if k == 2:
            return [
                self.copy(G.at[b, self.z1, rows, self.mine], m.rC.at[slot, 0], *sem(2), self.zat(self.z1)),
                self.copy(G.at[b, 3 - self.z1, rows, self.mine], m.rC.at[slot, 1], *sem(7), self.zat(self.z1)),
            ]
        if k == 3:
            return [self.copy(G.at[b, self.zt, rows, self.mine], m.rD.at[slot], *sem(3), self.zat(self.zt))]
        if k == 4:
            return [self.copy(G.at[b, z, rows, self.mine], m.rE.at[slot], *sem(4), n2)]
        if k == 5:
            ref = G.at[b, z, rows, self.mine]
            return [self.copy(ref, ref, *sem(5), n1)]
        ref = G.at[b, z, :, self.mine]
        return [self.copy(ref, ref, *sem(6), self.core)]

    def rs_step(self, k, b):
        m = self.m
        G, z = m.G, self.z
        rows = at(self.reduce_order(b)[0], 96)
        if k > 0:
            slot = b % SLOTS[k - 1]
            for cp in self.rs_copies(k - 1, b):
                cp.wait()
        if k == 1:

            @pl.loop(0, 4)
            def _(u):
                G[b, u, :, self.mine] = (G[b, u, :, self.mine].astype(f32) + m.rA[slot, u].astype(f32)).astype(bf)
        elif k == 2:

            @pl.loop(0, 4)
            def _(u):
                G[b, u, rows, self.mine] = (G[b, u, rows, self.mine].astype(f32) + m.rB[slot, u].astype(f32)).astype(bf)
        elif k == 3:
            for i, u in ((0, z), (1, self.zt)):
                G[b, u, rows, self.mine] = (G[b, u, rows, self.mine].astype(f32) + m.rC[slot, i].astype(f32)).astype(bf)
        elif k in (4, 5):
            r = (m.rD if k == 4 else m.rE)[slot]
            G[b, z, rows, self.mine] = (G[b, z, rows, self.mine].astype(f32) + r.astype(f32)).astype(bf)
        if k < 7:
            for cp in self.rs_copies(k, b):
                cp.start()
        else:
            self.fin_copy(b).start()

    def fin_copy(self, b):
        return pltpu.make_async_copy(self.m.G.at[b, self.z], self.m.fin.at[b], self.m.fsem.at[b])

    def vec_copy(self, i):
        m = self.m
        dev = [self.core, self.nx, self.ny, self.zat(self.z1), self.zat(self.zt)][i]
        return self.copy(m.gs.at[i], m.gr.at[i], m.vsem.at[0, i], m.vsem.at[1, i], dev)

    def vec_step(self, i):
        m = self.m
        if i == 0:
            m.gs[0] = m.gsum[...]
        else:
            self.vec_copy(i - 1).wait()
            m.gs[i] = m.gs[i - 1] + m.gr[i - 1]
        if i < 5:
            self.vec_copy(i).start()
        else:
            m.vec[...] = m.gs[5]

    def cat_copy(self, cat, k):
        half = cat.at[self.c]
        return self.copy(half, half, self.m.osem.at[0, k, 0], self.m.osem.at[1, k, 0], self.core)

    def quart(self, i):
        T, D = self.m.xs.shape
        return self.m.act.at[pl.ds(i * (T // 2), T // 2), pl.ds(3 * D, D)]

    def quarter_copies(self, dst, k):
        m = self.m
        far = self.copy(self.quart(1), dst.at[self.y], m.osem.at[0, k, 1], m.osem.at[1, k, 1], self.ny)
        near = pltpu.make_async_copy(self.quart(0), dst.at[self.y], m.osem.at[0, k, 2])
        return far, near

    def result_send(self, cat, dst, k):
        m = self.m
        self.cat_copy(cat, k).wait()
        restore_quarter(m, cat, 2 * (1 - self.y) + self.c, self.quart(1))
        far, near = self.quarter_copies(dst, k)
        far.start()
        restore_quarter(m, cat, 2 * self.y + self.c, self.quart(0))
        near.start()

    def result_wait(self, dst, k):
        far, near = self.quarter_copies(dst, k)
        far.wait()
        near.wait()


SCRATCH = lambda T, D, FF: dict(
    gains=((8, D), f32), maskq=((T, 128), bf), maskk=((T, 128), bf), xs=((T, D), bf), cot=((T, D), bf),
    mid=((T, D), bf), midT=((D, T), bf), cotT=((D, T), bf),
    qk=((2, T, D), bf), v=((T, D), bf), qkh=((T, 2 * D), bf), qkr=((T, 2 * D), bf),
    ebuf=((H, T, T), bf), att=((T, D), bf), resid=((T, D), f32),
    act=((T, FF), bf), gp=((T, FF), bf), dres=((T, D), f32), datt=((T, D), bf), gsum=((8, D), f32),
)


def prepare(m, lengths, y):
    T = m.xs.shape[0]
    l = [lengths[y, k] for k in range(4)]
    m.ends = [l[0], l[0] + l[1], l[0] + l[1] + l[2]]
    m.start = jnp.where(l[0] == T, 0, jnp.where(l[1] == T, m.ends[0], jnp.where(l[2] == T, m.ends[1], m.ends[2])))
    m.dattn = m.mid
    m.dqkv = m.act
    m.attT = m.cotT


def two(f):
    @pl.loop(0, 2)
    def _(i):
        f(i)


def compute_pieces(m):
    D = m.xs.shape[1]
    pieces = {
        entry("place"): lambda: place_stage(m),
        entry("norm1"): lambda: norm_stage(m.xs, m.gains[0:1, :], m.gains[1:2, :], m.mid),
        entry("nT"): lambda: (norm_stage(m.xs, m.gains[0:1, :], m.gains[1:2, :], m.mid), transpose_to(m.mid, m.midT)),
        entry("proj"): lambda: proj_stage(m),
        entry("norm2"): lambda: norm_stage(m.resid, m.gains[2:3, :], m.gains[3:4, :], m.mid),
        entry("midT"): lambda: transpose_to(m.mid, m.midT),
        entry("cotT"): lambda: transpose_to(m.cot, m.cotT),
        entry("dres"): lambda: dresid_stage(m),
        entry("attT"): lambda: transpose_to(m.att, m.attT),
        entry("gpj"): lambda: grad_block(m, 8, m.attT, m.dattn, 0),
        entry("datt"): lambda: datt_stage(m),
        entry("dtok"): lambda: dtokens_stage(m),
    }

    def several(name, n, f):
        for i in range(n):
            pieces[entry(name, i)] = functools.partial(f, i)

    several("qkv", 3, lambda i: qkv_stage(m, i))
    several("att", 3, lambda j: two(lambda i: attend_pair(m, 2 * j + i)))
    several("up", 4, lambda i: up_stage(m, i))
    several("gd", 4, lambda i: grad_down(m, i))
    several("out", 3, lambda i: out_stage(m, i))
    several("din", 4, lambda i: dinner_stage(m, i))
    several("dmid", 2, lambda i: dmid_stage(m, i))
    several("gu", 4, lambda i: grad_block(m, 4 + i, m.midT, m.gp, i * D))
    several("bk", 3, lambda j: two(lambda i: attend_back_pair(m, j, i)))
    several("gq", 3, lambda i: grad_block(m, 9 + i, m.midT, m.dqkv, i * D))
    several("dn", 2, lambda i: dnormed_stage(m, i))
    return pieces


def layer_kernel(comm_names, *refs):
    m = SimpleNamespace(**dict(zip(comm_names, refs)))
    cm = Comm(m)
    m.osel, m.dtok = m.rowx.at[cm.c], m.rowc.at[cm.c]
    m.maskq, m.maskk = m.rowx.at[0, :, pl.ds(512, 128)], m.rowx.at[1, :, pl.ds(512, 128)]
    m.core = cm.c
    prepare(m, m.lengths, cm.y)

    def meanwhile():
        m.gpack[...] = jnp.zeros_like(m.gpack)
        for i in range(6):
            g = getattr(m, "g%d" % i)
            m.gpack[i : i + 1, 0 : g.shape[0]] = g[...].astype(f32).reshape(1, g.shape[0])
        m.gsum[...] = jnp.zeros_like(m.gsum)
        for b in range(12):
            cm.own_start(b)
        place_stage(m)

    cm.barrier(meanwhile)
    cm.row_start(m.tokens, m.rowx, 0)
    for b in range(12):
        cm.z_start(b)
        if b == 2:
            for g in cm.gain_copies():
                g.start()

    def gains():
        for g in cm.gain_copies():
            g.wait()
        gains_stage(m)

    def selx():
        select_rows(m, m.rowx, m.xs)
        for h in range(2):
            m.rowx[h, :, 0 : m.ebuf.shape[1]] = m.ebuf[10 + h]
        mask_stage(m)

    pieces = compute_pieces(m)
    pieces[entry("place")] = lambda: None
    rows = ((m.tokens, m.rowx, 0), (m.cotangent, m.rowc, 1))
    pieces.update(
        {
            entry("gains"): gains,
            entry("selx"): selx,
            entry("selc"): lambda: select_cot(m),
            entry("rs", 1): lambda: cm.row_start(*rows[1]),
            entry("cat", 0): lambda: cm.cat_copy(m.rowx, 0).start(),
            entry("cat", 1): lambda: cm.cat_copy(m.rowc, 1).start(),
            entry("res", 0): lambda: cm.result_send(m.rowx, m.outq, 0),
            entry("res", 1): lambda: cm.result_send(m.rowc, m.dtokq, 1),
            entry("resw", 0): lambda: cm.result_wait(m.outq, 0),
        }
    )
    for k in range(2):
        pieces[entry("rp", k)] = functools.partial(cm.row_pass, *rows[k])
        pieces[entry("rw", k)] = functools.partial(cm.row_wait, *rows[k])
    for i in range(6):
        pieces[entry("v", i)] = functools.partial(cm.vec_step, i)
    for b in range(12):
        for k in range(1, 5):
            pieces[entry("g", 100 * k + b)] = functools.partial(cm.ag_step, k, b)
        for k in range(8):
            pieces[entry("r", 100 * k + b)] = functools.partial(cm.rs_step, k, b)
    assert sorted(pieces) == sorted(ORDER)
    for name in ORDER:
        pieces[name]()
    for b in range(12):
        cm.fin_copy(b).wait()
    cm.result_wait(m.dtokq, 1)


def fused_layer(tokens, lengths, cotangent, vectors, w_qkv, w_proj, w_up, w_down):
    T, D, FF = tokens.shape[0] * tokens.shape[1], tokens.shape[2], w_up.shape[1]
    any_, vmem = pl.BlockSpec(memory_space=pl.ANY), pl.BlockSpec(memory_space=pltpu.VMEM)
    ins = ["tokens", "lengths", "cotangent", "a_qkv", "a_proj", "a_up", "a_down"] + ["g%d" % i for i in range(6)]
    outs = dict(
        fin=((12, D // 4, D), bf), outq=(tokens.shape, bf), dtokq=(tokens.shape, bf), vec=((8, D), f32)
    )
    scratch = SCRATCH(T, D, FF)
    del scratch["maskq"], scratch["maskk"]
    scratch.update(
        W=((12, 4, D // 4, D), bf), G=((12, 4, D // 4, D), bf), rowx=((2, T, D), bf), rowc=((2, T, D), bf),
        gbuf=((4, 8, 256), f32), gpack=((8, 256), f32),
        rA=((SLOTS[0], 4, 192, 384), bf), rB=((SLOTS[1], 4, 96, 384), bf), rC=((SLOTS[2], 2, 96, 384), bf),
        rD=((SLOTS[3], 96, 384), bf),
        rE=((SLOTS[4], 96, 384), bf), gs=((6, 8, D), f32), gr=((5, 8, D), f32),
    )
    sems = dict(
        rsem=(2, 2, 4), gsem=(2, 4), wsem=(2, 5, 12), psem=(2, 8, 12), fsem=(12,), vsem=(2, 5), osem=(2, 2, 3)
    )
    names = ins + list(outs) + list(scratch) + list(sems)
    return pl.pallas_call(
        functools.partial(layer_kernel, names),
        out_shape=[jax.ShapeDtypeStruct(s, d) for s, d in outs.values()],
        in_specs=[any_, pl.BlockSpec(memory_space=pltpu.SMEM), any_] + [any_] * 4 + [vmem] * 6,
        out_specs=[any_, any_, any_, vmem],
        scratch_shapes=[pltpu.VMEM(s, d) for s, d in scratch.values()]
        + [pltpu.SemaphoreType.DMA(s) for s in sems.values()],
        compiler_params=pltpu.CompilerParams(collective_id=0, has_side_effects=True, vmem_limit_bytes=VMEM_LIMIT),
        name="layer",
    )(tokens, lengths, cotangent, w_qkv, w_proj, w_up, w_down, *vectors)


def plain_kernel(names, *refs):
    m = SimpleNamespace(**dict(zip(names, refs)))
    sp = lax.axis_index("sp")
    m.core = sp % 2
    prepare(m, m.lengths, sp // 2)
    m.gsum[...] = jnp.zeros_like(m.gsum)
    pieces = compute_pieces(m)
    pieces[entry("selx")] = lambda: (select_rows(m, m.rowx, m.xs), select_rows(m, m.rowc, m.cot), mask_stage(m))
    for name in ORDER:
        if name in pieces:
            pieces[name]()


def general_layer(tokens, lengths, cotangent, vectors, w_qkv, w_proj, w_up, w_down):
    T, D, FF = tokens.shape[0] * tokens.shape[1], tokens.shape[2], w_up.shape[1]
    n = D // 4
    gather = lambda v: lax.all_gather(v, "fsdp", axis=0, tiled=True)
    qkv, proj, up, down = (gather(w) for w in (w_qkv, w_proj, w_up, w_down))
    by_columns = lambda w: w.reshape(4, n, -1, D).transpose(2, 0, 1, 3)
    swap = lambda w: w.reshape(w.shape[0], 3, 3, -1).transpose(0, 2, 1, 3).reshape(w.shape)
    W = jnp.concatenate(
        [by_columns(swap(qkv)), by_columns(proj), by_columns(up), down.reshape(4, 4, n, D).transpose(1, 0, 2, 3)]
    )
    gains = [gather(v).astype(f32) for v in vectors]
    gains = [jnp.tile(g, D // g.shape[0]) for g in gains] + [jnp.zeros(D, f32)] * 2
    sp = lax.axis_index("sp")
    whole_row = lambda v: lax.dynamic_index_in_dim(lax.all_gather(v, "sp", axis=1, tiled=True), sp // 2, 0, False)
    rowx, rowc = (whole_row(v).reshape(2, T, D) for v in (tokens, cotangent))
    scratch = SCRATCH(T, D, FF)
    gsum = scratch.pop("gsum")
    del scratch["gains"]
    outs = dict(G=(W.shape, bf), osel=((T, D), bf), dtok=((T, D), bf), gsum=gsum)
    vmem = pl.BlockSpec(memory_space=pltpu.VMEM)
    names = ["lengths", "W", "rowx", "rowc", "gains"] + list(outs) + list(scratch)
    G, osel, dtok, gsum = pl.pallas_call(
        functools.partial(plain_kernel, names),
        out_shape=[jax.ShapeDtypeStruct(s, d) for s, d in outs.values()],
        in_specs=[pl.BlockSpec(memory_space=pltpu.SMEM)] + [vmem] * 4,
        out_specs=[vmem] * 4,
        scratch_shapes=[pltpu.VMEM(s, d) for s, d in scratch.values()],
        compiler_params=pltpu.CompilerParams(vmem_limit_bytes=VMEM_LIMIT),
        name="layer",
    )(lengths, W, rowx, rowc, jnp.stack(gains))

    def reduce(v):
        part = lax.psum_scatter(v.astype(bf), "fsdp", scatter_dimension=0, tiled=True)
        return lax.psum(part, ("rep", "sp")).astype(f32)

    natural = lambda g: g.reshape(-1, D, D).transpose(1, 0, 2).reshape(D, -1)
    g_down = G[0:4].transpose(1, 3, 0, 2).reshape(4 * D, D)
    heads = jnp.sum(gsum[4:6].reshape(2, -1, DH), axis=1)
    vecs = [reduce(v) for v in (gsum[0], gsum[1], gsum[2], gsum[3], heads[0], heads[1])]
    start = jnp.sum(jnp.where(jnp.arange(4)[None] < jnp.argmax(lengths, axis=1)[:, None], lengths, 0), axis=1)

    def back(half):
        rows = lax.all_gather(half, "sp", axis=0, tiled=True).reshape(2, 2 * T, D)
        rows = jnp.stack([jnp.roll(rows[r], start[r], axis=0) for r in range(2)])
        size = 2 * T // 4
        return lax.dynamic_slice_in_dim(rows, sp * size, size, axis=1).astype(f32)

    return (back(osel), back(dtok), vecs[0], vecs[1], reduce(swap(natural(G[9:12]))), vecs[4], vecs[5],
            reduce(natural(G[8:9])), vecs[2], vecs[3], reduce(natural(G[4:8])), reduce(g_down))


def widen(src, dst):
    @pl.loop(0, src.shape[0] // 64)
    def _(i):
        dst[at(i, 64), :] = src[at(i, 64), :].astype(f32)


def finish_kernel(names, *refs):
    m = SimpleNamespace(**dict(zip(names, refs)))
    n, D = m.fin.shape[1], m.fin.shape[2]
    loads = [pltpu.make_async_copy(m.fin.at[b], m.inb.at[b], m.lsem.at[b]) for b in range(12)]
    rows = [(m.outq, m.out, 0), (m.dtokq, m.dtok, 1)]
    row_loads = [pltpu.make_async_copy(src, m.inr.at[i], m.lsem.at[12 + i]) for src, _, i in rows]
    for cp in row_loads + loads[4:] + loads[:4]:
        cp.start()
    stores = []

    def store(src, dst):
        cp = pltpu.make_async_copy(src, dst, m.ssem.at[len(stores)])
        cp.start()
        stores.append(cp)

    def row(i):
        row_loads[i].wait()
        widen(m.inr.at[i, 0], m.outr.at[i, 0])
        widen(m.inr.at[i, 1], m.outr.at[i, 1])
        store(m.outr.at[i], rows[i][1])

    row(0)
    row(1)
    for b in range(4, 12):
        loads[b].wait()
        widen(m.inb.at[b], m.outb.at[b - 4])
        if b < 9:
            dst, col = (m.g_up, (b - 4) * D) if b < 8 else (m.g_proj, 0)
            store(m.outb.at[b - 4], dst.at[:, pl.ds(col, D)])
        else:
            for i in range(3):
                store(m.outb.at[b - 4, :, pl.ds(256 * i, 256)], m.g_qkv.at[:, pl.ds(D * i + 256 * (b - 9), 256)])
    for b in range(4):
        loads[b].wait()
        widen(m.inb.at[b], m.comb.at[b * n : (b + 1) * n])
    for h in range(2):

        @pl.loop(h * D // 256, (h + 1) * D // 256)
        def _(i):
            m.turned[at(i, 128), :] = m.comb[:, at(i, 128)].T

        half = pl.ds(h * (D // 2), D // 2)
        store(m.turned.at[half], m.g_down.at[half])
    z = lax.axis_index("fsdp")
    v = m.vec[...]
    wide = pltpu.roll(v, lax.rem(D - n * z, D), 1)
    for i, ref in enumerate((m.v0, m.v1, m.v2, m.v3)):
        ref[...] = wide[i, :n]
    h = v[:, :128]
    for i in range(1, D // 128):
        h += v[:, 128 * i : 128 * (i + 1)]
    h = h + pltpu.roll(h, DH, 1)
    h = pltpu.roll(h, lax.rem(128 - DH // 4 * z, 128), 1)
    for i, ref in enumerate((m.v4, m.v5)):
        ref[...] = h[4 + i, : DH // 4]
    for cp in stores:
        cp.wait()


def finish(fin, outq, dtokq, vec):
    n, D = fin.shape[1:]
    any_, vmem = pl.BlockSpec(memory_space=pl.ANY), pl.BlockSpec(memory_space=pltpu.VMEM)
    outs = dict(out=outq.shape, dtok=outq.shape, g_qkv=(n, 3 * D), g_proj=(n, D), g_up=(n, 4 * D), g_down=(D, D))
    vecs = {"v%d" % i: (n if i < 4 else DH // 4,) for i in range(6)}
    scratch = dict(
        inb=(fin.shape, bf), inr=((2,) + outq.shape, bf), outr=((2,) + outq.shape, f32), comb=((D, D), f32),
        turned=((D, D), f32), outb=((8, n, D), f32),
    )
    names = ["fin", "outq", "dtokq", "vec"] + list(outs) + list(vecs) + list(scratch) + ["lsem", "ssem"]
    out, dtok, qkv, proj, up, down, *v = pl.pallas_call(
        functools.partial(finish_kernel, names),
        out_shape=[jax.ShapeDtypeStruct(s, f32) for s in list(outs.values()) + list(vecs.values())],
        in_specs=[any_] * 3 + [vmem],
        out_specs=[any_] * 6 + [vmem] * 6,
        scratch_shapes=[pltpu.VMEM(s, d) for s, d in scratch.values()] + [pltpu.SemaphoreType.DMA((20,))] * 2,
        compiler_params=pltpu.CompilerParams(vmem_limit_bytes=VMEM_LIMIT),
        name="finish",
    )(fin, outq, dtokq, vec)
    return out, dtok, v[0], v[1], qkv, v[4], v[5], proj, v[2], v[3], up, down


def per_device(tokens, lengths, cotangent, pre_gain, pre_shift, w_qkv, query_gain, key_gain, w_proj, mid_gain,
               mid_shift, w_up, w_down):
    vectors = (pre_gain, pre_shift, mid_gain, mid_shift, query_gain, key_gain)
    if tuple(lax.axis_size(a) for a in ("rep", "fsdp", "sp")) != (2, 4, 4):
        return general_layer(tokens, lengths, cotangent, vectors, w_qkv, w_proj, w_up, w_down)
    return finish(*fused_layer(tokens, lengths, cotangent, vectors, w_qkv, w_proj, w_up, w_down))


def solution(mesh):
    rows, vec, mat = P(("rep", "fsdp"), "sp", None), P("fsdp"), P("fsdp", None)
    return jax.shard_map(
        per_device,
        mesh=mesh,
        in_specs=(rows, P(("rep", "fsdp"), None), rows, vec, vec, mat, vec, vec, mat, vec, vec, mat, mat),
        out_specs=(rows, rows, vec, vec, mat, vec, vec, mat, vec, vec, mat, mat),
        check_vma=False,
    )
```
